32 devices in a mesh: grp: 2 (over x), seq: 16 (over z, y, core).
Axes of the slice: x: 2, y: 2, z: 4, core: 2. Of those that a mesh axis runs over, the one named last changes fastest.
Arguments:
- queries: bfloat16 [4, 16384, 128], P(None, ('grp', 'seq')), parts along dimension 1, may hold values from -6 to 6
- key_pairs: bfloat16 [4, 16384, 256], P(None, ('grp', 'seq')), parts along dimension 1, may hold values from -6 to 6
- value_pairs: bfloat16 [4, 16384, 256], P(None, ('grp', 'seq')), parts along dimension 1, may hold values from -6 to 6
- write_rates: float32 [4, 32768], P(None, ('grp', 'seq')), parts along dimension 1, as said below
- conv_query: float32 [4, 4, 128], replicated, may hold values from -3 to 3
- conv_key: float32 [4, 4, 256], replicated, may hold values from -3 to 3
- conv_value: float32 [4, 4, 256], replicated, may hold values from -3 to 3
- out_gain: float32 [4, 128], replicated, may hold values from 0.5 to 1.5
Outputs:
- head_out: float32 [4, 16384, 128], P(None, ('grp', 'seq')), parts along dimension 1
The draws below stay inside these ranges and needn't reach their ends.
There are 2 independent parts, one for each index of `grp`. The reference program is written for one: setup_inputs(seed, part) draws one part's arguments, and reference() takes and returns one part's arrays. A program takes and returns all parts, laid end to end along the dimension named above; an argument that names none is the same for every part. Nothing has to cross between parts.
Inputs may be any that keep to these rules, and one draw needn't show every extreme that they name: `write_rates`: every rate is positive and at most 1.5.
All inputs are finite; a program needn't handle non-finite values.
Results may differ from the reference program's by a relative error of at most 0.0003.
Values may be sent and summed in bfloat16 or wider, within the bound.
No kernel may reach another device: no remote copies, remote signals or barrier semaphores. Data moves between devices by JAX's collectives and lax.ppermute only.
A program may use at most 192 MiB of HBM per device.

```python
import math
import jax
import jax.numpy as jnp
from jax import lax

GROUP_HEADS = 4
DK = 128
DV = 128
KW = 4
TOKENS = 8192
STEPS_DEV = 1024
REFLECT_STEPS = 16384


def draw_write_rates(key, part):
    shard_key_rows = jax.random.split(key, 6)
    slow_share = 5
    slow_heads = jax.random.randint(shard_key_rows[0], (GROUP_HEADS, 1), 0, 10) < slow_share
    blocks = REFLECT_STEPS // STEPS_DEV
    device_factor = jnp.exp(jax.random.uniform(shard_key_rows[1], (GROUP_HEADS, blocks, 1), jnp.float32, math.log(0.25), 0.0))
    device_factor = jnp.broadcast_to(device_factor, (GROUP_HEADS, blocks, STEPS_DEV)).reshape(GROUP_HEADS, REFLECT_STEPS)
    jitter = jnp.exp(jax.random.uniform(shard_key_rows[2], (GROUP_HEADS, REFLECT_STEPS), jnp.float32, math.log(0.5), math.log(1.5)))
    gradual_rate = DK / REFLECT_STEPS * device_factor * jitter
    fast_rate = jnp.exp(jax.random.uniform(shard_key_rows[3], (GROUP_HEADS, REFLECT_STEPS), jnp.float32, math.log(0.3), math.log(1.5)))
    shard_offsets = jax.random.randint(shard_key_rows[4], (3,), 0, REFLECT_STEPS - 32)
    token_position = jnp.arange(REFLECT_STEPS)
    inside_surge = jnp.any((token_position[None, :] >= shard_offsets[:, None]) & (token_position[None, :] < shard_offsets[:, None] + 32), 0)
    surge_rate = jax.random.uniform(shard_key_rows[5], (GROUP_HEADS, REFLECT_STEPS), jnp.float32, 0.8, 1.2)
    gradual_whole = jnp.where(inside_surge[None, :], surge_rate, gradual_rate)
    return jnp.where(slow_heads, gradual_whole, fast_rate).astype(jnp.float32)


def levels(stream_key, shape, cuts, low, high):
    def one(axis_at, blocks):
        steps = jax.random.uniform(jax.random.fold_in(jax.random.fold_in(stream_key, 6), axis_at), (blocks,), jnp.float32, low / len(cuts), high / len(cuts))
        return jnp.repeat(jnp.exp(steps), shape[axis_at] // blocks).reshape((-1,) + (1,) * (len(shape) - axis_at - 1))

    gain = one(*cuts[0])
    for cut in cuts[1:]:
        gain = gain * one(*cut)
    return gain


def normal_values(stream_key, dims, scale, reach, cuts=(), held_as=jnp.bfloat16):
    factor_of = levels(stream_key, dims, cuts, -0.22, 0.18) if cuts else 1.0
    values = jax.random.normal(stream_key, dims, jnp.float32) * scale * factor_of
    return jnp.minimum(jnp.maximum(values, -reach), reach).astype(held_as)


def setup_inputs(seed: int = 0, part: int = 0) -> dict:
    splits = jax.random.split(jax.random.key(seed), 9)
    part_keys = jax.random.split(jax.random.fold_in(splits[8], part), 9)
    queries = normal_values(part_keys[0], (GROUP_HEADS, TOKENS, DK), 1.0, 6.0, ((1, 16),))
    key_pairs = normal_values(part_keys[1], (GROUP_HEADS, TOKENS, 2 * DK), 1.0, 6.0, ((1, 16),))
    value_pairs = normal_values(part_keys[2], (GROUP_HEADS, TOKENS, 2 * DV), 1.0, 6.0, ((1, 16),))
    write_rates = draw_write_rates(jax.random.fold_in(jax.random.fold_in(splits[8], part), 71), part)
    conv_query = normal_values(splits[4], (GROUP_HEADS, KW, DK), KW ** -0.5, 3.0, (), jnp.float32)
    conv_key = normal_values(splits[5], (GROUP_HEADS, KW, 2 * DK), KW ** -0.5, 3.0, (), jnp.float32)
    conv_value = normal_values(splits[6], (GROUP_HEADS, KW, 2 * DV), KW ** -0.5, 3.0, (), jnp.float32)
    out_gain = jnp.clip(1.0 + 0.1 * jax.random.normal(splits[7], (GROUP_HEADS, DV), jnp.float32), 0.5, 1.5)
    return dict(queries=queries, key_pairs=key_pairs, value_pairs=value_pairs, write_rates=write_rates, conv_query=conv_query, conv_key=conv_key, conv_value=conv_value, out_gain=out_gain)


def conv_full(inputs, weights):
    kernel_len = weights.shape[1]
    length = inputs.shape[1]
    padded = jnp.pad(inputs.astype(jnp.float32), ((0, 0), (kernel_len - 1, 0), (0, 0)))
    summed = jnp.zeros(inputs.shape, jnp.float32)
    for shift_pos in range(kernel_len):
        summed = summed + weights[:, shift_pos][:, None, :] * padded[:, shift_pos:shift_pos + length]
    return jax.nn.silu(summed)

def reference(queries, key_pairs, value_pairs, write_rates, conv_query, conv_key, conv_value, out_gain):
    query_act = conv_full(queries, conv_query)
    key_act = conv_full(key_pairs, conv_key).reshape(GROUP_HEADS, TOKENS, 2, DK)
    key_act = key_act * lax.rsqrt(lax.optimization_barrier(jnp.sum(key_act * key_act, -1, keepdims=True)) + 1e-06)
    value_act = conv_full(value_pairs, conv_value).reshape(GROUP_HEADS, TOKENS, 2, DV)
    rates = write_rates.reshape(GROUP_HEADS, TOKENS, 2)
    inputs = (jnp.moveaxis(query_act, 1, 0), jnp.moveaxis(key_act, 1, 0), jnp.moveaxis(value_act, 1, 0), jnp.moveaxis(rates, 1, 0))

    def token_step(carried, inputs_t):
        query_t, key_t, value_t, rate_t = inputs_t
        for pair_idx in range(2):
            key_one = key_t[:, pair_idx]
            readback = jnp.einsum('hd,hde->he', key_one, carried, precision=lax.Precision.HIGHEST)
            carried = carried + rate_t[:, pair_idx][:, None, None] * key_one[:, :, None] * (value_t[:, pair_idx] - readback)[:, None, :]
        result = jnp.einsum('hd,hde->he', query_t, carried, precision=lax.Precision.HIGHEST)
        return (carried, result)
    start = jnp.zeros((GROUP_HEADS, DK, DV), jnp.float32)
    _, read_all = lax.scan(token_step, start, inputs)
    raw_out = jnp.moveaxis(read_all, 0, 1)
    squares = lax.optimization_barrier(jnp.mean(raw_out * raw_out, -1, keepdims=True))
    return raw_out * lax.rsqrt(squares + 1e-06) * out_gain[:, None, :]
```

```python
import jax
import jax.numpy as jnp
from jax import lax
from jax.experimental import pallas as pl
from jax.experimental.pallas import tpu as pltpu
from jax.sharding import PartitionSpec as P

BLOCK = 128
GROUP = 16
HALF = BLOCK // 2

f32 = jnp.float32
bf16 = jnp.bfloat16


def split(x):
    high = x.astype(bf16)
    low = (x - high.astype(f32)).astype(bf16)
    return jnp.concatenate([high, low], 1)


def mm(a, b):
    n = b.shape[1] // 2
    p = jnp.dot(a, jnp.concatenate([b, b], 0), preferred_element_type=f32)
    return p[:, :n] + p[:, n:]


def silu(x):
    return x / (1.0 + jnp.exp(-x))


def step_time(r):
    return (r // GROUP) * GROUP + 2 * (r % 8) + (r // 8) % 2


def interleave(a, b):
    parts = []
    for g in range(0, a.shape[0], 8):
        parts += [a[g : g + 8], b[g : g + 8]]
    return jnp.concatenate(parts, 0)


def conv_taps(ref, weights, start, count):
    taps = weights.shape[0]
    total = weights[0:1] * ref[pl.ds(start + 9 - taps, count), :]
    for s in range(1, taps):
        total = total + weights[s : s + 1] * ref[pl.ds(start + 9 - taps + s, count), :]
    return silu(total)


def fill_rows(ref, halo, rows):
    rim = halo.shape[0]
    ref[8 - rim : 8, :] = halo.astype(f32)
    ref[8:, :] = rows.astype(f32)


def maps_kernel(
    key_ref, value_ref, halo_ref, rate_ref, ck_ref, cv_ref,
    kb_ref, w_ref, u_ref, p_ref, s_ref, total_ref,
    k0, k1, v0, v1, kv, nref, dref, cref, xref, brow,
):
    dim = k0.shape[1]
    tokens = key_ref.shape[1]
    blocks = tokens // HALF
    halo = halo_ref[0]
    fill_rows(k0, halo[:, dim : 2 * dim], key_ref[0, :, :dim])
    fill_rows(k1, halo[:, 2 * dim : 3 * dim], key_ref[0, :, dim:])
    fill_rows(v0, halo[:, 3 * dim : 4 * dim], value_ref[0, :, :dim])
    fill_rows(v1, halo[:, 4 * dim :], value_ref[0, :, dim:])
    ck = ck_ref[0]
    cv = cv_ref[0]

    row = lax.broadcasted_iota(jnp.int32, (BLOCK, BLOCK), 0)
    col = lax.broadcasted_iota(jnp.int32, (BLOCK, BLOCK), 1)
    for n in range(blocks):
        brow[n : n + 1, :] = rate_ref[0, :, n * BLOCK : (n + 1) * BLOCK]
    order = (row == step_time(col)).astype(f32)
    rates = jnp.dot(brow[...], order, precision=lax.Precision.HIGHEST, preferred_element_type=f32)

    strict = step_time(col) < step_time(row)
    lane = lax.broadcasted_iota(jnp.int32, (GROUP, BLOCK), 1)
    eye = (row == col).astype(f32)

    for n in range(blocks):
        t0 = n * HALF
        ka = conv_taps(k0, ck[:, :dim], t0, HALF)
        kb = conv_taps(k1, ck[:, dim:], t0, HALF)
        keys = interleave(ka, kb)
        keys = keys * lax.rsqrt(jnp.sum(keys * keys, 1, keepdims=True) + 1e-06)
        va = conv_taps(v0, cv[:, :dim], t0, HALF)
        vb = conv_taps(v1, cv[:, dim:], t0, HALF)
        ks = split(keys)
        kv[n, :, : 2 * dim] = ks
        kv[n, :, 2 * dim :] = split(interleave(va, vb))
        kbs = split(keys.T * rates[n : n + 1, :])
        kb_ref[0, n] = kbs
        lower = jnp.where(strict, mm(ks, kbs), 0.0)
        nref[n] = lower
        diag = jnp.zeros((GROUP, BLOCK), f32)
        for g in range(BLOCK // GROUP):
            diag = jnp.where(lane // GROUP == g, lower[g * GROUP : (g + 1) * GROUP], diag)
        cref[n * GROUP : (n + 1) * GROUP, :] = diag

    lane8 = lax.broadcasted_iota(jnp.int32, (blocks, BLOCK), 1)
    times = [t // 2 + 8 * (t % 2) for t in range(GROUP)]
    coef = [cref[pl.ds(r, blocks, stride=GROUP), :] for r in range(GROUP)]
    sol = [(lane8 % GROUP == r).astype(f32) for r in range(GROUP)]
    for i, s in enumerate(times):
        pick = (lane8 // GROUP) * GROUP + s
        for r in times[i + 1 :]:
            sol[r] = sol[r] - jnp.take_along_axis(coef[r], pick, axis=1) * sol[s]
    for r in range(GROUP):
        xref[pl.ds(r, blocks, stride=GROUP), :] = sol[r]
    for n in range(blocks):
        base = xref[n * GROUP : (n + 1) * GROUP, :]
        dref[n] = split(
            jnp.concatenate(
                [jnp.where(lane // GROUP == g, base, 0.0) for g in range(BLOCK // GROUP)], 0
            )
        )

    lane_h = lax.broadcasted_iota(jnp.int32, (HALF, BLOCK), 1)
    row_h = lax.broadcasted_iota(jnp.int32, (HALF, BLOCK), 0)
    size = GROUP
    while size < BLOCK:
        keep = lane_h // size == 2 * (row_h // size)
        starts = range(size, BLOCK, 2 * size)
        for n in range(blocks):
            inv = dref[n]
            low = jnp.concatenate([nref[n, a : a + size] for a in starts], 0)
            z = split(mm(split(jnp.where(keep, low, 0.0)), inv))
            twice = []
            for i in range(len(starts)):
                twice += [z[i * size : (i + 1) * size]] * 2
            odd = jnp.concatenate([inv[a : a + size] for a in starts], 0)
            new = mm(odd, jnp.concatenate(twice, 0))
            new = split(odd[:, :BLOCK].astype(f32) + odd[:, BLOCK:].astype(f32) - new)
            for i, a in enumerate(starts):
                dref[n, a : a + size] = new[i * size : (i + 1) * size]
        size *= 2

    before_map = split(eye)
    before_state = jnp.zeros((dim, 2 * dim), bf16)
    state = jnp.zeros((dim, dim), f32)
    for n in range(blocks):
        inv = dref[n]
        w = split(mm(inv, kv[n, :, : 2 * dim]))
        u = split(mm(inv, kv[n, :, 2 * dim :]))
        w_ref[0, n] = w
        u_ref[0, n] = u
        p_ref[0, n] = before_map
        s_ref[0, n] = before_state
        kbs = kb_ref[0, n]
        move = split(eye - mm(kbs, w))
        written = mm(kbs, u)
        map_now = mm(move, before_map)
        state = mm(move, before_state) + written
        before_map = split(map_now)
        before_state = split(state)
        if n == blocks - 1:
            total_ref[0, :, :dim] = map_now
            total_ref[0, :, dim:] = state


def reads_kernel(
    query_ref, halo_ref, cq_ref, kb_ref, w_ref, u_ref, p_ref, s_ref, pulled_ref, local_ref, q0
):
    dim = q0.shape[1]
    tokens = query_ref.shape[1]
    blocks = tokens // HALF
    fill_rows(q0, halo_ref[0][:, :dim], query_ref[0])
    cq = cq_ref[0]
    row = lax.broadcasted_iota(jnp.int32, (HALF, BLOCK), 0)
    col = lax.broadcasted_iota(jnp.int32, (HALF, BLOCK), 1)
    causal = step_time(col) <= 2 * row + 1
    for n in range(blocks):
        rows = slice(n * HALF, (n + 1) * HALF)
        query = conv_taps(q0, cq, n * HALF, HALF)
        scores = split(jnp.where(causal, mm(split(query), kb_ref[0, n]), 0.0))
        pulled = query - mm(scores, w_ref[0, n])
        local = mm(scores, u_ref[0, n])
        pulled = split(pulled)
        local_ref[0, rows] = local + mm(pulled, s_ref[0, n])
        pulled_ref[0, rows] = split(mm(pulled, p_ref[0, n]))


def out_kernel(pulled_ref, local_ref, state_ref, gain_ref, out_ref):
    raw = mm(pulled_ref[0], split(state_ref[0])) + local_ref[0]
    mean = jnp.mean(raw * raw, 1, keepdims=True)
    out_ref[0] = raw * lax.rsqrt(mean + 1e-06) * gain_ref[0]


def head_spec(shape):
    rest = tuple(shape[1:])
    return pl.BlockSpec((1,) + rest, lambda h: (h,) + (0,) * len(rest))


def call(kernel, args, outs, scratch=()):
    outs = [jax.ShapeDtypeStruct(s, t) for s, t in outs]
    return pl.pallas_call(
        kernel,
        grid=(args[0].shape[0],),
        in_specs=[head_spec(a.shape) for a in args],
        out_specs=[head_spec(o.shape) for o in outs],
        out_shape=outs,
        scratch_shapes=list(scratch),
        compiler_params=pltpu.CompilerParams(vmem_limit_bytes=56 << 20),
    )(*args)


def compose(later, earlier):
    dim = later.shape[1]
    prod = jnp.einsum(
        "hij,hjk->hik", later[:, :, :dim], earlier, precision=lax.Precision.HIGHEST
    )
    cols = earlier.shape[2]
    return prod + jnp.where(
        jnp.arange(cols)[None, None, :] >= cols - dim, later[:, :, 2 * dim - cols :], 0.0
    )


def swap(x, bit, count):
    return lax.ppermute(x, "seq", [(i, i ^ bit) for i in range(count)])


def start_state(total):
    heads, dim, _ = total.shape
    count = lax.axis_size("seq")
    index = lax.axis_index("seq")
    current = total
    earlier_maps = []
    bit = 1
    while bit < count and current.shape[0] % 2 == 0:
        half = current.shape[0] // 2
        upper = (index & bit) != 0
        mine = jnp.where(upper, current[half:], current[:half])
        got = swap(jnp.where(upper, current[:half], current[half:]), bit, count)
        earlier = jnp.where(upper, got, mine)
        later = jnp.where(upper, mine, got)
        earlier_maps.append((bit, earlier))
        current = compose(later, earlier)
        bit *= 2
    stride = bit
    groups = count // stride
    hop = 1
    while hop < groups - 1:
        got = lax.ppermute(
            current, "seq", [(i, i + hop * stride) for i in range(count - hop * stride)]
        )
        current = compose(current, got)
        hop *= 2
    state = current[:, :, dim:]
    state = lax.ppermute(state, "seq", [(i, i + stride) for i in range(count - stride)])
    for bit, earlier in reversed(earlier_maps):
        upper = (index & bit) != 0
        after = compose(earlier, state)
        got = swap(jnp.where(upper, state, after), bit, count)
        mine = jnp.where(upper, after, state)
        state = jnp.concatenate(
            [jnp.where(upper, got, mine), jnp.where(upper, mine, got)], 0
        )
    return state


def per_device(
    queries, key_pairs, value_pairs, write_rates, conv_query, conv_key, conv_value, out_gain
):
    heads, tokens, dim = queries.shape
    blocks = tokens // HALF
    rim = conv_query.shape[1] - 1
    count = lax.axis_size("seq")
    tails = jnp.concatenate(
        [x[:, tokens - rim :] for x in (queries, key_pairs, value_pairs)], 2
    )
    halo = lax.ppermute(tails, "seq", [(i, i + 1) for i in range(count - 1)])
    rates = write_rates.reshape(heads, 1, 2 * tokens)
    wide = (heads, blocks, BLOCK, 2 * dim)
    rows = pltpu.VMEM((tokens + 8, dim), f32)
    kb, w, u, p, s, total = call(
        maps_kernel,
        (key_pairs, value_pairs, halo, rates, conv_key, conv_value),
        [(wide, bf16)] * 5 + [((heads, dim, 2 * dim), f32)],
        [rows] * 4
        + [
            pltpu.VMEM((blocks, BLOCK, 4 * dim), bf16),
            pltpu.VMEM((blocks, BLOCK, BLOCK), f32),
            pltpu.VMEM((blocks, BLOCK, 2 * BLOCK), bf16),
            pltpu.VMEM((blocks * GROUP, BLOCK), f32),
            pltpu.VMEM((blocks * GROUP, BLOCK), f32),
            pltpu.VMEM((blocks, BLOCK), f32),
        ],
    )
    pulled, local = call(
        reads_kernel,
        (queries, halo, conv_query, kb, w, u, p, s),
        [((heads, tokens, 2 * dim), bf16), ((heads, tokens, dim), f32)],
        [rows],
    )
    state = start_state(total)
    return call(
        out_kernel,
        (pulled, local, state, out_gain.reshape(heads, 1, dim)),
        [((heads, tokens, dim), f32)],
    )[0]


def solution(mesh):
    return jax.shard_map(
        per_device,
        mesh=mesh,
        in_specs=(
            P(None, ("grp", "seq"), None),
            P(None, ("grp", "seq"), None),
            P(None, ("grp", "seq"), None),
            P(None, ("grp", "seq")),
            P(),
            P(),
            P(),
            P(),
        ),
        out_specs=P(None, ("grp", "seq"), None),
        check_vma=False,
    )
```

```python
import jax
import jax.numpy as jnp
from jax import lax
from jax.experimental import pallas as pl
from jax.experimental.pallas import tpu as pltpu
from jax.sharding import PartitionSpec as P

BLOCK = 128
GROUP = 16
HALF = BLOCK // 2

f32 = jnp.float32
bf16 = jnp.bfloat16


def split(x):
    high = x.astype(bf16)
    low = (x - high.astype(f32)).astype(bf16)
    return jnp.concatenate([high, low], 1)


def mm(a, b):
    n = b.shape[1] // 2
    p = jnp.dot(a, jnp.concatenate([b, b], 0), preferred_element_type=f32)
    return p[:, :n] + p[:, n:]


def pick_row(x, r):
    row = lax.broadcasted_iota(jnp.int32, x.shape, 0)
    return jnp.sum(jnp.where(row == r, x, 0.0), 0, keepdims=True)


def silu(x):
    return x / (1.0 + jnp.exp(-x))


def step_time(r):
    return (r // GROUP) * GROUP + 2 * (r % 8) + (r // 8) % 2


def interleave(a, b):
    parts = []
    for g in range(0, a.shape[0], 8):
        parts += [a[g : g + 8], b[g : g + 8]]
    return jnp.concatenate(parts, 0)


def conv_taps(ref, weights, start, count):
    taps = weights.shape[0]
    total = weights[0:1] * ref[pl.ds(start + 9 - taps, count), :]
    for s in range(1, taps):
        total = total + weights[s : s + 1] * ref[pl.ds(start + 9 - taps + s, count), :]
    return silu(total)


def fill_rows(ref, halo, rows):
    rim = halo.shape[0]
    ref[8 - rim : 8, :] = halo.astype(f32)
    ref[8:, :] = rows.astype(f32)


def maps_kernel(
    first_ref, key_ref, value_ref, halo_ref, rate_ref, ck_ref, cv_ref,
    kb_ref, w_ref, u_ref, p_ref, s_ref, total_ref,
    k0, k1, v0, v1, kv, nref, dref, cref, xref, brow,
):
    head = first_ref[0] + pl.program_id(0)
    dim = k0.shape[1]
    tokens = key_ref.shape[1]
    blocks = tokens // HALF
    halo = halo_ref[0]
    fill_rows(k0, halo[:, dim : 2 * dim], key_ref[0, :, :dim])
    fill_rows(k1, halo[:, 2 * dim : 3 * dim], key_ref[0, :, dim:])
    fill_rows(v0, halo[:, 3 * dim : 4 * dim], value_ref[0, :, :dim])
    fill_rows(v1, halo[:, 4 * dim :], value_ref[0, :, dim:])
    ck = ck_ref[0]
    cv = cv_ref[0]

    row = lax.broadcasted_iota(jnp.int32, (BLOCK, BLOCK), 0)
    col = lax.broadcasted_iota(jnp.int32, (BLOCK, BLOCK), 1)
    for n in range(blocks):
        brow[n : n + 1, :] = pick_row(rate_ref[:, n * BLOCK : (n + 1) * BLOCK], head)
    order = (row == step_time(col)).astype(f32)
    rates = jnp.dot(brow[...], order, precision=lax.Precision.HIGHEST, preferred_element_type=f32)

    strict = step_time(col) < step_time(row)
    lane = lax.broadcasted_iota(jnp.int32, (GROUP, BLOCK), 1)
    eye = (row == col).astype(f32)

    for n in range(blocks):
        t0 = n * HALF
        ka = conv_taps(k0, ck[:, :dim], t0, HALF)
        kb = conv_taps(k1, ck[:, dim:], t0, HALF)
        keys = interleave(ka, kb)
        keys = keys * lax.rsqrt(jnp.sum(keys * keys, 1, keepdims=True) + 1e-06)
        va = conv_taps(v0, cv[:, :dim], t0, HALF)
        vb = conv_taps(v1, cv[:, dim:], t0, HALF)
        ks = split(keys)
        kv[n, :, : 2 * dim] = ks
        kv[n, :, 2 * dim :] = split(interleave(va, vb))
        kbs = split(keys.T * rates[n : n + 1, :])
        kb_ref[0, n] = kbs
        lower = jnp.where(strict, mm(ks, kbs), 0.0)
        nref[n] = lower
        diag = jnp.zeros((GROUP, BLOCK), f32)
        for g in range(BLOCK // GROUP):
            diag = jnp.where(lane // GROUP == g, lower[g * GROUP : (g + 1) * GROUP], diag)
        cref[n * GROUP : (n + 1) * GROUP, :] = diag

    lane8 = lax.broadcasted_iota(jnp.int32, (blocks, BLOCK), 1)
    times = [t // 2 + 8 * (t % 2) for t in range(GROUP)]
    coef = [cref[pl.ds(r, blocks, stride=GROUP), :] for r in range(GROUP)]
    sol = [(lane8 % GROUP == r).astype(f32) for r in range(GROUP)]
    for i, s in enumerate(times):
        pick = (lane8 // GROUP) * GROUP + s
        for r in times[i + 1 :]:
            sol[r] = sol[r] - jnp.take_along_axis(coef[r], pick, axis=1) * sol[s]
    for r in range(GROUP):
        xref[pl.ds(r, blocks, stride=GROUP), :] = sol[r]
    for n in range(blocks):
        base = xref[n * GROUP : (n + 1) * GROUP, :]
        dref[n] = split(
            jnp.concatenate(
                [jnp.where(lane // GROUP == g, base, 0.0) for g in range(BLOCK // GROUP)], 0
            )
        )

    lane_h = lax.broadcasted_iota(jnp.int32, (HALF, BLOCK), 1)
    row_h = lax.broadcasted_iota(jnp.int32, (HALF, BLOCK), 0)
    size = GROUP
    while size < BLOCK:
        keep = lane_h // size == 2 * (row_h // size)
        starts = range(size, BLOCK, 2 * size)
        for n in range(blocks):
            inv = dref[n]
            low = jnp.concatenate([nref[n, a : a + size] for a in starts], 0)
            z = split(mm(split(jnp.where(keep, low, 0.0)), inv))
            twice = []
            for i in range(len(starts)):
                twice += [z[i * size : (i + 1) * size]] * 2
            odd = jnp.concatenate([inv[a : a + size] for a in starts], 0)
            new = mm(odd, jnp.concatenate(twice, 0))
            new = split(odd[:, :BLOCK].astype(f32) + odd[:, BLOCK:].astype(f32) - new)
            for i, a in enumerate(starts):
                dref[n, a : a + size] = new[i * size : (i + 1) * size]
        size *= 2

    before_map = split(eye)
    before_state = jnp.zeros((dim, 2 * dim), bf16)
    state = jnp.zeros((dim, dim), f32)
    for n in range(blocks):
        inv = dref[n]
        w = split(mm(inv, kv[n, :, : 2 * dim]))
        u = split(mm(inv, kv[n, :, 2 * dim :]))
        w_ref[0, n] = w
        u_ref[0, n] = u
        p_ref[0, n] = before_map
        s_ref[0, n] = before_state
        kbs = kb_ref[0, n]
        move = split(eye - mm(kbs, w))
        written = mm(kbs, u)
        map_now = mm(move, before_map)
        state = mm(move, before_state) + written
        before_map = split(map_now)
        before_state = split(state)
        if n == blocks - 1:
            total_ref[0, :, :dim] = map_now
            total_ref[0, :, dim:] = state


def reads_kernel(
    first_ref, query_ref, halo_ref, cq_ref, kb_ref, w_ref, u_ref, p_ref, s_ref, *rest
):
    pulled_ref, local_ref, q0 = rest[-3:]
    dim = q0.shape[1]
    tokens = query_ref.shape[1]
    blocks = tokens // HALF
    fill_rows(q0, halo_ref[0][:, :dim], query_ref[0])
    cq = cq_ref[0]
    row = lax.broadcasted_iota(jnp.int32, (HALF, BLOCK), 0)
    col = lax.broadcasted_iota(jnp.int32, (HALF, BLOCK), 1)
    causal = step_time(col) <= 2 * row + 1
    for n in range(blocks):
        rows = slice(n * HALF, (n + 1) * HALF)
        query = conv_taps(q0, cq, n * HALF, HALF)
        scores = split(jnp.where(causal, mm(split(query), kb_ref[0, n]), 0.0))
        pulled = query - mm(scores, w_ref[0, n])
        local = mm(scores, u_ref[0, n])
        pulled = split(pulled)
        local_ref[0, rows] = local + mm(pulled, s_ref[0, n])
        pulled_ref[0, rows] = split(mm(pulled, p_ref[0, n]))


def out_kernel(first_ref, pulled_ref, local_ref, kept_ref, sent_ref, gain_ref, out_ref):
    heads = kept_ref.shape[0]
    h = pl.program_id(0)
    slot = h % heads
    state = jnp.where(h // heads == first_ref[0], kept_ref[slot], sent_ref[slot])
    raw = mm(pulled_ref[0], split(state)) + local_ref[0]
    mean = jnp.mean(raw * raw, 1, keepdims=True)
    out_ref[0] = raw * lax.rsqrt(mean + 1e-06) * pick_row(gain_ref[...], h)


def then(later, earlier):
    dim = later.shape[0]
    prod = mm(split(later[:, :dim]), split(earlier))
    wide = prod.shape[1]
    if wide == dim:
        return prod + later[:, dim:]
    return jnp.concatenate([prod[:, :dim], prod[:, dim:] + later[:, dim:]], 1)


def pair_kernel(upper_ref, mine_ref, got_ref, total_ref, earlier_ref):
    upper = upper_ref[0] != 0
    for h in range(mine_ref.shape[0]):
        mine = mine_ref[h]
        got = got_ref[h]
        earlier = jnp.where(upper, got, mine)
        earlier_ref[h] = earlier
        total_ref[h] = then(jnp.where(upper, mine, got), earlier)


def join_kernel(upper_ref, mine_ref, got_ref, before_ref, total_ref, after_ref):
    upper = upper_ref[0] != 0
    dim = mine_ref.shape[1]
    for h in range(mine_ref.shape[0]):
        mine = mine_ref[h]
        got = got_ref[h]
        earlier = jnp.where(upper, got, mine)
        if total_ref.shape[2] == dim:
            earlier = earlier[:, dim:]
        total_ref[h] = then(jnp.where(upper, mine, got), earlier)
        before = before_ref[h]
        after_ref[h] = jnp.where(upper, then(before, got), before)


def down_kernel(upper_ref, before_ref, got_ref, earlier_ref, mine_ref, other_ref):
    upper = upper_ref[0] != 0
    for h in range(before_ref.shape[0]):
        state = then(before_ref[h], got_ref[h])
        after = then(earlier_ref[h], state)
        mine_ref[h] = jnp.where(upper, after, state)
        other_ref[h] = jnp.where(upper, state, after)


def tails_kernel(query_ref, key_ref, value_ref, out_ref):
    rim = out_ref.shape[1]
    at = 0
    for ref in (query_ref, key_ref, value_ref):
        wide = ref.shape[2]
        out_ref[:, :, at : at + wide] = ref[:, ref.shape[1] - rim :, :]
        at += wide


def by_head(a):
    rest = tuple(a.shape[1:])
    return pl.BlockSpec((1,) + rest, lambda i, first: (first[0] + i,) + (0,) * len(rest))


def by_slot(a, slot=0):
    rest = tuple(a.shape[1:])
    return pl.BlockSpec((1,) + rest, lambda i, first: (slot + i,) + (0,) * len(rest))


def whole(a):
    return pl.BlockSpec(a.shape, lambda i, first: (0,) * len(a.shape))


def shape(dims, dtype):
    return jax.ShapeDtypeStruct(dims, dtype)


def call(kernel, steps, first, args, outs, scratch=(), aliases={}):
    return pl.pallas_call(
        kernel,
        grid_spec=pltpu.PrefetchScalarGridSpec(
            num_scalar_prefetch=1,
            grid=(steps,),
            in_specs=[spec for _, spec in args],
            out_specs=[spec for _, spec in outs],
            scratch_shapes=list(scratch),
        ),
        out_shape=[a for a, _ in outs],
        input_output_aliases=aliases,
        compiler_params=pltpu.CompilerParams(vmem_limit_bytes=56 << 20),
    )(first, *[a for a, _ in args])


def small(kernel, flag, args, outs):
    smem = pl.BlockSpec(memory_space=pltpu.SMEM)
    vmem = pl.BlockSpec(memory_space=pltpu.VMEM)
    return pl.pallas_call(
        kernel,
        in_specs=[smem] + [vmem] * len(args),
        out_specs=[vmem] * len(outs),
        out_shape=outs,
    )(flag, *args)


def swap(x, bit, count):
    return lax.ppermute(x, "seq", [(i, i ^ bit) for i in range(count)])


def per_device(
    queries, key_pairs, value_pairs, write_rates, conv_query, conv_key, conv_value, out_gain
):
    heads, tokens, dim = queries.shape
    blocks = tokens // HALF
    half = heads // 2
    rim = conv_query.shape[1] - 1
    count = lax.axis_size("seq")
    index = lax.axis_index("seq")

    def flag(bit):
        return ((index & bit) != 0).astype(jnp.int32).reshape(1)

    last = [
        pl.BlockSpec((heads, 16, x.shape[2]), lambda i: (0, tokens // 16 - 1, 0))
        for x in (queries, key_pairs, value_pairs)
    ]
    tails = pl.pallas_call(
        tails_kernel,
        grid=(1,),
        in_specs=last,
        out_specs=pl.BlockSpec((heads, rim, 5 * dim), lambda i: (0, 0, 0)),
        out_shape=shape((heads, rim, 5 * dim), bf16),
    )(queries, key_pairs, value_pairs)
    halo = lax.ppermute(tails, "seq", [(i, i + 1) for i in range(count - 1)])

    upper = flag(1)
    keep_first = upper * half
    send_first = half - keep_first
    rows = pltpu.VMEM((tokens + 8, dim), f32)
    wide = shape((half, blocks, BLOCK, 2 * dim), bf16)
    total_shape = shape((half, dim, 2 * dim), f32)
    state_shape = shape((half, dim, dim), f32)

    def maps(first):
        outs = [wide] * 5 + [total_shape]
        ins = (key_pairs, value_pairs, halo)
        return call(
            maps_kernel,
            half,
            first,
            [(a, by_head(a)) for a in ins]
            + [(write_rates, whole(write_rates))]
            + [(a, by_head(a)) for a in (conv_key, conv_value)],
            [(a, by_slot(a)) for a in outs],
            [rows] * 4
            + [
                pltpu.VMEM((blocks, BLOCK, 4 * dim), bf16),
                pltpu.VMEM((blocks, BLOCK, BLOCK), f32),
                pltpu.VMEM((blocks, BLOCK, 2 * BLOCK), bf16),
                pltpu.VMEM((blocks * GROUP, BLOCK), f32),
                pltpu.VMEM((blocks * GROUP, BLOCK), f32),
                pltpu.VMEM((blocks, BLOCK), f32),
            ],
        )

    out_arrays = (shape((heads, tokens, 2 * dim), bf16), shape((heads, tokens, dim), f32))
    any_spec = pl.BlockSpec(memory_space=pl.ANY)

    def reads(first, slot, saved, before):
        args = [(a, by_head(a)) for a in (queries, halo, conv_query)]
        args += [(a, by_slot(a, slot)) for a in saved]
        n = len(args) + 1
        args += [(a, any_spec) for a in before]
        aliases = {n + i: i for i in range(len(before))}
        return call(
            reads_kernel, 1, first + slot, args, [(a, by_head(a)) for a in out_arrays], [rows], aliases
        )

    *sent_saved, sent_total = maps(send_first)
    got = swap(sent_total, 1, count)
    *kept_saved, kept_total = maps(keep_first)
    work = [(send_first, i, sent_saved) for i in range(half)]
    work += [(keep_first, i, kept_saved) for i in range(half)]
    read = ()

    def beside(x, got, pieces):
        nonlocal read
        for _ in range(min(pieces, len(work))):
            first, slot, saved = work.pop(0)
            saved, _ = lax.optimization_barrier((saved, x))
            read = reads(first, slot, saved, read)
        if pieces:
            got, read = lax.optimization_barrier((got, tuple(read)))
        return got

    current, earlier = small(pair_kernel, upper, (kept_total, got), [total_shape] * 2)
    before = jnp.broadcast_to(
        jnp.concatenate([jnp.eye(dim, dtype=f32), jnp.zeros((dim, dim), f32)], 1),
        (half, dim, 2 * dim),
    )
    bit = 2
    while bit < count // 2:
        got = beside(current, swap(current, bit, count), 1 if bit == 2 else 2)
        final = 2 * bit >= count // 2
        current, before = small(
            join_kernel,
            flag(bit),
            (current, got, before),
            [state_shape if final else total_shape, total_shape],
        )
        bit *= 2
    got = lax.ppermute(current, "seq", [(i, i + bit) for i in range(count - bit)])
    got = beside(current, got, len(work))
    mine, other = small(down_kernel, upper, (before, got, earlier), [state_shape] * 2)
    other = swap(other, 1, count)
    pulled, local = read
    return call(
        out_kernel,
        heads,
        upper,
        [(pulled, by_slot(pulled)), (local, by_slot(local))]
        + [(a, whole(a)) for a in (mine, other, out_gain)],
        [(out_arrays[1], by_slot(out_arrays[1]))],
    )[0]


def solution(mesh):
    return jax.shard_map(
        per_device,
        mesh=mesh,
        in_specs=(
            P(None, ("grp", "seq"), None),
            P(None, ("grp", "seq"), None),
            P(None, ("grp", "seq"), None),
            P(None, ("grp", "seq")),
            P(),
            P(),
            P(),
            P(),
        ),
        out_specs=P(None, ("grp", "seq"), None),
        check_vma=False,
    )
```

```python
import functools

import jax
import jax.numpy as jnp
from jax import lax
from jax.experimental import pallas as pl
from jax.experimental.pallas import tpu as pltpu
from jax.sharding import PartitionSpec as P

BLOCK = 128
GROUP = 16
HALF = BLOCK // 2
LIMIT = 12 << 20

f32 = jnp.float32
bf16 = jnp.bfloat16


def split(x):
    high = x.astype(bf16)
    low = (x - high.astype(f32)).astype(bf16)
    return jnp.concatenate([high, low], 1)


def mm(a, b):
    n = b.shape[1] // 2
    p = jnp.dot(a, jnp.concatenate([b, b], 0), preferred_element_type=f32)
    return p[:, :n] + p[:, n:]


def pick_row(x, r):
    row = lax.broadcasted_iota(jnp.int32, x.shape, 0)
    return jnp.sum(jnp.where(row == r, x, 0.0), 0, keepdims=True)


def silu(x):
    return x / (1.0 + jnp.exp(-x))


def step_time(r):
    return (r // GROUP) * GROUP + 2 * (r % 8) + (r // 8) % 2


def interleave(a, b):
    parts = []
    for g in range(0, a.shape[0], 8):
        parts += [a[g : g + 8], b[g : g + 8]]
    return jnp.concatenate(parts, 0)


def conv_taps(ref, weights, start, count):
    taps = weights.shape[0]
    total = weights[0:1] * ref[pl.ds(start + 9 - taps, count), :]
    for s in range(1, taps):
        total = total + weights[s : s + 1] * ref[pl.ds(start + 9 - taps + s, count), :]
    return silu(total)


def fill_rows(ref, halo, rows):
    rim = halo.shape[0]
    ref[8 - rim : 8, :] = halo.astype(f32)
    ref[8:, :] = rows.astype(f32)


def first_head(index_ref, kept, half):
    upper = index_ref[0] & 1
    return (upper if kept else 1 - upper) * half


def maps_kernel(
    kept, index_ref, key_ref, value_ref, halo_ref, rate_ref, ck_ref, cv_ref,
    kb_ref, w_ref, u_ref, p_ref, s_ref, total_ref,
    k0, k1, v0, v1, kv, nref, dref, cref, xref, brow,
):
    first = first_head(index_ref, kept, total_ref.shape[0])

    def one(slot, carry):
        one_head_maps(
            slot, first + slot, key_ref, value_ref, halo_ref, rate_ref, ck_ref, cv_ref,
            kb_ref, w_ref, u_ref, p_ref, s_ref, total_ref,
            k0, k1, v0, v1, kv, nref, dref, cref, xref, brow,
        )
        return carry

    lax.fori_loop(0, total_ref.shape[0], one, 0)


def one_head_maps(
    slot, head, key_ref, value_ref, halo_ref, rate_ref, ck_ref, cv_ref,
    kb_ref, w_ref, u_ref, p_ref, s_ref, total_ref,
    k0, k1, v0, v1, kv, nref, dref, cref, xref, brow,
):
    dim = k0.shape[1]
    tokens = key_ref.shape[1]
    blocks = tokens // HALF
    halo = halo_ref[head]
    fill_rows(k0, halo[:, dim : 2 * dim], key_ref[head, :, :dim])
    fill_rows(k1, halo[:, 2 * dim : 3 * dim], key_ref[head, :, dim:])
    fill_rows(v0, halo[:, 3 * dim : 4 * dim], value_ref[head, :, :dim])
    fill_rows(v1, halo[:, 4 * dim :], value_ref[head, :, dim:])
    ck = ck_ref[head]
    cv = cv_ref[head]

    row = lax.broadcasted_iota(jnp.int32, (BLOCK, BLOCK), 0)
    col = lax.broadcasted_iota(jnp.int32, (BLOCK, BLOCK), 1)
    for n in range(blocks):
        brow[n : n + 1, :] = pick_row(rate_ref[:, n * BLOCK : (n + 1) * BLOCK], head)
    order = (row == step_time(col)).astype(f32)
    rates = jnp.dot(brow[...], order, precision=lax.Precision.HIGHEST, preferred_element_type=f32)

    strict = step_time(col) < step_time(row)
    lane = lax.broadcasted_iota(jnp.int32, (GROUP, BLOCK), 1)
    eye = (row == col).astype(f32)

    for n in range(blocks):
        t0 = n * HALF
        ka = conv_taps(k0, ck[:, :dim], t0, HALF)
        kb = conv_taps(k1, ck[:, dim:], t0, HALF)
        keys = interleave(ka, kb)
        keys = keys * lax.rsqrt(jnp.sum(keys * keys, 1, keepdims=True) + 1e-06)
        va = conv_taps(v0, cv[:, :dim], t0, HALF)
        vb = conv_taps(v1, cv[:, dim:], t0, HALF)
        ks = split(keys)
        kv[n, :, : 2 * dim] = ks
        kv[n, :, 2 * dim :] = split(interleave(va, vb))
        kbs = split(keys.T * rates[n : n + 1, :])
        kb_ref[slot, n] = kbs
        lower = jnp.where(strict, mm(ks, kbs), 0.0)
        nref[n] = lower
        diag = jnp.zeros((GROUP, BLOCK), f32)
        for g in range(BLOCK // GROUP):
            diag = jnp.where(lane // GROUP == g, lower[g * GROUP : (g + 1) * GROUP], diag)
        cref[n * GROUP : (n + 1) * GROUP, :] = diag

    lane8 = lax.broadcasted_iota(jnp.int32, (blocks, BLOCK), 1)
    times = [t // 2 + 8 * (t % 2) for t in range(GROUP)]
    coef = [cref[pl.ds(r, blocks, stride=GROUP), :] for r in range(GROUP)]
    sol = [(lane8 % GROUP == r).astype(f32) for r in range(GROUP)]
    for i, s in enumerate(times):
        pick = (lane8 // GROUP) * GROUP + s
        for r in times[i + 1 :]:
            sol[r] = sol[r] - jnp.take_along_axis(coef[r], pick, axis=1) * sol[s]
    for r in range(GROUP):
        xref[pl.ds(r, blocks, stride=GROUP), :] = sol[r]
    for n in range(blocks):
        base = xref[n * GROUP : (n + 1) * GROUP, :]
        dref[n] = split(
            jnp.concatenate(
                [jnp.where(lane // GROUP == g, base, 0.0) for g in range(BLOCK // GROUP)], 0
            )
        )

    lane_h = lax.broadcasted_iota(jnp.int32, (HALF, BLOCK), 1)
    row_h = lax.broadcasted_iota(jnp.int32, (HALF, BLOCK), 0)
    size = GROUP
    while size < BLOCK:
        keep = lane_h // size == 2 * (row_h // size)
        starts = range(size, BLOCK, 2 * size)
        for n in range(blocks):
            inv = dref[n]
            low = jnp.concatenate([nref[n, a : a + size] for a in starts], 0)
            z = split(mm(split(jnp.where(keep, low, 0.0)), inv))
            twice = []
            for i in range(len(starts)):
                twice += [z[i * size : (i + 1) * size]] * 2
            odd = jnp.concatenate([inv[a : a + size] for a in starts], 0)
            new = mm(odd, jnp.concatenate(twice, 0))
            new = split(odd[:, :BLOCK].astype(f32) + odd[:, BLOCK:].astype(f32) - new)
            for i, a in enumerate(starts):
                dref[n, a : a + size] = new[i * size : (i + 1) * size]
        size *= 2

    before_map = split(eye)
    before_state = jnp.zeros((dim, 2 * dim), bf16)
    state = jnp.zeros((dim, dim), f32)
    for n in range(blocks):
        inv = dref[n]
        w = split(mm(inv, kv[n, :, : 2 * dim]))
        u = split(mm(inv, kv[n, :, 2 * dim :]))
        w_ref[slot, n] = w
        u_ref[slot, n] = u
        p_ref[slot, n] = before_map
        s_ref[slot, n] = before_state
        kbs = kb_ref[slot, n]
        move = split(eye - mm(kbs, w))
        written = mm(kbs, u)
        map_now = mm(move, before_map)
        state = mm(move, before_state) + written
        before_map = split(map_now)
        before_state = split(state)
        if n == blocks - 1:
            total_ref[slot, :, :dim] = map_now
            total_ref[slot, :, dim:] = state


def reads_kernel(
    kept, slot, index_ref, query_ref, halo_ref, cq_ref, kb_ref, w_ref, u_ref, p_ref, s_ref,
    pulled_ref, local_ref, q0,
):
    head = first_head(index_ref, kept, w_ref.shape[0]) + slot
    dim = q0.shape[1]
    tokens = query_ref.shape[1]
    blocks = tokens // HALF
    fill_rows(q0, halo_ref[head][:, :dim], query_ref[head])
    cq = cq_ref[head]
    row = lax.broadcasted_iota(jnp.int32, (HALF, BLOCK), 0)
    col = lax.broadcasted_iota(jnp.int32, (HALF, BLOCK), 1)
    causal = step_time(col) <= 2 * row + 1
    for n in range(blocks):
        rows = slice(n * HALF, (n + 1) * HALF)
        query = conv_taps(q0, cq, n * HALF, HALF)
        scores = split(jnp.where(causal, mm(split(query), kb_ref[slot, n]), 0.0))
        pulled = query - mm(scores, w_ref[slot, n])
        local = mm(scores, u_ref[slot, n])
        pulled = split(pulled)
        local_ref[rows] = local + mm(pulled, s_ref[slot, n])
        pulled_ref[rows] = split(mm(pulled, p_ref[slot, n]))


def out_kernel(index_ref, mine_ref, other_ref, gain_ref, *rest):
    out_ref = rest[-1]
    half = mine_ref.shape[0]
    for i in range(2 * half):

        @pl.when(pl.program_id(0) == i)
        def _():
            kept = i < half
            slot = i % half
            h = first_head(index_ref, kept, half) + slot
            state = mine_ref[slot] if kept else other_ref[slot]
            raw = mm(rest[2 * i][...], split(state)) + rest[2 * i + 1][...]
            mean = jnp.mean(raw * raw, 1, keepdims=True)
            out_ref[0] = raw * lax.rsqrt(mean + 1e-06) * pick_row(gain_ref[...], h)


def then(later, earlier):
    dim = later.shape[0]
    prod = mm(split(later[:, :dim]), split(earlier))
    wide = prod.shape[1]
    if wide == dim:
        return prod + later[:, dim:]
    return jnp.concatenate([prod[:, :dim], prod[:, dim:] + later[:, dim:]], 1)


def pair_kernel(index_ref, mine_ref, got_ref, total_ref, earlier_ref):
    upper = (index_ref[0] & 1) != 0
    for h in range(mine_ref.shape[0]):
        mine = mine_ref[h]
        got = got_ref[h]
        earlier = jnp.where(upper, got, mine)
        earlier_ref[h] = earlier
        total_ref[h] = then(jnp.where(upper, mine, got), earlier)


def join_kernel(bit, index_ref, mine_ref, got_ref, *rest):
    *before_ref, total_ref, after_ref = rest
    upper = (index_ref[0] & bit) != 0
    dim = mine_ref.shape[1]
    row = lax.broadcasted_iota(jnp.int32, (dim, 2 * dim), 0)
    col = lax.broadcasted_iota(jnp.int32, (dim, 2 * dim), 1)
    for h in range(mine_ref.shape[0]):
        mine = mine_ref[h]
        got = got_ref[h]
        earlier = jnp.where(upper, got, mine)
        if total_ref.shape[2] == dim:
            earlier = earlier[:, dim:]
        total_ref[h] = then(jnp.where(upper, mine, got), earlier)
        if before_ref:
            before = before_ref[0][h]
            after_ref[h] = jnp.where(upper, then(before, got), before)
        else:
            after_ref[h] = jnp.where(upper, got, (row == col).astype(f32))


def down_kernel(index_ref, before_ref, got_ref, earlier_ref, mine_ref, other_ref):
    upper = (index_ref[0] & 1) != 0
    for h in range(before_ref.shape[0]):
        state = then(before_ref[h], got_ref[h])
        after = then(earlier_ref[h], state)
        mine_ref[h] = jnp.where(upper, after, state)
        other_ref[h] = jnp.where(upper, state, after)


def tails_kernel(index_ref, query_ref, key_ref, value_ref, out_ref):
    rim = out_ref.shape[1]
    at = 0
    for ref in (query_ref, key_ref, value_ref):
        wide = ref.shape[2]
        out_ref[:, :, at : at + wide] = ref[:, ref.shape[1] - rim :, :]
        at += wide


def shape(dims, dtype):
    return jax.ShapeDtypeStruct(dims, dtype)


def resident(kernel, index, args, outs, scratch=(), limit=4 << 20):
    smem = pl.BlockSpec(memory_space=pltpu.SMEM)
    vmem = pl.BlockSpec(memory_space=pltpu.VMEM)
    return pl.pallas_call(
        kernel,
        in_specs=[smem] + [vmem] * len(args),
        out_specs=[vmem] * len(outs),
        out_shape=[pltpu.VMEM(o.shape, o.dtype) for o in outs],
        scratch_shapes=list(scratch),
        compiler_params=pltpu.CompilerParams(vmem_limit_bytes=limit),
    )(index, *[pltpu.with_memory_space_constraint(a, pltpu.VMEM) for a in args])


def swap(x, bit, count):
    return lax.ppermute(x, "seq", [(i, i ^ bit) for i in range(count)])


def per_device(
    queries, key_pairs, value_pairs, write_rates, conv_query, conv_key, conv_value, out_gain
):
    heads, tokens, dim = queries.shape
    blocks = tokens // HALF
    half = heads // 2
    rim = conv_query.shape[1] - 1
    count = lax.axis_size("seq")
    index = lax.axis_index("seq").reshape(1)

    parts = (queries, key_pairs, value_pairs)
    last = [
        pl.BlockSpec((heads, 16, x.shape[2]), lambda i, index_ref: (0, tokens // 16 - 1, 0))
        for x in parts
    ]
    tails = pl.pallas_call(
        tails_kernel,
        grid_spec=pltpu.PrefetchScalarGridSpec(
            num_scalar_prefetch=1,
            grid=(1,),
            in_specs=last,
            out_specs=pl.BlockSpec((heads, rim, 5 * dim), lambda i, index_ref: (0, 0, 0)),
        ),
        out_shape=shape((heads, rim, 5 * dim), bf16),
        compiler_params=pltpu.CompilerParams(vmem_limit_bytes=4 << 20),
    )(index, *[pltpu.with_memory_space_constraint(x, pltpu.HBM) for x in parts])
    halo = lax.ppermute(tails, "seq", [(i, i + 1) for i in range(count - 1)])

    rows = pltpu.VMEM((tokens + 8, dim), f32)
    wide = shape((half, blocks, BLOCK, 2 * dim), bf16)
    total_shape = shape((half, dim, 2 * dim), f32)
    state_shape = shape((half, dim, dim), f32)

    def maps(kept):
        return resident(
            functools.partial(maps_kernel, kept),
            index,
            (key_pairs, value_pairs, halo, write_rates, conv_key, conv_value),
            [wide] * 5 + [total_shape],
            [rows] * 4
            + [
                pltpu.VMEM((blocks, BLOCK, 4 * dim), bf16),
                pltpu.VMEM((blocks, BLOCK, BLOCK), f32),
                pltpu.VMEM((blocks, BLOCK, 2 * BLOCK), bf16),
                pltpu.VMEM((blocks * GROUP, BLOCK), f32),
                pltpu.VMEM((blocks * GROUP, BLOCK), f32),
                pltpu.VMEM((blocks, BLOCK), f32),
            ],
            LIMIT,
        )

    def reads(kept, slot, saved, after):
        at, _ = lax.optimization_barrier((index, after))
        return resident(
            functools.partial(reads_kernel, kept, slot),
            at,
            (queries, halo, conv_query, *saved),
            [shape((tokens, 2 * dim), bf16), shape((tokens, dim), f32)],
            [rows],
            LIMIT,
        )

    *sent_saved, sent_total = maps(False)
    got = swap(sent_total, 1, count)
    *kept_saved, kept_total = maps(True)
    work = [(False, i, sent_saved) for i in range(half)]
    work += [(True, i, kept_saved) for i in range(half)]
    read = {}

    def beside(x, got, pieces):
        for _ in range(min(pieces, len(work))):
            kept, slot, saved = work.pop(0)
            one = reads(kept, slot, saved, x)
            got, read[kept, slot] = lax.optimization_barrier((got, one))
        return got

    current, earlier = resident(pair_kernel, index, (kept_total, got), [total_shape] * 2)
    before = ()
    bit = 2
    while bit < count // 2:
        got = beside(current, swap(current, bit, count), 1 if bit == 2 else 2)
        final = 2 * bit >= count // 2
        current, before = resident(
            functools.partial(join_kernel, bit),
            index,
            (current, got) + ((before,) if bit > 2 else ()),
            [state_shape if final else total_shape, total_shape],
        )
        bit *= 2
    got = lax.ppermute(current, "seq", [(i, i + bit) for i in range(count - bit)])
    got = beside(current, got, len(work))
    mine, other = resident(down_kernel, index, (before, got, earlier), [state_shape] * 2)
    other = swap(other, 1, count)
    pieces = [a for kept in (True, False) for i in range(half) for a in read[kept, i]]
    vmem = pl.BlockSpec(memory_space=pltpu.VMEM)

    def out_block(i, index_ref):
        upper = index_ref[0] & 1
        side = jnp.where(i < half, upper, 1 - upper)
        return (side * half + i % half, 0, 0)

    args = [mine, other, out_gain, *pieces]
    return pl.pallas_call(
        out_kernel,
        grid_spec=pltpu.PrefetchScalarGridSpec(
            num_scalar_prefetch=1,
            grid=(heads,),
            in_specs=[vmem] * len(args),
            out_specs=pl.BlockSpec((1, tokens, dim), out_block),
        ),
        out_shape=shape((heads, tokens, dim), f32),
        compiler_params=pltpu.CompilerParams(vmem_limit_bytes=LIMIT),
    )(index, *[pltpu.with_memory_space_constraint(a, pltpu.VMEM) for a in args])


def solution(mesh):
    return jax.shard_map(
        per_device,
        mesh=mesh,
        in_specs=(
            P(None, ("grp", "seq"), None),
            P(None, ("grp", "seq"), None),
            P(None, ("grp", "seq"), None),
            P(None, ("grp", "seq")),
            P(),
            P(),
            P(),
            P(),
        ),
        out_specs=P(None, ("grp", "seq"), None),
        check_vma=False,
    )
```

```python
import functools

import jax
import jax.numpy as jnp
from jax import lax
from jax.experimental import pallas as pl
from jax.experimental.pallas import tpu as pltpu
from jax.sharding import PartitionSpec as P

BLOCK = 128
GROUP = 16
HALF = BLOCK // 2
LIMIT = 16 << 20

f32 = jnp.float32
bf16 = jnp.bfloat16


def split(x):
    high = x.astype(bf16)
    low = (x - high.astype(f32)).astype(bf16)
    return jnp.concatenate([high, low], 1)


def mm(a, b):
    n = b.shape[1] // 2
    p = jnp.dot(a, jnp.concatenate([b, b], 0), preferred_element_type=f32)
    return p[:, :n] + p[:, n:]


def pick_row(x, r):
    row = lax.broadcasted_iota(jnp.int32, x.shape, 0)
    return jnp.sum(jnp.where(row == r, x, 0.0), 0, keepdims=True)


def silu(x):
    return x / (1.0 + jnp.exp(-x))


def step_time(r):
    return (r // GROUP) * GROUP + 2 * (r % 8) + (r // 8) % 2


def interleave(a, b):
    parts = []
    for g in range(0, a.shape[0], 8):
        parts += [a[g : g + 8], b[g : g + 8]]
    return jnp.concatenate(parts, 0)


def conv_taps(ref, weights, start, count):
    taps = weights.shape[0]
    total = weights[0:1] * ref[pl.ds(start + 9 - taps, count), :]
    for s in range(1, taps):
        total = total + weights[s : s + 1] * ref[pl.ds(start + 9 - taps + s, count), :]
    return silu(total)


def fill_rows(ref, halo, rows):
    rim = halo.shape[0]
    ref[8 - rim : 8, :] = halo.astype(f32)
    ref[8:, :] = rows.astype(f32)


def first_head(index_ref, kept, half):
    upper = index_ref[0] & 1
    return (upper if kept else 1 - upper) * half


def maps_kernel(
    kept, index_ref, key_ref, value_ref, halo_ref, rate_ref, ck_ref, cv_ref,
    kb_ref, w_ref, u_ref, p_ref, s_ref, total_ref,
    rows, kv, nref, dref, cref, xref, brow, move, written,
):
    half, blocks = kb_ref.shape[:2]
    dim = rows.shape[3]
    first = first_head(index_ref, kept, half)
    for slots in (tuple(range(half)),):
        heads_maps(
            slots, first, blocks, dim, key_ref, value_ref, halo_ref, rate_ref, ck_ref, cv_ref,
            kb_ref, w_ref, u_ref, p_ref, s_ref, total_ref,
            rows, kv, nref, dref, cref, xref, brow, move, written,
        )


def heads_maps(
    slots, first, blocks, dim, key_ref, value_ref, halo_ref, rate_ref, ck_ref, cv_ref,
    kb_ref, w_ref, u_ref, p_ref, s_ref, total_ref,
    rows, kv, nref, dref, cref, xref, brow, move, written,
):
    row = lax.broadcasted_iota(jnp.int32, (BLOCK, BLOCK), 0)
    col = lax.broadcasted_iota(jnp.int32, (BLOCK, BLOCK), 1)
    strict = step_time(col) < step_time(row)
    lane = lax.broadcasted_iota(jnp.int32, (GROUP, BLOCK), 1)
    eye = (row == col).astype(f32)
    order = (row == step_time(col)).astype(f32)

    rates = {}
    for h in slots:
        head = first + h
        halo = halo_ref[head]
        for i, ref in enumerate((key_ref, value_ref)):
            for j in range(2):
                at = (1 + 2 * i + j) * dim
                fill_rows(
                    rows.at[h, 2 * i + j], halo[:, at : at + dim], ref[head, :, j * dim : (j + 1) * dim]
                )
        for n in range(blocks):
            brow[h, n : n + 1, :] = pick_row(rate_ref[:, n * BLOCK : (n + 1) * BLOCK], head)
        rates[h] = jnp.dot(
            brow[h], order, precision=lax.Precision.HIGHEST, preferred_element_type=f32
        )

    for h in slots:
        ck = ck_ref[first + h]
        cv = cv_ref[first + h]
        for n in range(blocks):
            t0 = n * HALF
            ka = conv_taps(rows.at[h, 0], ck[:, :dim], t0, HALF)
            kb = conv_taps(rows.at[h, 1], ck[:, dim:], t0, HALF)
            keys = interleave(ka, kb)
            keys = keys * lax.rsqrt(jnp.sum(keys * keys, 1, keepdims=True) + 1e-06)
            va = conv_taps(rows.at[h, 2], cv[:, :dim], t0, HALF)
            vb = conv_taps(rows.at[h, 3], cv[:, dim:], t0, HALF)
            ks = split(keys)
            kv[h, n, :, : 2 * dim] = ks
            kv[h, n, :, 2 * dim :] = split(interleave(va, vb))
            kbs = split(keys.T * rates[h][n : n + 1, :])
            kb_ref[h, n] = kbs
            lower = jnp.where(strict, mm(ks, kbs), 0.0)
            nref[h, n] = lower
            diag = jnp.zeros((GROUP, BLOCK), f32)
            for g in range(BLOCK // GROUP):
                diag = jnp.where(lane // GROUP == g, lower[g * GROUP : (g + 1) * GROUP], diag)
            cref[h, n * GROUP : (n + 1) * GROUP, :] = diag

    lane8 = lax.broadcasted_iota(jnp.int32, (blocks, BLOCK), 1)
    times = [t // 2 + 8 * (t % 2) for t in range(GROUP)]
    for h in slots:
        coef = [cref[h, pl.ds(r, blocks, stride=GROUP), :] for r in range(GROUP)]
        sol = [(lane8 % GROUP == r).astype(f32) for r in range(GROUP)]
        for i, s in enumerate(times):
            pick = (lane8 // GROUP) * GROUP + s
            for r in times[i + 1 :]:
                sol[r] = sol[r] - jnp.take_along_axis(coef[r], pick, axis=1) * sol[s]
        for r in range(GROUP):
            xref[h, pl.ds(r, blocks, stride=GROUP), :] = sol[r]
    for h in slots:
        for n in range(blocks):
            base = xref[h, n * GROUP : (n + 1) * GROUP, :]
            dref[h, n] = split(
                jnp.concatenate(
                    [jnp.where(lane // GROUP == g, base, 0.0) for g in range(BLOCK // GROUP)], 0
                )
            )

    lane_h = lax.broadcasted_iota(jnp.int32, (HALF, BLOCK), 1)
    row_h = lax.broadcasted_iota(jnp.int32, (HALF, BLOCK), 0)
    size = GROUP
    while size < BLOCK:
        keep = lane_h // size == 2 * (row_h // size)
        starts = range(size, BLOCK, 2 * size)
        for h in slots:
            for n in range(blocks):
                inv = dref[h, n]
                low = jnp.concatenate([nref[h, n, a : a + size] for a in starts], 0)
                z = split(mm(split(jnp.where(keep, low, 0.0)), inv))
                twice = []
                for i in range(len(starts)):
                    twice += [z[i * size : (i + 1) * size]] * 2
                odd = jnp.concatenate([inv[a : a + size] for a in starts], 0)
                new = mm(odd, jnp.concatenate(twice, 0))
                new = split(odd[:, :BLOCK].astype(f32) + odd[:, BLOCK:].astype(f32) - new)
                for i, a in enumerate(starts):
                    dref[h, n, a : a + size] = new[i * size : (i + 1) * size]
        size *= 2

    for h in slots:
        for n in range(blocks):
            inv = dref[h, n]
            w_ref[h, n] = split(mm(inv, kv[h, n, :, : 2 * dim]))
            u_ref[h, n] = split(mm(inv, kv[h, n, :, 2 * dim :]))
    for h in slots:
        for n in range(blocks):
            kbs = kb_ref[h, n]
            move[h, n] = split(eye - mm(kbs, w_ref[h, n]))
            written[h, n] = mm(kbs, u_ref[h, n])
    before_map = {h: split(eye) for h in slots}
    before_state = {h: jnp.zeros((dim, 2 * dim), bf16) for h in slots}
    for n in range(blocks):
        for h in slots:
            p_ref[h, n] = before_map[h]
            s_ref[h, n] = before_state[h]
            map_now = mm(move[h, n], before_map[h])
            state = mm(move[h, n], before_state[h]) + written[h, n]
            before_map[h] = split(map_now)
            before_state[h] = split(state)
            if n == blocks - 1:
                total_ref[h, :, :dim] = map_now
                total_ref[h, :, dim:] = state


def reads_kernel(
    kept, slot, index_ref, query_ref, halo_ref, cq_ref, kb_ref, w_ref, u_ref, p_ref, s_ref,
    pulled_ref, local_ref, q0, query, scores, pulled,
):
    head = first_head(index_ref, kept, w_ref.shape[0]) + slot
    dim = q0.shape[1]
    blocks = w_ref.shape[1]
    fill_rows(q0, halo_ref[head][:, :dim], query_ref[head])
    cq = cq_ref[head]
    row = lax.broadcasted_iota(jnp.int32, (HALF, BLOCK), 0)
    col = lax.broadcasted_iota(jnp.int32, (HALF, BLOCK), 1)
    causal = step_time(col) <= 2 * row + 1
    rows = [slice(n * HALF, (n + 1) * HALF) for n in range(blocks)]
    for n in range(blocks):
        q = conv_taps(q0, cq, n * HALF, HALF)
        query[rows[n]] = q
        scores[rows[n]] = split(jnp.where(causal, mm(split(q), kb_ref[slot, n]), 0.0))
    for n in range(blocks):
        pulled[rows[n]] = split(query[rows[n]] - mm(scores[rows[n]], w_ref[slot, n]))
        local_ref[rows[n]] = mm(scores[rows[n]], u_ref[slot, n])
    for n in range(blocks):
        local_ref[rows[n]] += mm(pulled[rows[n]], s_ref[slot, n])
        pulled_ref[rows[n]] = split(mm(pulled[rows[n]], p_ref[slot, n]))


def out_kernel(index_ref, mine_ref, other_ref, gain_ref, *rest):
    out_ref = rest[-1]
    half = mine_ref.shape[0]
    for i in range(2 * half):

        @pl.when(pl.program_id(0) == i)
        def _():
            kept = i < half
            slot = i % half
            h = first_head(index_ref, kept, half) + slot
            state = mine_ref[slot] if kept else other_ref[slot]
            raw = mm(rest[2 * i][...], split(state)) + rest[2 * i + 1][...]
            mean = jnp.mean(raw * raw, 1, keepdims=True)
            out_ref[0] = raw * lax.rsqrt(mean + 1e-06) * pick_row(gain_ref[...], h)


def then(later, earlier):
    dim = later.shape[0]
    prod = mm(split(later[:, :dim]), split(earlier))
    wide = prod.shape[1]
    if wide == dim:
        return prod + later[:, dim:]
    return jnp.concatenate([prod[:, :dim], prod[:, dim:] + later[:, dim:]], 1)


def pair_kernel(index_ref, mine_ref, got_ref, total_ref, earlier_ref):
    upper = (index_ref[0] & 1) != 0
    for h in range(mine_ref.shape[0]):
        mine = mine_ref[h]
        got = got_ref[h]
        earlier = jnp.where(upper, got, mine)
        earlier_ref[h] = earlier
        total_ref[h] = then(jnp.where(upper, mine, got), earlier)


def join_kernel(bit, index_ref, mine_ref, got_ref, *rest):
    *before_ref, total_ref, after_ref = rest
    upper = (index_ref[0] & bit) != 0
    dim = mine_ref.shape[1]
    row = lax.broadcasted_iota(jnp.int32, (dim, 2 * dim), 0)
    col = lax.broadcasted_iota(jnp.int32, (dim, 2 * dim), 1)
    for h in range(mine_ref.shape[0]):
        mine = mine_ref[h]
        got = got_ref[h]
        earlier = jnp.where(upper, got, mine)
        if total_ref.shape[2] == dim:
            earlier = earlier[:, dim:]
        total_ref[h] = then(jnp.where(upper, mine, got), earlier)
        if before_ref:
            before = before_ref[0][h]
            after_ref[h] = jnp.where(upper, then(before, got), before)
        else:
            after_ref[h] = jnp.where(upper, got, (row == col).astype(f32))


def down_kernel(index_ref, before_ref, got_ref, earlier_ref, mine_ref, other_ref):
    upper = (index_ref[0] & 1) != 0
    for h in range(before_ref.shape[0]):
        state = then(before_ref[h], got_ref[h])
        after = then(earlier_ref[h], state)
        mine_ref[h] = jnp.where(upper, after, state)
        other_ref[h] = jnp.where(upper, state, after)


def tails_kernel(index_ref, query_ref, key_ref, value_ref, out_ref):
    rim = out_ref.shape[1]
    at = 0
    for ref in (query_ref, key_ref, value_ref):
        wide = ref.shape[2]
        out_ref[:, :, at : at + wide] = ref[:, ref.shape[1] - rim :, :]
        at += wide


def shape(dims, dtype):
    return jax.ShapeDtypeStruct(dims, dtype)


def resident(kernel, index, args, outs, scratch=(), limit=4 << 20):
    smem = pl.BlockSpec(memory_space=pltpu.SMEM)
    vmem = pl.BlockSpec(memory_space=pltpu.VMEM)
    return pl.pallas_call(
        kernel,
        in_specs=[smem] + [vmem] * len(args),
        out_specs=[vmem] * len(outs),
        out_shape=[pltpu.VMEM(o.shape, o.dtype) for o in outs],
        scratch_shapes=list(scratch),
        compiler_params=pltpu.CompilerParams(vmem_limit_bytes=limit),
    )(index, *[pltpu.with_memory_space_constraint(a, pltpu.VMEM) for a in args])


def maps_call(index, kept, key_pairs, value_pairs, halo, write_rates, conv_key, conv_value):
    heads, tokens, _ = key_pairs.shape
    dim = key_pairs.shape[2] // 2
    half = heads // 2
    blocks = tokens // HALF
    wide = shape((half, blocks, BLOCK, 2 * dim), bf16)
    return resident(
        functools.partial(maps_kernel, kept),
        index,
        (key_pairs, value_pairs, halo, write_rates, conv_key, conv_value),
        [wide] * 5 + [shape((half, dim, 2 * dim), f32)],
        [
            pltpu.VMEM((half, 4, tokens + 8, dim), f32),
            pltpu.VMEM((half, blocks, BLOCK, 4 * dim), bf16),
            pltpu.VMEM((half, blocks, BLOCK, BLOCK), f32),
            pltpu.VMEM((half, blocks, BLOCK, 2 * BLOCK), bf16),
            pltpu.VMEM((half, blocks * GROUP, BLOCK), f32),
            pltpu.VMEM((half, blocks * GROUP, BLOCK), f32),
            pltpu.VMEM((half, blocks, BLOCK), f32),
            pltpu.VMEM((half, blocks, dim, 2 * dim), bf16),
            pltpu.VMEM((half, blocks, dim, dim), f32),
        ],
        LIMIT,
    )


def swap(x, bit, count):
    return lax.ppermute(x, "seq", [(i, i ^ bit) for i in range(count)])


def per_device(
    queries, key_pairs, value_pairs, write_rates, conv_query, conv_key, conv_value, out_gain
):
    heads, tokens, dim = queries.shape
    blocks = tokens // HALF
    half = heads // 2
    rim = conv_query.shape[1] - 1
    count = lax.axis_size("seq")
    index = lax.axis_index("seq").reshape(1)

    parts = (queries, key_pairs, value_pairs)
    last = [
        pl.BlockSpec((heads, 16, x.shape[2]), lambda i, index_ref: (0, tokens // 16 - 1, 0))
        for x in parts
    ]
    tails = pl.pallas_call(
        tails_kernel,
        grid_spec=pltpu.PrefetchScalarGridSpec(
            num_scalar_prefetch=1,
            grid=(1,),
            in_specs=last,
            out_specs=pl.BlockSpec((heads, rim, 5 * dim), lambda i, index_ref: (0, 0, 0)),
        ),
        out_shape=shape((heads, rim, 5 * dim), bf16),
        compiler_params=pltpu.CompilerParams(vmem_limit_bytes=4 << 20),
    )(index, *[pltpu.with_memory_space_constraint(x, pltpu.HBM) for x in parts])
    halo = lax.ppermute(tails, "seq", [(i, i + 1) for i in range(count - 1)])

    total_shape = shape((half, dim, 2 * dim), f32)
    state_shape = shape((half, dim, dim), f32)

    def maps(kept):
        return maps_call(index, kept, key_pairs, value_pairs, halo, write_rates, conv_key, conv_value)

    def reads(kept, slot, saved, after):
        at, _ = lax.optimization_barrier((index, after))
        return resident(
            functools.partial(reads_kernel, kept, slot),
            at,
            (queries, halo, conv_query, *saved),
            [shape((tokens, 2 * dim), bf16), shape((tokens, dim), f32)],
            [
                pltpu.VMEM((tokens + 8, dim), f32),
                pltpu.VMEM((tokens, dim), f32),
                pltpu.VMEM((tokens, 2 * dim), bf16),
                pltpu.VMEM((tokens, 2 * dim), bf16),
            ],
            LIMIT,
        )

    *sent_saved, sent_total = maps(False)
    got = swap(sent_total, 1, count)
    *kept_saved, kept_total = maps(True)
    work = [(False, i, sent_saved) for i in range(half)]
    work += [(True, i, kept_saved) for i in range(half)]
    read = {}

    def beside(x, got, pieces):
        for _ in range(min(pieces, len(work))):
            kept, slot, saved = work.pop(0)
            one = reads(kept, slot, saved, x)
            got, read[kept, slot] = lax.optimization_barrier((got, one))
        return got

    current, earlier = resident(pair_kernel, index, (kept_total, got), [total_shape] * 2)
    before = ()
    bit = 2
    while bit < count // 2:
        got = beside(current, swap(current, bit, count), 1 if bit == 2 else 2)
        final = 2 * bit >= count // 2
        current, before = resident(
            functools.partial(join_kernel, bit),
            index,
            (current, got) + ((before,) if bit > 2 else ()),
            [state_shape if final else total_shape, total_shape],
        )
        bit *= 2
    got = lax.ppermute(current, "seq", [(i, i + bit) for i in range(count - bit)])
    got = beside(current, got, len(work))
    mine, other = resident(down_kernel, index, (before, got, earlier), [state_shape] * 2)
    other = swap(other, 1, count)
    pieces = [a for kept in (True, False) for i in range(half) for a in read[kept, i]]
    vmem = pl.BlockSpec(memory_space=pltpu.VMEM)

    def out_block(i, index_ref):
        upper = index_ref[0] & 1
        side = jnp.where(i < half, upper, 1 - upper)
        return (side * half + i % half, 0, 0)

    args = [mine, other, out_gain, *pieces]
    return pl.pallas_call(
        out_kernel,
        grid_spec=pltpu.PrefetchScalarGridSpec(
            num_scalar_prefetch=1,
            grid=(heads,),
            in_specs=[vmem] * len(args),
            out_specs=pl.BlockSpec((1, tokens, dim), out_block),
        ),
        out_shape=shape((heads, tokens, dim), f32),
        compiler_params=pltpu.CompilerParams(vmem_limit_bytes=LIMIT),
    )(index, *[pltpu.with_memory_space_constraint(a, pltpu.VMEM) for a in args])


def solution(mesh):
    return jax.shard_map(
        per_device,
        mesh=mesh,
        in_specs=(
            P(None, ("grp", "seq"), None),
            P(None, ("grp", "seq"), None),
            P(None, ("grp", "seq"), None),
            P(None, ("grp", "seq")),
            P(),
            P(),
            P(),
            P(),
        ),
        out_specs=P(None, ("grp", "seq"), None),
        check_vma=False,
    )
```

```python
import functools

import jax
import jax.numpy as jnp
from jax import lax
from jax.experimental import pallas as pl
from jax.experimental.pallas import tpu as pltpu
from jax.sharding import PartitionSpec as P

BLOCK = 128
GROUP = 16
HALF = BLOCK // 2
LIMIT = 20 << 20

f32 = jnp.float32
bf16 = jnp.bfloat16


def split(x):
    high = x.astype(bf16)
    low = (x - high.astype(f32)).astype(bf16)
    return jnp.concatenate([high, low], 1)


def mm(a, b):
    n = b.shape[1] // 2
    p = jnp.dot(a, jnp.concatenate([b, b], 0), preferred_element_type=f32)
    return p[:, :n] + p[:, n:]


def pick_row(x, r):
    row = lax.broadcasted_iota(jnp.int32, x.shape, 0)
    return jnp.sum(jnp.where(row == r, x, 0.0), 0, keepdims=True)


def silu(x):
    return x / (1.0 + jnp.exp(-x))


def step_time(r):
    return (r // GROUP) * GROUP + 2 * (r % 8) + (r // 8) % 2


def interleave(a, b):
    parts = []
    for g in range(0, a.shape[0], 8):
        parts += [a[g : g + 8], b[g : g + 8]]
    return jnp.concatenate(parts, 0)


def conv_taps(ref, weights, start, count):
    taps = weights.shape[0]
    total = weights[0:1] * ref[pl.ds(start + 9 - taps, count), :]
    for s in range(1, taps):
        total = total + weights[s : s + 1] * ref[pl.ds(start + 9 - taps + s, count), :]
    return silu(total)


def fill_rows(ref, halo, rows):
    rim = halo.shape[0]
    ref[8 - rim : 8, :] = halo.astype(f32)
    ref[8:, :] = rows.astype(f32)


def first_head(index_ref, kept, half):
    upper = index_ref[0] & 1
    return (upper if kept else 1 - upper) * half


def block_masks():
    row = lax.broadcasted_iota(jnp.int32, (BLOCK, BLOCK), 0)
    col = lax.broadcasted_iota(jnp.int32, (BLOCK, BLOCK), 1)
    lane = lax.broadcasted_iota(jnp.int32, (GROUP, BLOCK), 1)
    return row, col, lane


def block_inputs(key_rows, value_rows, ck, cv, t0, rates):
    row, col, lane = block_masks()
    dim = key_rows[0].shape[1]
    ka, kb = [conv_taps(r, ck[:, j * dim : (j + 1) * dim], t0, HALF) for j, r in enumerate(key_rows)]
    keys = interleave(ka, kb)
    keys = keys * lax.rsqrt(jnp.sum(keys * keys, 1, keepdims=True) + 1e-06)
    va, vb = [conv_taps(r, cv[:, j * dim : (j + 1) * dim], t0, HALF) for j, r in enumerate(value_rows)]
    ks = split(keys)
    kv = jnp.concatenate([ks, split(interleave(va, vb))], 1)
    kbs = split(keys.T * rates)
    lower = jnp.where(step_time(col) < step_time(row), mm(ks, kbs), 0.0)
    diag = jnp.zeros((GROUP, BLOCK), f32)
    for g in range(BLOCK // GROUP):
        diag = jnp.where(lane // GROUP == g, lower[g * GROUP : (g + 1) * GROUP], diag)
    return kv, kbs, lower, diag


def front_kernel(
    index_ref, key_ref, value_ref, rate_ref, ck_ref, cv_ref,
    kv_ref, kb_ref, low_ref, diag_ref, rates_ref, rows, brow,
):
    dim = rows.shape[2]
    blocks = rates_ref.shape[1]
    row, col, _ = block_masks()
    order = (row == step_time(col)).astype(f32)

    def one(h, carry):
        for i, ref in enumerate((key_ref, value_ref)):
            for j in range(2):
                rows[2 * i + j, 8:, :] = ref[h, :, j * dim : (j + 1) * dim].astype(f32)
        for n in range(blocks):
            brow[n : n + 1, :] = pick_row(rate_ref[:, n * BLOCK : (n + 1) * BLOCK], h)
        rates = jnp.dot(
            brow[...], order, precision=lax.Precision.HIGHEST, preferred_element_type=f32
        )
        rates_ref[h] = rates
        for n in range(1, blocks):
            kv_ref[h, n - 1], kb_ref[h, n - 1], low_ref[h, n - 1], diag_ref[h, n - 1] = block_inputs(
                [rows.at[0], rows.at[1]], [rows.at[2], rows.at[3]],
                ck_ref[h], cv_ref[h], n * HALF, rates[n : n + 1],
            )
        return carry

    lax.fori_loop(0, key_ref.shape[0], one, 0)


def own_halo(index_ref, halo):
    return jnp.where(index_ref[0] == 0, 0.0, halo.astype(f32))


def maps_kernel(
    kept, start, half, index_ref, key_ref, value_ref, halo_ref, ck_ref, cv_ref,
    kv_ref, kb_ref, low_ref, diag_ref, rates_ref,
    kb0_ref, w_ref, u_ref, p_ref, s_ref, total_ref,
    rows, kv0, low0, dref, cref, xref, move, written,
):
    count, blocks = w_ref.shape[:2]
    dim = rows.shape[2]
    slots = range(count)
    first = first_head(index_ref, kept, half) + start
    row, col, lane = block_masks()
    eye = (row == col).astype(f32)

    for h in slots:
        head = first + h
        halo = own_halo(index_ref, halo_ref[head])
        for i, ref in enumerate((key_ref, value_ref)):
            for j in range(2):
                at = (1 + 2 * i + j) * dim
                fill_rows(
                    rows.at[2 * i + j],
                    halo[:, at : at + dim],
                    ref[head, :HALF, j * dim : (j + 1) * dim],
                )
        kv0[h], kb0_ref[h], low0[h], diag = block_inputs(
            [rows.at[0], rows.at[1]], [rows.at[2], rows.at[3]],
            ck_ref[head], cv_ref[head], 0, rates_ref[head][0:1],
        )
        cref[h, 0:GROUP, :] = diag
        for n in range(1, blocks):
            cref[h, n * GROUP : (n + 1) * GROUP, :] = diag_ref[head, n - 1]

    def keys_values(h, n):
        return kv0[h] if n == 0 else kv_ref[first + h, n - 1]

    def key_columns(h, n):
        return kb0_ref[h] if n == 0 else kb_ref[first + h, n - 1]

    def lower_rows(h, n, a, size):
        return low0[h, a : a + size] if n == 0 else low_ref[first + h, n - 1, a : a + size]

    lane8 = lax.broadcasted_iota(jnp.int32, (blocks, BLOCK), 1)
    times = [t // 2 + 8 * (t % 2) for t in range(GROUP)]
    for h in slots:
        coef = [cref[h, pl.ds(r, blocks, stride=GROUP), :] for r in range(GROUP)]
        sol = [(lane8 % GROUP == r).astype(f32) for r in range(GROUP)]
        for i, s in enumerate(times):
            pick = (lane8 // GROUP) * GROUP + s
            for r in times[i + 1 :]:
                sol[r] = sol[r] - jnp.take_along_axis(coef[r], pick, axis=1) * sol[s]
        for r in range(GROUP):
            xref[h, pl.ds(r, blocks, stride=GROUP), :] = sol[r]
    for h in slots:
        for n in range(blocks):
            base = xref[h, n * GROUP : (n + 1) * GROUP, :]
            dref[h, n] = split(
                jnp.concatenate(
                    [jnp.where(lane // GROUP == g, base, 0.0) for g in range(BLOCK // GROUP)], 0
                )
            )

    lane_h = lax.broadcasted_iota(jnp.int32, (HALF, BLOCK), 1)
    row_h = lax.broadcasted_iota(jnp.int32, (HALF, BLOCK), 0)
    size = GROUP
    while size < BLOCK:
        keep = lane_h // size == 2 * (row_h // size)
        starts = range(size, BLOCK, 2 * size)
        for h in slots:
            for n in range(blocks):
                inv = dref[h, n]
                low = jnp.concatenate([lower_rows(h, n, a, size) for a in starts], 0)
                z = split(mm(split(jnp.where(keep, low, 0.0)), inv))
                twice = []
                for i in range(len(starts)):
                    twice += [z[i * size : (i + 1) * size]] * 2
                odd = jnp.concatenate([inv[a : a + size] for a in starts], 0)
                new = mm(odd, jnp.concatenate(twice, 0))
                new = split(odd[:, :BLOCK].astype(f32) + odd[:, BLOCK:].astype(f32) - new)
                for i, a in enumerate(starts):
                    dref[h, n, a : a + size] = new[i * size : (i + 1) * size]
        size *= 2

    for h in slots:
        for n in range(blocks):
            inv = dref[h, n]
            both = keys_values(h, n)
            w_ref[h, n] = split(mm(inv, both[:, : 2 * dim]))
            u_ref[h, n] = split(mm(inv, both[:, 2 * dim :]))
    for h in slots:
        for n in range(blocks):
            kbs = key_columns(h, n)
            move[h, n] = split(eye - mm(kbs, w_ref[h, n]))
            written[h, n] = mm(kbs, u_ref[h, n])
    before_map = {h: split(eye) for h in slots}
    before_state = {h: jnp.zeros((dim, 2 * dim), bf16) for h in slots}
    for n in range(blocks):
        for h in slots:
            p_ref[h, n] = before_map[h]
            s_ref[h, n] = before_state[h]
            map_now = mm(move[h, n], before_map[h])
            state = mm(move[h, n], before_state[h]) + written[h, n]
            before_map[h] = split(map_now)
            before_state[h] = split(state)
            if n == blocks - 1:
                total_ref[h, :, :dim] = map_now
                total_ref[h, :, dim:] = state


def reads_kernel(
    kept, slot, at, half, index_ref, query_ref, halo_ref, cq_ref, kb_ref, kb0_ref, w_ref, u_ref, p_ref, s_ref,
    pulled_ref, local_ref, q0, query, scores, pulled,
):
    head = first_head(index_ref, kept, half) + at
    dim = q0.shape[1]
    blocks = w_ref.shape[1]
    fill_rows(q0, own_halo(index_ref, halo_ref[head])[:, :dim], query_ref[head])
    cq = cq_ref[head]
    row = lax.broadcasted_iota(jnp.int32, (HALF, BLOCK), 0)
    col = lax.broadcasted_iota(jnp.int32, (HALF, BLOCK), 1)
    causal = step_time(col) <= 2 * row + 1
    rows = [slice(n * HALF, (n + 1) * HALF) for n in range(blocks)]
    for n in range(blocks):
        q = conv_taps(q0, cq, n * HALF, HALF)
        query[rows[n]] = q
        kbs = kb0_ref[slot] if n == 0 else kb_ref[head, n - 1]
        scores[rows[n]] = split(jnp.where(causal, mm(split(q), kbs), 0.0))
    for n in range(blocks):
        pulled[rows[n]] = split(query[rows[n]] - mm(scores[rows[n]], w_ref[slot, n]))
        local_ref[rows[n]] = mm(scores[rows[n]], u_ref[slot, n])
    for n in range(blocks):
        local_ref[rows[n]] += mm(pulled[rows[n]], s_ref[slot, n])
        pulled_ref[rows[n]] = split(mm(pulled[rows[n]], p_ref[slot, n]))


def out_kernel(slot, half, index_ref, mine_ref, other_ref, gain_ref, *rest):
    out_ref = rest[-1]
    for i in range(2):

        @pl.when(pl.program_id(0) == i)
        def _():
            h = first_head(index_ref, i == 0, half) + slot
            state = mine_ref[0] if i == 0 else other_ref[0]
            raw = mm(rest[2 * i][...], split(state)) + rest[2 * i + 1][...]
            mean = jnp.mean(raw * raw, 1, keepdims=True)
            out_ref[0] = raw * lax.rsqrt(mean + 1e-06) * pick_row(gain_ref[...], h)


def then(later, earlier):
    dim = later.shape[0]
    prod = mm(split(later[:, :dim]), split(earlier))
    wide = prod.shape[1]
    if wide == dim:
        return prod + later[:, dim:]
    return jnp.concatenate([prod[:, :dim], prod[:, dim:] + later[:, dim:]], 1)


def pair_kernel(slot, index_ref, mine_ref, got_ref, total_ref, earlier_ref):
    upper = (index_ref[0] & 1) != 0
    for h in range(mine_ref.shape[0]):
        mine = mine_ref[h]
        got = got_ref[slot + h]
        earlier = jnp.where(upper, got, mine)
        earlier_ref[h] = earlier
        total_ref[h] = then(jnp.where(upper, mine, got), earlier)


def join_kernel(bit, index_ref, mine_ref, got_ref, *rest):
    *before_ref, total_ref, after_ref = rest
    upper = (index_ref[0] & bit) != 0
    dim = mine_ref.shape[1]
    row = lax.broadcasted_iota(jnp.int32, (dim, 2 * dim), 0)
    col = lax.broadcasted_iota(jnp.int32, (dim, 2 * dim), 1)
    for h in range(mine_ref.shape[0]):
        mine = mine_ref[h]
        got = got_ref[h]
        earlier = jnp.where(upper, got, mine)
        if total_ref.shape[2] == dim:
            earlier = earlier[:, dim:]
        total_ref[h] = then(jnp.where(upper, mine, got), earlier)
        if before_ref:
            before = before_ref[0][h]
            after_ref[h] = jnp.where(upper, then(before, got), before)
        else:
            after_ref[h] = jnp.where(upper, got, (row == col).astype(f32))


def down_kernel(bit, index_ref, before_ref, got_ref, earlier_ref, mine_ref, other_ref):
    upper = (index_ref[0] & 1) != 0
    for h in range(before_ref.shape[0]):
        got = jnp.where((index_ref[0] & bit) != 0, got_ref[h], 0.0)
        state = then(before_ref[h], got)
        after = then(earlier_ref[h], state)
        mine_ref[h] = jnp.where(upper, after, state)
        other_ref[h] = jnp.where(upper, state, after)


def tails_kernel(index_ref, query_ref, key_ref, value_ref, out_ref):
    rim = out_ref.shape[1]
    at = 0
    for ref in (query_ref, key_ref, value_ref):
        wide = ref.shape[2]
        out_ref[:, :, at : at + wide] = ref[:, ref.shape[1] - rim :, :]
        at += wide


def shape(dims, dtype):
    return jax.ShapeDtypeStruct(dims, dtype)


def resident(kernel, index, args, outs, scratch=(), limit=4 << 20):
    smem = pl.BlockSpec(memory_space=pltpu.SMEM)
    vmem = pl.BlockSpec(memory_space=pltpu.VMEM)
    return pl.pallas_call(
        kernel,
        in_specs=[smem] + [vmem] * len(args),
        out_specs=[vmem] * len(outs),
        out_shape=[pltpu.VMEM(o.shape, o.dtype) for o in outs],
        scratch_shapes=list(scratch),
        compiler_params=pltpu.CompilerParams(vmem_limit_bytes=limit),
    )(index, *[pltpu.with_memory_space_constraint(a, pltpu.VMEM) for a in args])


def swap(x, bit, count):
    return lax.ppermute(x, "seq", [(i, i ^ bit) for i in range(count)])


def per_device(
    queries, key_pairs, value_pairs, write_rates, conv_query, conv_key, conv_value, out_gain
):
    heads, tokens, dim = queries.shape
    blocks = tokens // HALF
    half = heads // 2
    rim = conv_query.shape[1] - 1
    count = lax.axis_size("seq")
    index = lax.axis_index("seq").reshape(1)

    parts = (queries, key_pairs, value_pairs)
    last = [
        pl.BlockSpec((heads, 16, x.shape[2]), lambda i, index_ref: (0, tokens // 16 - 1, 0))
        for x in parts
    ]
    tails = pl.pallas_call(
        tails_kernel,
        grid_spec=pltpu.PrefetchScalarGridSpec(
            num_scalar_prefetch=1,
            grid=(1,),
            in_specs=last,
            out_specs=pl.BlockSpec((heads, rim, 5 * dim), lambda i, index_ref: (0, 0, 0)),
        ),
        out_shape=shape((heads, rim, 5 * dim), bf16),
        compiler_params=pltpu.CompilerParams(vmem_limit_bytes=4 << 20),
    )(index, *[pltpu.with_memory_space_constraint(x, pltpu.HBM) for x in parts])
    halo = lax.ppermute(tails, "seq", [(i, (i + 1) % count) for i in range(count)])

    def in_order(*after):
        return lax.optimization_barrier((index, after))[0]

    inner = (heads, blocks - 1, BLOCK)
    front = resident(
        front_kernel,
        in_order(tails),
        (key_pairs, value_pairs, write_rates, conv_key, conv_value),
        [
            shape(inner + (4 * dim,), bf16),
            shape(inner + (2 * dim,), bf16),
            shape(inner + (BLOCK,), f32),
            shape((heads, blocks - 1, GROUP, BLOCK), f32),
            shape((heads, blocks, BLOCK), f32),
        ],
        [pltpu.VMEM((4, tokens + 8, dim), f32), pltpu.VMEM((blocks, BLOCK), f32)],
        LIMIT,
    )
    halo = lax.optimization_barrier((halo, front[-1]))[0]

    def maps(kept, start, size, *after):
        wide = shape((size, blocks, BLOCK, 2 * dim), bf16)
        return resident(
            functools.partial(maps_kernel, kept, start, half),
            in_order(*after),
            (key_pairs, value_pairs, halo, conv_key, conv_value, *front),
            [shape((size, BLOCK, 2 * dim), bf16)] + [wide] * 4 + [shape((size, dim, 2 * dim), f32)],
            [
                pltpu.VMEM((4, HALF + 8, dim), f32),
                pltpu.VMEM((size, BLOCK, 4 * dim), bf16),
                pltpu.VMEM((size, BLOCK, BLOCK), f32),
                pltpu.VMEM((size, blocks, BLOCK, 2 * BLOCK), bf16),
                pltpu.VMEM((size, blocks * GROUP, BLOCK), f32),
                pltpu.VMEM((size, blocks * GROUP, BLOCK), f32),
                pltpu.VMEM((size, blocks, dim, 2 * dim), bf16),
                pltpu.VMEM((size, blocks, dim, dim), f32),
            ],
            LIMIT,
        )

    def reads(kept, at, *after):
        slot, saved = (0, kept_saved[at]) if kept else (at, sent_saved)
        return resident(
            functools.partial(reads_kernel, kept, slot, at, half),
            in_order(*after),
            (queries, halo, conv_query, front[1], *saved),
            [shape((tokens, 2 * dim), bf16), shape((tokens, dim), f32)],
            [
                pltpu.VMEM((tokens + 8, dim), f32),
                pltpu.VMEM((tokens, dim), f32),
                pltpu.VMEM((tokens, 2 * dim), bf16),
                pltpu.VMEM((tokens, 2 * dim), bf16),
            ],
            LIMIT,
        )

    total_shape = shape((1, dim, 2 * dim), f32)
    state_shape = shape((1, dim, dim), f32)
    bits = []
    while 2 << len(bits) < count:
        bits.append(2 << len(bits))
    chains = {}

    def begin(at, got):
        total, earlier = resident(
            functools.partial(pair_kernel, at), index, (kept_total[at], got), [total_shape] * 2
        )
        chains[at] = dict(current=total, earlier=earlier, before=None, left=list(bits))
        send(at)
        return total

    def send(at):
        chain = chains[at]
        chain["got"] = swap(chain["current"], chain["left"][0], count)

    def join(at, *after):
        chain = chains[at]
        bit = chain["left"].pop(0)
        got = lax.optimization_barrier((chain["got"], after))[0]
        before = () if chain["before"] is None else (chain["before"],)
        last = len(chain["left"]) == 1
        chain["current"], chain["before"] = resident(
            functools.partial(join_kernel, bit),
            index,
            (chain["current"], got) + before,
            [state_shape if last else total_shape, total_shape],
        )
        send(at)
        return chain["current"]

    def down(at, *after):
        chain = chains[at]
        got = lax.optimization_barrier((chain["got"], after))[0]
        mine, other = resident(
            functools.partial(down_kernel, bits[-1]), index, (chain["before"], got, chain["earlier"]), [state_shape] * 2
        )
        return mine, swap(other, 1, count)

    out_shape = shape((heads, tokens, dim), f32)

    def finish(at, mine, other, done, *after):
        vmem = pl.BlockSpec(memory_space=pltpu.VMEM)

        def out_block(i, index_ref):
            upper = index_ref[0] & 1
            return (jnp.where(i == 0, upper, 1 - upper) * half + at, 0, 0)

        args = [mine, other, out_gain, *read[True, at], *read[False, at]]
        args = [pltpu.with_memory_space_constraint(a, pltpu.VMEM) for a in args]
        return pl.pallas_call(
            functools.partial(out_kernel, at, half),
            grid_spec=pltpu.PrefetchScalarGridSpec(
                num_scalar_prefetch=1,
                grid=(2,),
                in_specs=[vmem] * len(args) + [pl.BlockSpec(memory_space=pl.ANY)] * len(done),
                out_specs=pl.BlockSpec((1, tokens, dim), out_block),
            ),
            out_shape=out_shape,
            input_output_aliases={len(args) + 1: 0} if done else {},
            compiler_params=pltpu.CompilerParams(vmem_limit_bytes=LIMIT),
        )(in_order(*after), *args, *done)

    kept_saved, kept_total, read = {}, {}, {}

    def keep(at, *after):
        *kept_saved[at], kept_total[at] = maps(True, at, 1, *after)

    *sent_saved, sent_total = maps(False, 0, half)
    got = swap(sent_total, 1, count)
    keep(0, sent_total)
    step = begin(0, got)
    for at in range(1, half):
        keep(at, step)
        for other in range(at):
            if len(chains[other]["left"]) > 1:
                step = join(other, kept_total[at])
        step = begin(at, got)
    todo = [(kept, at) for at in range(half) for kept in (False, True)]

    def read_one(after):
        if todo:
            kept, at = todo.pop(0)
            read[kept, at] = reads(kept, at, after)
            return read[kept, at][1]
        return after

    step = read_one(read_one(step))
    while any(len(chain["left"]) > 1 for chain in chains.values()):
        for at in range(half):
            if len(chains[at]["left"]) > 1:
                step = read_one(join(at, step))
    while todo:
        step = read_one(step)
    done = ()
    states = [down(0, step)]
    for at in range(half):
        out = finish(at, *states[at], done)
        if at + 1 < half:
            states.append(down(at + 1, out))
        done = (out,)
    return done[0]


def solution(mesh):
    return jax.shard_map(
        per_device,
        mesh=mesh,
        in_specs=(
            P(None, ("grp", "seq"), None),
            P(None, ("grp", "seq"), None),
            P(None, ("grp", "seq"), None),
            P(None, ("grp", "seq")),
            P(),
            P(),
            P(),
            P(),
        ),
        out_specs=P(None, ("grp", "seq"), None),
        check_vma=False,
    )
```

```python
import functools

import jax
import jax.numpy as jnp
from jax import lax
from jax.experimental import pallas as pl
from jax.experimental.pallas import tpu as pltpu
from jax.sharding import PartitionSpec as P

BLOCK = 128
GROUP = 16
HALF = BLOCK // 2
LIMIT = 20 << 20

f32 = jnp.float32
bf16 = jnp.bfloat16


def split(x):
    high = x.astype(bf16)
    low = (x - high.astype(f32)).astype(bf16)
    return jnp.concatenate([high, low], 1)


def mm(a, b):
    n = b.shape[1] // 2
    p = jnp.dot(a, jnp.concatenate([b, b], 0), preferred_element_type=f32)
    return p[:, :n] + p[:, n:]


def pick_row(x, r):
    row = lax.broadcasted_iota(jnp.int32, x.shape, 0)
    return jnp.sum(jnp.where(row == r, x, 0.0), 0, keepdims=True)


def silu(x):
    return x / (1.0 + jnp.exp(-x))


def step_time(r):
    return (r // GROUP) * GROUP + 2 * (r % 8) + (r // 8) % 2


def interleave(a, b):
    parts = []
    for g in range(0, a.shape[0], 8):
        parts += [a[g : g + 8], b[g : g + 8]]
    return jnp.concatenate(parts, 0)


def conv_taps(ref, weights, start, count):
    taps = weights.shape[0]
    total = weights[0:1] * ref[pl.ds(start + 9 - taps, count), :]
    for s in range(1, taps):
        total = total + weights[s : s + 1] * ref[pl.ds(start + 9 - taps + s, count), :]
    return silu(total)


def fill_rows(ref, halo, rows):
    rim = halo.shape[0]
    ref[8 - rim : 8, :] = halo.astype(f32)
    ref[8:, :] = rows.astype(f32)


def first_head(index_ref, kept, half):
    upper = index_ref[0] & 1
    return (upper if kept else 1 - upper) * half


def block_masks():
    row = lax.broadcasted_iota(jnp.int32, (BLOCK, BLOCK), 0)
    col = lax.broadcasted_iota(jnp.int32, (BLOCK, BLOCK), 1)
    lane = lax.broadcasted_iota(jnp.int32, (GROUP, BLOCK), 1)
    return row, col, lane


def block_inputs(key_rows, value_rows, ck, cv, t0, rates):
    row, col, lane = block_masks()
    dim = key_rows[0].shape[1]
    ka, kb = [conv_taps(r, ck[:, j * dim : (j + 1) * dim], t0, HALF) for j, r in enumerate(key_rows)]
    keys = interleave(ka, kb)
    keys = keys * lax.rsqrt(jnp.sum(keys * keys, 1, keepdims=True) + 1e-06)
    va, vb = [conv_taps(r, cv[:, j * dim : (j + 1) * dim], t0, HALF) for j, r in enumerate(value_rows)]
    ks = split(keys)
    kv = jnp.concatenate([ks, split(interleave(va, vb))], 1)
    kbs = split(keys.T * rates)
    lower = jnp.where(step_time(col) < step_time(row), mm(ks, kbs), 0.0)
    diag = jnp.zeros((GROUP, BLOCK), f32)
    for g in range(BLOCK // GROUP):
        diag = jnp.where(lane // GROUP == g, lower[g * GROUP : (g + 1) * GROUP], diag)
    return kv, kbs, lower, diag


def invert_groups(diag, out, blocks):
    lane = lax.broadcasted_iota(jnp.int32, (blocks, BLOCK), 1)
    times = [t // 2 + 8 * (t % 2) for t in range(GROUP)]
    coef = [diag[pl.ds(r, blocks, stride=GROUP), :] for r in range(GROUP)]
    sol = [(lane % GROUP == r).astype(f32) for r in range(GROUP)]
    for i, s in enumerate(times):
        pick = (lane // GROUP) * GROUP + s
        for r in times[i + 1 :]:
            sol[r] = sol[r] - jnp.take_along_axis(coef[r], pick, axis=1) * sol[s]
    for r in range(GROUP):
        out[pl.ds(r, blocks, stride=GROUP), :] = sol[r]


def front_kernel(
    index_ref, key_ref, value_ref, rate_ref, ck_ref, cv_ref,
    kv_ref, kb_ref, low_ref, sol_ref, rates_ref, rows, brow, diag,
):
    dim = rows.shape[2]
    blocks = rates_ref.shape[1]
    row, col, _ = block_masks()
    order = (row == step_time(col)).astype(f32)

    def one(h, carry):
        for i, ref in enumerate((key_ref, value_ref)):
            for j in range(2):
                rows[2 * i + j, 8:, :] = ref[h, :, j * dim : (j + 1) * dim].astype(f32)
        for n in range(blocks):
            brow[n : n + 1, :] = pick_row(rate_ref[:, n * BLOCK : (n + 1) * BLOCK], h)
        rates = jnp.dot(
            brow[...], order, precision=lax.Precision.HIGHEST, preferred_element_type=f32
        )
        rates_ref[h] = rates
        for n in range(1, blocks):
            kv_ref[h, n - 1], kb_ref[h, n - 1], low_ref[h, n - 1], groups = block_inputs(
                [rows.at[0], rows.at[1]], [rows.at[2], rows.at[3]],
                ck_ref[h], cv_ref[h], n * HALF, rates[n : n + 1],
            )
            diag[h, n * GROUP : (n + 1) * GROUP] = groups
        diag[h, 0:GROUP] = jnp.zeros((GROUP, BLOCK), f32)
        return carry

    lax.fori_loop(0, key_ref.shape[0], one, 0)
    for h in range(key_ref.shape[0]):
        invert_groups(diag.at[h], sol_ref.at[h], blocks)


def first_kernel(
    index_ref, key_ref, value_ref, halo_ref, ck_ref, cv_ref, rates_ref,
    kv_ref, kb_ref, low_ref, sol_ref, rows, diag,
):
    heads = key_ref.shape[0]
    dim = rows.shape[3]
    for h in range(heads):
        halo = own_halo(index_ref, halo_ref[h])
        for i, ref in enumerate((key_ref, value_ref)):
            for j in range(2):
                at = (1 + 2 * i + j) * dim
                fill_rows(
                    rows.at[h, 2 * i + j],
                    halo[:, at : at + dim],
                    ref[h, :HALF, j * dim : (j + 1) * dim],
                )
    for h in range(heads):
        kv_ref[h], kb_ref[h], low_ref[h], groups = block_inputs(
            [rows.at[h, 0], rows.at[h, 1]], [rows.at[h, 2], rows.at[h, 3]],
            ck_ref[h], cv_ref[h], 0, rates_ref[h][0:1],
        )
        diag[h * GROUP : (h + 1) * GROUP] = groups
    invert_groups(diag, sol_ref, heads)


def own_halo(index_ref, halo):
    return jnp.where(index_ref[0] == 0, 0.0, halo.astype(f32))


def maps_kernel(
    kept, start, half, index_ref, kv_ref, kb_ref, low_ref, sol_ref,
    kv0_ref, kb0_ref, low0_ref, sol0_ref,
    w_ref, u_ref, p_ref, s_ref, total_ref,
    dref, move, written,
):
    count, blocks = w_ref.shape[:2]
    dim = total_ref.shape[1]
    slots = range(count)
    first = first_head(index_ref, kept, half) + start
    row, col, lane = block_masks()
    eye = (row == col).astype(f32)

    def at(inner, first_one, h, n):
        return first_one[first + h] if n == 0 else inner[first + h, n - 1]

    for h in slots:
        for n in range(blocks):
            if n == 0:
                base = sol0_ref[pl.ds((first + h) * GROUP, GROUP), :]
            else:
                base = sol_ref[first + h, n * GROUP : (n + 1) * GROUP, :]
            dref[h, n] = split(
                jnp.concatenate(
                    [jnp.where(lane // GROUP == g, base, 0.0) for g in range(BLOCK // GROUP)], 0
                )
            )

    lane_h = lax.broadcasted_iota(jnp.int32, (HALF, BLOCK), 1)
    row_h = lax.broadcasted_iota(jnp.int32, (HALF, BLOCK), 0)
    size = GROUP
    while size < BLOCK:
        keep = lane_h // size == 2 * (row_h // size)
        starts = range(size, BLOCK, 2 * size)
        for h in slots:
            for n in range(blocks):
                inv = dref[h, n]
                lower = at(low_ref, low0_ref, h, n)
                low = jnp.concatenate([lower[a : a + size] for a in starts], 0)
                z = split(mm(split(jnp.where(keep, low, 0.0)), inv))
                twice = []
                for i in range(len(starts)):
                    twice += [z[i * size : (i + 1) * size]] * 2
                odd = jnp.concatenate([inv[a : a + size] for a in starts], 0)
                new = mm(odd, jnp.concatenate(twice, 0))
                new = split(odd[:, :BLOCK].astype(f32) + odd[:, BLOCK:].astype(f32) - new)
                for i, a in enumerate(starts):
                    dref[h, n, a : a + size] = new[i * size : (i + 1) * size]
        size *= 2

    for h in slots:
        for n in range(blocks):
            inv = dref[h, n]
            both = at(kv_ref, kv0_ref, h, n)
            w_ref[h, n] = split(mm(inv, both[:, : 2 * dim]))
            u_ref[h, n] = split(mm(inv, both[:, 2 * dim :]))
    for h in slots:
        for n in range(blocks):
            kbs = at(kb_ref, kb0_ref, h, n)
            move[h, n] = split(eye - mm(kbs, w_ref[h, n]))
            written[h, n] = mm(kbs, u_ref[h, n])

    span = {(h, n, n + 1): (move[h, n], split(written[h, n])) for h in slots for n in range(blocks)}

    def run(h, i, mid, j):
        later, earlier = span[h, mid, j], span[h, i, mid]
        state = later[1]
        added = state[:, :dim].astype(f32) + state[:, dim:].astype(f32)
        full = (mm(later[0], earlier[0]), mm(later[0], earlier[1]) + added)
        if (i, j) == (0, blocks):
            total_ref[h, :, :dim], total_ref[h, :, dim:] = full
        span[h, i, j] = tuple(split(x) for x in full)

    size = 2
    while size <= blocks:
        for h in slots:
            for i in range(0, blocks, size):
                run(h, i, i + size // 2, i + size)
        for j in range(size // 2 + 1, size):
            low_bit = j & -j
            if low_bit < size // 2:
                for h in slots:
                    run(h, 0, j - low_bit, j)
        size *= 2
    for h in slots:
        p_ref[h, 0] = split(eye)
        s_ref[h, 0] = jnp.zeros((dim, 2 * dim), bf16)
        for n in range(1, blocks):
            p_ref[h, n], s_ref[h, n] = span[h, 0, n]


def reads_kernel(
    kept, slot, at, half, index_ref, query_ref, halo_ref, cq_ref, kb_ref, kb0_ref, w_ref, u_ref, p_ref, s_ref,
    pulled_ref, local_ref, q0, query, scores, pulled,
):
    head = first_head(index_ref, kept, half) + at
    dim = q0.shape[1]
    blocks = w_ref.shape[1]
    fill_rows(q0, own_halo(index_ref, halo_ref[head])[:, :dim], query_ref[head])
    cq = cq_ref[head]
    row = lax.broadcasted_iota(jnp.int32, (HALF, BLOCK), 0)
    col = lax.broadcasted_iota(jnp.int32, (HALF, BLOCK), 1)
    causal = step_time(col) <= 2 * row + 1
    rows = [slice(n * HALF, (n + 1) * HALF) for n in range(blocks)]
    for n in range(blocks):
        q = conv_taps(q0, cq, n * HALF, HALF)
        query[rows[n]] = q
        kbs = kb0_ref[head] if n == 0 else kb_ref[head, n - 1]
        scores[rows[n]] = split(jnp.where(causal, mm(split(q), kbs), 0.0))
    for n in range(blocks):
        pulled[rows[n]] = split(query[rows[n]] - mm(scores[rows[n]], w_ref[slot, n]))
        local_ref[rows[n]] = mm(scores[rows[n]], u_ref[slot, n])
    for n in range(blocks):
        local_ref[rows[n]] += mm(pulled[rows[n]], s_ref[slot, n])
        pulled_ref[rows[n]] = split(mm(pulled[rows[n]], p_ref[slot, n]))


def out_kernel(kept, start, half, index_ref, gain_ref, *rest):
    out_ref = rest[-1]
    for i in range(len(rest) // 3):
        state_ref, pulled_ref, local_ref = rest[3 * i : 3 * i + 3]

        @pl.when(pl.program_id(0) == i)
        def _():
            h = first_head(index_ref, kept, half) + start + i
            raw = mm(pulled_ref[...], split(state_ref[0])) + local_ref[...]
            mean = jnp.mean(raw * raw, 1, keepdims=True)
            out_ref[0] = raw * lax.rsqrt(mean + 1e-06) * pick_row(gain_ref[...], h)


def then(later, earlier):
    dim = later.shape[0]
    prod = mm(split(later[:, :dim]), split(earlier))
    wide = prod.shape[1]
    if wide == dim:
        return prod + later[:, dim:]
    return jnp.concatenate([prod[:, :dim], prod[:, dim:] + later[:, dim:]], 1)


def pair_kernel(slot, index_ref, mine_ref, got_ref, total_ref, earlier_ref):
    upper = (index_ref[0] & 1) != 0
    for h in range(mine_ref.shape[0]):
        mine = mine_ref[h]
        got = got_ref[slot + h]
        earlier = jnp.where(upper, got, mine)
        earlier_ref[h] = earlier
        total_ref[h] = then(jnp.where(upper, mine, got), earlier)


def join_kernel(bits, index_ref, *refs):
    size = 1 << len(bits)
    got_refs, before_ref, (total_ref, after_ref) = refs[:size], refs[size:-2], refs[-2:]
    ups = [(index_ref[0] & bit) != 0 for bit in bits]
    dim = got_refs[0].shape[1]
    row = lax.broadcasted_iota(jnp.int32, (dim, 2 * dim), 0)
    col = lax.broadcasted_iota(jnp.int32, (dim, 2 * dim), 1)
    for h in range(got_refs[0].shape[0]):
        maps = [ref[h] for ref in got_refs]
        for i, up in enumerate(ups):
            maps = [jnp.where(up, maps[j ^ (1 << i)], maps[j]) for j in range(size)]
        part = slice(dim, None) if total_ref.shape[2] == dim else slice(None)
        identity = (row == col).astype(f32)
        if size == 2:
            total_ref[h] = then(maps[1], maps[0][:, part])
            prefix = jnp.where(ups[0], maps[0], identity)
        else:
            low = then(maps[1], maps[0])
            total_ref[h] = then(then(maps[3], maps[2]), low[:, part])
            prefix = jnp.where(
                ups[1],
                jnp.where(ups[0], then(maps[2], low), low),
                jnp.where(ups[0], maps[0], identity),
            )
        after_ref[h] = then(before_ref[0][h], prefix) if before_ref else prefix


def down_kernel(bit, index_ref, before_ref, got_ref, earlier_ref, mine_ref, other_ref):
    upper = (index_ref[0] & 1) != 0
    got = jnp.where((index_ref[0] & bit) != 0, got_ref[0], 0.0)
    state = then(before_ref[0], got)
    after = then(earlier_ref[0], state)
    mine_ref[0] = jnp.where(upper, after, state)
    other_ref[0] = jnp.where(upper, state, after)


def tails_kernel(index_ref, query_ref, key_ref, value_ref, out_ref):
    rim = out_ref.shape[1]
    at = 0
    for ref in (query_ref, key_ref, value_ref):
        wide = ref.shape[2]
        out_ref[:, :, at : at + wide] = ref[:, ref.shape[1] - rim :, :]
        at += wide


def shape(dims, dtype):
    return jax.ShapeDtypeStruct(dims, dtype)


def resident(kernel, index, args, outs, scratch=(), limit=4 << 20):
    smem = pl.BlockSpec(memory_space=pltpu.SMEM)
    vmem = pl.BlockSpec(memory_space=pltpu.VMEM)
    return pl.pallas_call(
        kernel,
        in_specs=[smem] + [vmem] * len(args),
        out_specs=[vmem] * len(outs),
        out_shape=[pltpu.VMEM(o.shape, o.dtype) for o in outs],
        scratch_shapes=list(scratch),
        compiler_params=pltpu.CompilerParams(vmem_limit_bytes=limit),
    )(index, *[pltpu.with_memory_space_constraint(a, pltpu.VMEM) for a in args])


def swap(x, bit, count):
    return lax.ppermute(x, "seq", [(i, i ^ bit) for i in range(count)])


def per_device(
    queries, key_pairs, value_pairs, write_rates, conv_query, conv_key, conv_value, out_gain
):
    heads, tokens, dim = queries.shape
    blocks = tokens // HALF
    half = heads // 2
    rim = conv_query.shape[1] - 1
    count = lax.axis_size("seq")
    index = lax.axis_index("seq").reshape(1)

    parts = (queries, key_pairs, value_pairs)
    last = [
        pl.BlockSpec((heads, 16, x.shape[2]), lambda i, index_ref: (0, tokens // 16 - 1, 0))
        for x in parts
    ]
    tails = pl.pallas_call(
        tails_kernel,
        grid_spec=pltpu.PrefetchScalarGridSpec(
            num_scalar_prefetch=1,
            grid=(1,),
            in_specs=last,
            out_specs=pl.BlockSpec((heads, rim, 5 * dim), lambda i, index_ref: (0, 0, 0)),
        ),
        out_shape=shape((heads, rim, 5 * dim), bf16),
        compiler_params=pltpu.CompilerParams(vmem_limit_bytes=4 << 20),
    )(index, *[pltpu.with_memory_space_constraint(x, pltpu.HBM) for x in parts])
    halo = lax.ppermute(tails, "seq", [(i, (i + 1) % count) for i in range(count)])

    def in_order(*after):
        return lax.optimization_barrier((index, after))[0]

    inner = (heads, blocks - 1, BLOCK)
    front = resident(
        front_kernel,
        in_order(tails),
        (key_pairs, value_pairs, write_rates, conv_key, conv_value),
        [
            shape(inner + (4 * dim,), bf16),
            shape(inner + (2 * dim,), bf16),
            shape(inner + (BLOCK,), f32),
            shape((heads, blocks * GROUP, BLOCK), f32),
            shape((heads, blocks, BLOCK), f32),
        ],
        [
            pltpu.VMEM((4, tokens + 8, dim), f32),
            pltpu.VMEM((blocks, BLOCK), f32),
            pltpu.VMEM((heads, blocks * GROUP, BLOCK), f32),
        ],
        LIMIT,
    )
    *front, rates = front
    halo = lax.optimization_barrier((halo, rates))[0]
    opening = resident(
        first_kernel,
        in_order(rates),
        (key_pairs, value_pairs, halo, conv_key, conv_value, rates),
        [
            shape((heads, BLOCK, 4 * dim), bf16),
            shape((heads, BLOCK, 2 * dim), bf16),
            shape((heads, BLOCK, BLOCK), f32),
            shape((heads * GROUP, BLOCK), f32),
        ],
        [pltpu.VMEM((heads, 4, HALF + 8, dim), f32), pltpu.VMEM((heads * GROUP, BLOCK), f32)],
        LIMIT,
    )

    def maps(kept, start, size, *after):
        wide = shape((size, blocks, BLOCK, 2 * dim), bf16)
        return resident(
            functools.partial(maps_kernel, kept, start, half),
            in_order(*after),
            (*front, *opening),
            [wide] * 4 + [shape((size, dim, 2 * dim), f32)],
            [
                pltpu.VMEM((size, blocks, BLOCK, 2 * BLOCK), bf16),
                pltpu.VMEM((size, blocks, dim, 2 * dim), bf16),
                pltpu.VMEM((size, blocks, dim, dim), f32),
            ],
            LIMIT,
        )

    def reads(kept, at, *after):
        slot, saved = (0, kept_saved[at]) if kept else (at, sent_saved)
        return resident(
            functools.partial(reads_kernel, kept, slot, at, half),
            in_order(*after),
            (queries, halo, conv_query, front[1], opening[1], *saved),
            [shape((tokens, 2 * dim), bf16), shape((tokens, dim), f32)],
            [
                pltpu.VMEM((tokens + 8, dim), f32),
                pltpu.VMEM((tokens, dim), f32),
                pltpu.VMEM((tokens, 2 * dim), bf16),
                pltpu.VMEM((tokens, 2 * dim), bf16),
            ],
            LIMIT,
        )

    total_shape = shape((1, dim, 2 * dim), f32)
    state_shape = shape((1, dim, dim), f32)
    bits = []
    while 2 << len(bits) < count:
        bits.append(2 << len(bits))
    chains = {}

    def begin(at, got, *after):
        total, earlier = resident(
            functools.partial(pair_kernel, at),
            in_order(*after),
            (kept_total[at], got),
            [total_shape] * 2,
        )
        chains[at] = dict(current=total, earlier=earlier, before=(), left=[(bit,) for bit in bits[:-1]])
        send(at)
        return total

    def send(at):
        chain = chains[at]
        now = chain["left"][0] if chain["left"] else bits[-1:]
        flips = [sum(b for i, b in enumerate(now) if j >> i & 1) for j in range(1 << len(now))]
        chain["got"] = [swap(chain["current"], flip, count) for flip in flips[1:]]

    def join(at, *after):
        chain = chains[at]
        now = chain["left"].pop(0)
        got = lax.optimization_barrier((chain["got"], after))[0]
        chain["current"], before = resident(
            functools.partial(join_kernel, now),
            index,
            (chain["current"], *got, *chain["before"]),
            [total_shape if chain["left"] else state_shape, total_shape],
        )
        chain["before"] = (before,)
        send(at)
        return chain["current"]

    def down(at, *after):
        chain = chains[at]
        got = lax.optimization_barrier((chain["got"], after))[0][0]
        return resident(
            functools.partial(down_kernel, bits[-1]),
            index,
            (*chain["before"], got, chain["earlier"]),
            [state_shape] * 2,
        )

    out_shape = shape((heads, tokens, dim), f32)
    done = ()

    def finish(kept, start, states, *after):
        nonlocal done
        vmem = pl.BlockSpec(memory_space=pltpu.VMEM)

        def out_block(i, index_ref):
            upper = index_ref[0] & 1
            return ((upper if kept else 1 - upper) * half + start + i, 0, 0)

        args = [out_gain]
        for i, state in enumerate(states):
            args += [state, *read[kept, start + i]]
        args = [pltpu.with_memory_space_constraint(a, pltpu.VMEM) for a in args]

        def kernel(index_ref, *refs):
            out_kernel(kept, start, half, index_ref, *refs[: len(args)], refs[-1])

        out = pl.pallas_call(
            kernel,
            grid_spec=pltpu.PrefetchScalarGridSpec(
                num_scalar_prefetch=1,
                grid=(len(states),),
                in_specs=[vmem] * len(args) + [pl.BlockSpec(memory_space=pl.ANY)] * len(done),
                out_specs=pl.BlockSpec((1, tokens, dim), out_block),
            ),
            out_shape=out_shape,
            input_output_aliases={len(args) + 1: 0} if done else {},
            compiler_params=pltpu.CompilerParams(vmem_limit_bytes=LIMIT),
        )(in_order(*after), *args, *done)
        done = (out,)
        return out

    kept_saved, kept_total, read = {}, {}, {}

    def keep(at, *after):
        *kept_saved[at], kept_total[at] = maps(True, at, 1, *after)

    *sent_saved, sent_total = maps(False, 0, half)
    got = swap(sent_total, 1, count)
    keep(0, sent_total)
    step = begin(0, got)
    for at in range(1, half):
        keep(at, step)
        step = begin(at, got, kept_total[at])
    step = (step,)
    todo = [(kept, at) for at in range(half) for kept in (False, True)]

    def read_some(pieces, *after):
        for _ in range(min(pieces, len(todo))):
            kept, at = todo.pop(0)
            read[kept, at] = reads(kept, at, *after)
            after = tuple(read[kept, at])
        return after

    while any(chain["left"] for chain in chains.values()):
        for at in range(half):
            if chains[at]["left"]:
                step = read_some(1, join(at, *step))
    step = read_some(len(todo), *step)
    mine, other = {}, {}
    for at in range(half):
        mine[at], other[at] = down(at, *(done or step))
        if at + 1 < half:
            finish(True, at, [mine[at]])
    others = swap(jnp.concatenate([other[at] for at in range(half)], 0), 1, count)
    last = finish(True, half - 1, [mine[half - 1]])
    others = lax.optimization_barrier((others, last))[0]
    return finish(False, 0, [others[at : at + 1] for at in range(half)])


def solution(mesh):
    return jax.shard_map(
        per_device,
        mesh=mesh,
        in_specs=(
            P(None, ("grp", "seq"), None),
            P(None, ("grp", "seq"), None),
            P(None, ("grp", "seq"), None),
            P(None, ("grp", "seq")),
            P(),
            P(),
            P(),
            P(),
        ),
        out_specs=P(None, ("grp", "seq"), None),
        check_vma=False,
    )
```

```python
import functools

import jax
import jax.numpy as jnp
from jax import lax
from jax.experimental import pallas as pl
from jax.experimental.pallas import tpu as pltpu
from jax.sharding import PartitionSpec as P

BLOCK = 128
GROUP = 16
HALF = BLOCK // 2
LIMIT = 20 << 20

f32 = jnp.float32
bf16 = jnp.bfloat16


def split(x):
    high = x.astype(bf16)
    low = (x - high.astype(f32)).astype(bf16)
    return jnp.concatenate([high, low], 1)


def mm(a, b):
    n = b.shape[1] // 2
    p = jnp.dot(a, jnp.concatenate([b, b], 0), preferred_element_type=f32)
    return p[:, :n] + p[:, n:]


def pick_row(x, r):
    row = lax.broadcasted_iota(jnp.int32, x.shape, 0)
    return jnp.sum(jnp.where(row == r, x, 0.0), 0, keepdims=True)


def silu(x):
    return x / (1.0 + jnp.exp(-x))


def step_time(r):
    return (r // GROUP) * GROUP + 2 * (r % 8) + (r // 8) % 2


def interleave(a, b):
    parts = []
    for g in range(0, a.shape[0], 8):
        parts += [a[g : g + 8], b[g : g + 8]]
    return jnp.concatenate(parts, 0)


def conv_taps(ref, weights, start, count):
    taps = weights.shape[0]
    total = weights[0:1] * ref[pl.ds(start + 9 - taps, count), :]
    for s in range(1, taps):
        total = total + weights[s : s + 1] * ref[pl.ds(start + 9 - taps + s, count), :]
    return silu(total)


def fill_rows(ref, halo, rows):
    rim = halo.shape[0]
    ref[8 - rim : 8, :] = halo.astype(f32)
    ref[8:, :] = rows.astype(f32)


def first_head(index_ref, kept, half):
    upper = index_ref[0] & 1
    return (upper if kept else 1 - upper) * half


def block_masks():
    row = lax.broadcasted_iota(jnp.int32, (BLOCK, BLOCK), 0)
    col = lax.broadcasted_iota(jnp.int32, (BLOCK, BLOCK), 1)
    lane = lax.broadcasted_iota(jnp.int32, (GROUP, BLOCK), 1)
    return row, col, lane


def block_inputs(units, keys):
    row, col, lane = block_masks()
    strict = step_time(col) < step_time(row)
    for i, (rows, ck, cv, t0, rates, kv, kb, low, diag) in enumerate(units):
        dim = rows[0].shape[1]
        taps = [w[:, j * dim : (j + 1) * dim] for w in (ck, cv) for j in range(2)]
        ka, kb_, va, vb = [conv_taps(r, w, t0, HALF) for r, w in zip(rows, taps)]
        k = interleave(ka, kb_)
        k = k * lax.rsqrt(jnp.sum(k * k, 1, keepdims=True) + 1e-06)
        keys[i] = k
        kv[:, : 2 * dim] = split(k)
        kv[:, 2 * dim :] = split(interleave(va, vb))
    for i, (rows, ck, cv, t0, rates, kv, kb, low, diag) in enumerate(units):
        kb[...] = split(keys[i].T * rates)
    for i, (rows, ck, cv, t0, rates, kv, kb, low, diag) in enumerate(units):
        lower = jnp.where(strict, mm(kv[:, : kb.shape[1]], kb[...]), 0.0)
        low[...] = lower
        groups = jnp.zeros((GROUP, BLOCK), f32)
        for g in range(BLOCK // GROUP):
            groups = jnp.where(lane // GROUP == g, lower[g * GROUP : (g + 1) * GROUP], groups)
        diag[...] = groups


def invert_groups(diag, out, blocks):
    lane = lax.broadcasted_iota(jnp.int32, (blocks, BLOCK), 1)
    times = [t // 2 + 8 * (t % 2) for t in range(GROUP)]
    coef = [diag[pl.ds(r, blocks, stride=GROUP), :] for r in range(GROUP)]
    sol = [(lane % GROUP == r).astype(f32) for r in range(GROUP)]
    for i, s in enumerate(times):
        pick = (lane // GROUP) * GROUP + s
        for r in times[i + 1 :]:
            sol[r] = sol[r] - jnp.take_along_axis(coef[r], pick, axis=1) * sol[s]
    for r in range(GROUP):
        out[pl.ds(r, blocks, stride=GROUP), :] = sol[r]


def front_kernel(
    index_ref, key_ref, value_ref, rate_ref, ck_ref, cv_ref,
    kv_ref, kb_ref, low_ref, sol_ref, rates_ref, rows, brow, diag, keys,
):
    dim = rows.shape[2]
    blocks = rates_ref.shape[1]
    row, col, _ = block_masks()
    order = (row == step_time(col)).astype(f32)

    def one(h, carry):
        for i, ref in enumerate((key_ref, value_ref)):
            for j in range(2):
                rows[2 * i + j, 8:, :] = ref[h, :, j * dim : (j + 1) * dim].astype(f32)
        for n in range(blocks):
            brow[n : n + 1, :] = pick_row(rate_ref[:, n * BLOCK : (n + 1) * BLOCK], h)
        rates = jnp.dot(
            brow[...], order, precision=lax.Precision.HIGHEST, preferred_element_type=f32
        )
        rates_ref[h] = rates
        ck, cv = ck_ref[h], cv_ref[h]
        block_inputs(
            [
                (
                    [rows.at[i] for i in range(4)], ck, cv, n * HALF, rates[n : n + 1],
                    kv_ref.at[h, n - 1], kb_ref.at[h, n - 1], low_ref.at[h, n - 1],
                    diag.at[h, n * GROUP : (n + 1) * GROUP],
                )
                for n in range(1, blocks)
            ],
            keys,
        )
        diag[h, 0:GROUP] = jnp.zeros((GROUP, BLOCK), f32)
        return carry

    lax.fori_loop(0, key_ref.shape[0], one, 0)
    for h in range(key_ref.shape[0]):
        invert_groups(diag.at[h], sol_ref.at[h], blocks)


def first_kernel(
    index_ref, key_ref, value_ref, halo_ref, ck_ref, cv_ref, rates_ref,
    kv_ref, kb_ref, low_ref, sol_ref, rows, diag, keys,
):
    heads = key_ref.shape[0]
    dim = rows.shape[3]
    for h in range(heads):
        halo = own_halo(index_ref, halo_ref[h])
        for i, ref in enumerate((key_ref, value_ref)):
            for j in range(2):
                at = (1 + 2 * i + j) * dim
                fill_rows(
                    rows.at[h, 2 * i + j],
                    halo[:, at : at + dim],
                    ref[h, :HALF, j * dim : (j + 1) * dim],
                )
    block_inputs(
        [
            (
                [rows.at[h, i] for i in range(4)], ck_ref[h], cv_ref[h], 0, rates_ref[h][0:1],
                kv_ref.at[h], kb_ref.at[h], low_ref.at[h], diag.at[h * GROUP : (h + 1) * GROUP],
            )
            for h in range(heads)
        ],
        keys,
    )
    invert_groups(diag, sol_ref, heads)


def own_halo(index_ref, halo):
    return jnp.where(index_ref[0] == 0, 0.0, halo.astype(f32))


def maps_kernel(
    kept, start, half, index_ref, kv_ref, kb_ref, low_ref, sol_ref,
    kv0_ref, kb0_ref, low0_ref, sol0_ref,
    inv_ref, p_ref, s_ref, total_ref, move, written,
):
    count, blocks = inv_ref.shape[:2]
    dim = total_ref.shape[1]
    slots = range(count)
    first = first_head(index_ref, kept, half) + start
    row, col, lane = block_masks()
    eye = (row == col).astype(f32)

    def at(inner, first_one, h, n):
        return first_one[first + h] if n == 0 else inner[first + h, n - 1]

    for h in slots:
        for n in range(blocks):
            if n == 0:
                base = sol0_ref[pl.ds((first + h) * GROUP, GROUP), :]
            else:
                base = sol_ref[first + h, n * GROUP : (n + 1) * GROUP, :]
            inv_ref[h, n] = split(
                jnp.concatenate(
                    [jnp.where(lane // GROUP == g, base, 0.0) for g in range(BLOCK // GROUP)], 0
                )
            )

    lane_h = lax.broadcasted_iota(jnp.int32, (HALF, BLOCK), 1)
    row_h = lax.broadcasted_iota(jnp.int32, (HALF, BLOCK), 0)
    size = GROUP
    while size < BLOCK:
        keep = lane_h // size == 2 * (row_h // size)
        starts = range(size, BLOCK, 2 * size)
        for h in slots:
            for n in range(blocks):
                inv = inv_ref[h, n]
                lower = at(low_ref, low0_ref, h, n)
                low = jnp.concatenate([lower[a : a + size] for a in starts], 0)
                z = split(mm(split(jnp.where(keep, low, 0.0)), inv))
                twice = []
                for i in range(len(starts)):
                    twice += [z[i * size : (i + 1) * size]] * 2
                odd = jnp.concatenate([inv[a : a + size] for a in starts], 0)
                new = mm(odd, jnp.concatenate(twice, 0))
                new = split(odd[:, :BLOCK].astype(f32) + odd[:, BLOCK:].astype(f32) - new)
                for i, a in enumerate(starts):
                    inv_ref[h, n, a : a + size] = new[i * size : (i + 1) * size]
        size *= 2

    for h in slots:
        for n in range(blocks):
            move[h, n] = split(mm(at(kb_ref, kb0_ref, h, n), inv_ref[h, n]))
    for h in slots:
        for n in range(blocks):
            both = at(kv_ref, kv0_ref, h, n)
            solved = move[h, n]
            written[h, n] = split(mm(solved, both[:, 2 * dim :]))
            move[h, n] = split(eye - mm(solved, both[:, : 2 * dim]))

    span = {(h, n, n + 1): (move[h, n], written[h, n]) for h in slots for n in range(blocks)}

    def run(h, i, mid, j):
        later, earlier = span[h, mid, j], span[h, i, mid]
        state = later[1]
        added = state[:, :dim].astype(f32) + state[:, dim:].astype(f32)
        full = (mm(later[0], earlier[0]), mm(later[0], earlier[1]) + added)
        if (i, j) == (0, blocks):
            total_ref[h, :, :dim], total_ref[h, :, dim:] = full
        span[h, i, j] = tuple(split(x) for x in full)

    size = 2
    while size <= blocks:
        for h in slots:
            for i in range(0, blocks, size):
                run(h, i, i + size // 2, i + size)
        for j in range(size // 2 + 1, size):
            low_bit = j & -j
            if low_bit < size // 2:
                for h in slots:
                    run(h, 0, j - low_bit, j)
        size *= 2
    for h in slots:
        p_ref[h, 0] = split(eye)
        s_ref[h, 0] = jnp.zeros((dim, 2 * dim), bf16)
        for n in range(1, blocks):
            p_ref[h, n], s_ref[h, n] = span[h, 0, n]


def reads_kernel(
    kept, slot, at, half, index_ref, query_ref, halo_ref, cq_ref, kv_ref, kb_ref, kv0_ref, kb0_ref,
    inv_ref, p_ref, s_ref, pulled_ref, local_ref, q0, query, scores, pulled,
):
    head = first_head(index_ref, kept, half) + at
    dim = q0.shape[1]
    blocks = inv_ref.shape[1]
    fill_rows(q0, own_halo(index_ref, halo_ref[head])[:, :dim], query_ref[head])
    cq = cq_ref[head]
    row = lax.broadcasted_iota(jnp.int32, (HALF, BLOCK), 0)
    col = lax.broadcasted_iota(jnp.int32, (HALF, BLOCK), 1)
    causal = step_time(col) <= 2 * row + 1
    rows = [slice(n * HALF, (n + 1) * HALF) for n in range(blocks)]
    for n in range(blocks):
        q = conv_taps(q0, cq, n * HALF, HALF)
        query[rows[n]] = q
        kbs = kb0_ref[head] if n == 0 else kb_ref[head, n - 1]
        scores[rows[n]] = split(jnp.where(causal, mm(split(q), kbs), 0.0))
    for n in range(blocks):
        scores[rows[n]] = split(mm(scores[rows[n]], inv_ref[slot, n]))
    for n in range(blocks):
        both = kv0_ref[head] if n == 0 else kv_ref[head, n - 1]
        pulled[rows[n]] = split(query[rows[n]] - mm(scores[rows[n]], both[:, : 2 * dim]))
        local_ref[rows[n]] = mm(scores[rows[n]], both[:, 2 * dim :])
    for n in range(blocks):
        local_ref[rows[n]] += mm(pulled[rows[n]], s_ref[slot, n])
        pulled_ref[rows[n]] = split(mm(pulled[rows[n]], p_ref[slot, n]))


def out_kernel(kept, start, half, index_ref, gain_ref, *rest):
    out_ref = rest[-1]
    for i in range(len(rest) // 3):
        state_ref, pulled_ref, local_ref = rest[3 * i : 3 * i + 3]

        @pl.when(pl.program_id(0) == i)
        def _():
            h = first_head(index_ref, kept, half) + start + i
            state = split(state_ref[0])
            gain = pick_row(gain_ref[...], h)
            for at in range(0, pulled_ref.shape[0], BLOCK):
                rows = slice(at, at + BLOCK)
                raw = mm(pulled_ref[rows], state) + local_ref[rows]
                mean = jnp.mean(raw * raw, 1, keepdims=True)
                out_ref[0, rows] = raw * lax.rsqrt(mean + 1e-06) * gain


def then(later, earlier):
    dim = later.shape[0]
    prod = mm(split(later[:, :dim]), split(earlier))
    wide = prod.shape[1]
    if wide == dim:
        return prod + later[:, dim:]
    return jnp.concatenate([prod[:, :dim], prod[:, dim:] + later[:, dim:]], 1)


def pair_kernel(slot, index_ref, mine_ref, got_ref, total_ref, earlier_ref):
    upper = (index_ref[0] & 1) != 0
    for h in range(mine_ref.shape[0]):
        mine = mine_ref[h]
        got = got_ref[slot + h]
        earlier = jnp.where(upper, got, mine)
        earlier_ref[h] = earlier
        total_ref[h] = then(jnp.where(upper, mine, got), earlier)


def join_kernel(bits, index_ref, *refs):
    size = 1 << len(bits)
    got_refs, before_ref, (total_ref, after_ref) = refs[:size], refs[size:-2], refs[-2:]
    ups = [(index_ref[0] & bit) != 0 for bit in bits]
    dim = got_refs[0].shape[1]
    row = lax.broadcasted_iota(jnp.int32, (dim, 2 * dim), 0)
    col = lax.broadcasted_iota(jnp.int32, (dim, 2 * dim), 1)
    for h in range(got_refs[0].shape[0]):
        maps = [ref[h] for ref in got_refs]
        for i, up in enumerate(ups):
            maps = [jnp.where(up, maps[j ^ (1 << i)], maps[j]) for j in range(size)]
        part = slice(dim, None) if total_ref.shape[2] == dim else slice(None)
        identity = (row == col).astype(f32)
        if size == 2:
            total_ref[h] = then(maps[1], maps[0][:, part])
            prefix = jnp.where(ups[0], maps[0], identity)
        else:
            low = then(maps[1], maps[0])
            total_ref[h] = then(then(maps[3], maps[2]), low[:, part])
            prefix = jnp.where(
                ups[1],
                jnp.where(ups[0], then(maps[2], low), low),
                jnp.where(ups[0], maps[0], identity),
            )
        after_ref[h] = then(before_ref[0][h], prefix) if before_ref else prefix


def down_kernel(bit, index_ref, before_ref, got_ref, earlier_ref, mine_ref, other_ref):
    upper = (index_ref[0] & 1) != 0
    got = jnp.where((index_ref[0] & bit) != 0, got_ref[0], 0.0)
    state = then(before_ref[0], got)
    after = then(earlier_ref[0], state)
    mine_ref[0] = jnp.where(upper, after, state)
    other_ref[0] = jnp.where(upper, state, after)


def tails_kernel(index_ref, query_ref, key_ref, value_ref, out_ref):
    rim = out_ref.shape[1]
    at = 0
    for ref in (query_ref, key_ref, value_ref):
        wide = ref.shape[2]
        out_ref[:, :, at : at + wide] = ref[:, ref.shape[1] - rim :, :]
        at += wide


def shape(dims, dtype):
    return jax.ShapeDtypeStruct(dims, dtype)


def resident(kernel, index, args, outs, scratch=(), limit=4 << 20):
    smem = pl.BlockSpec(memory_space=pltpu.SMEM)
    vmem = pl.BlockSpec(memory_space=pltpu.VMEM)
    return pl.pallas_call(
        kernel,
        in_specs=[smem] + [vmem] * len(args),
        out_specs=[vmem] * len(outs),
        out_shape=[pltpu.VMEM(o.shape, o.dtype) for o in outs],
        scratch_shapes=list(scratch),
        compiler_params=pltpu.CompilerParams(vmem_limit_bytes=limit),
    )(index, *[pltpu.with_memory_space_constraint(a, pltpu.VMEM) for a in args])


def swap(x, bit, count):
    return lax.ppermute(x, "seq", [(i, i ^ bit) for i in range(count)])


def per_device(
    queries, key_pairs, value_pairs, write_rates, conv_query, conv_key, conv_value, out_gain
):
    heads, tokens, dim = queries.shape
    blocks = tokens // HALF
    half = heads // 2
    rim = conv_query.shape[1] - 1
    count = lax.axis_size("seq")
    index = lax.axis_index("seq").reshape(1)

    parts = (queries, key_pairs, value_pairs)
    last = [
        pl.BlockSpec((heads, 16, x.shape[2]), lambda i, index_ref: (0, tokens // 16 - 1, 0))
        for x in parts
    ]
    tails = pl.pallas_call(
        tails_kernel,
        grid_spec=pltpu.PrefetchScalarGridSpec(
            num_scalar_prefetch=1,
            grid=(1,),
            in_specs=last,
            out_specs=pl.BlockSpec((heads, rim, 5 * dim), lambda i, index_ref: (0, 0, 0)),
        ),
        out_shape=shape((heads, rim, 5 * dim), bf16),
        compiler_params=pltpu.CompilerParams(vmem_limit_bytes=4 << 20),
    )(index, *[pltpu.with_memory_space_constraint(x, pltpu.HBM) for x in parts])
    halo = lax.ppermute(tails, "seq", [(i, (i + 1) % count) for i in range(count)])

    def in_order(*after):
        return lax.optimization_barrier((index, after))[0]

    inner = (heads, blocks - 1, BLOCK)
    front = resident(
        front_kernel,
        in_order(tails),
        (key_pairs, value_pairs, write_rates, conv_key, conv_value),
        [
            shape(inner + (4 * dim,), bf16),
            shape(inner + (2 * dim,), bf16),
            shape(inner + (BLOCK,), f32),
            shape((heads, blocks * GROUP, BLOCK), f32),
            shape((heads, blocks, BLOCK), f32),
        ],
        [
            pltpu.VMEM((4, tokens + 8, dim), f32),
            pltpu.VMEM((blocks, BLOCK), f32),
            pltpu.VMEM((heads, blocks * GROUP, BLOCK), f32),
            pltpu.VMEM((blocks - 1, BLOCK, dim), f32),
        ],
        LIMIT,
    )
    *front, rates = front
    halo = lax.optimization_barrier((halo, rates))[0]
    opening = resident(
        first_kernel,
        in_order(rates),
        (key_pairs, value_pairs, halo, conv_key, conv_value, rates),
        [
            shape((heads, BLOCK, 4 * dim), bf16),
            shape((heads, BLOCK, 2 * dim), bf16),
            shape((heads, BLOCK, BLOCK), f32),
            shape((heads * GROUP, BLOCK), f32),
        ],
        [
            pltpu.VMEM((heads, 4, HALF + 8, dim), f32),
            pltpu.VMEM((heads * GROUP, BLOCK), f32),
            pltpu.VMEM((heads, BLOCK, dim), f32),
        ],
        LIMIT,
    )

    def maps(kept, start, size, *after):
        wide = shape((size, blocks, BLOCK, 2 * dim), bf16)
        return resident(
            functools.partial(maps_kernel, kept, start, half),
            in_order(*after),
            (*front, *opening),
            [wide] * 3 + [shape((size, dim, 2 * dim), f32)],
            [pltpu.VMEM((size, blocks, dim, 2 * dim), bf16)] * 2,
            LIMIT,
        )

    def reads(kept, at, *after):
        slot, saved = (0, kept_saved[at]) if kept else (at, sent_saved)
        return resident(
            functools.partial(reads_kernel, kept, slot, at, half),
            in_order(*after),
            (queries, halo, conv_query, *front[:2], *opening[:2], *saved),
            [shape((tokens, 2 * dim), bf16), shape((tokens, dim), f32)],
            [
                pltpu.VMEM((tokens + 8, dim), f32),
                pltpu.VMEM((tokens, dim), f32),
                pltpu.VMEM((tokens, 2 * dim), bf16),
                pltpu.VMEM((tokens, 2 * dim), bf16),
            ],
            LIMIT,
        )

    total_shape = shape((1, dim, 2 * dim), f32)
    state_shape = shape((1, dim, dim), f32)
    bits = []
    while 2 << len(bits) < count:
        bits.append(2 << len(bits))
    chains = {}

    def begin(at, got, *after):
        total, earlier = resident(
            functools.partial(pair_kernel, at),
            in_order(*after),
            (kept_total[at], got),
            [total_shape] * 2,
        )
        chains[at] = dict(current=total, earlier=earlier, before=(), left=[(bit,) for bit in bits[:-1]])
        send(at)
        return total

    def send(at):
        chain = chains[at]
        now = chain["left"][0] if chain["left"] else bits[-1:]
        flips = [sum(b for i, b in enumerate(now) if j >> i & 1) for j in range(1 << len(now))]
        chain["got"] = [swap(chain["current"], flip, count) for flip in flips[1:]]

    def join(at, *after):
        chain = chains[at]
        now = chain["left"].pop(0)
        got = lax.optimization_barrier((chain["got"], after))[0]
        chain["current"], before = resident(
            functools.partial(join_kernel, now),
            index,
            (chain["current"], *got, *chain["before"]),
            [total_shape if chain["left"] else state_shape, total_shape],
        )
        chain["before"] = (before,)
        send(at)
        return chain["current"]

    def down(at, *after):
        chain = chains[at]
        got = lax.optimization_barrier((chain["got"], after))[0][0]
        return resident(
            functools.partial(down_kernel, bits[-1]),
            index,
            (*chain["before"], got, chain["earlier"]),
            [state_shape] * 2,
        )

    out_shape = shape((heads, tokens, dim), f32)
    done = ()

    def finish(kept, start, states, *after):
        nonlocal done
        vmem = pl.BlockSpec(memory_space=pltpu.VMEM)

        def out_block(i, index_ref):
            upper = index_ref[0] & 1
            return ((upper if kept else 1 - upper) * half + start + i, 0, 0)

        args = [out_gain]
        for i, state in enumerate(states):
            args += [state, *read[kept, start + i]]
        args = [pltpu.with_memory_space_constraint(a, pltpu.VMEM) for a in args]

        def kernel(index_ref, *refs):
            out_kernel(kept, start, half, index_ref, *refs[: len(args)], refs[-1])

        out = pl.pallas_call(
            kernel,
            grid_spec=pltpu.PrefetchScalarGridSpec(
                num_scalar_prefetch=1,
                grid=(len(states),),
                in_specs=[vmem] * len(args) + [pl.BlockSpec(memory_space=pl.ANY)] * len(done),
                out_specs=pl.BlockSpec((1, tokens, dim), out_block),
            ),
            out_shape=out_shape,
            input_output_aliases={len(args) + 1: 0} if done else {},
            compiler_params=pltpu.CompilerParams(vmem_limit_bytes=LIMIT),
        )(in_order(*after), *args, *done)
        done = (out,)
        return out

    kept_saved, kept_total, read = {}, {}, {}

    def keep(at, *after):
        *kept_saved[at], kept_total[at] = maps(True, at, 1, *after)

    *sent_saved, sent_total = maps(False, 0, half)
    got = swap(sent_total, 1, count)
    keep(0, sent_total)
    step = begin(0, got)
    for at in range(1, half):
        keep(at, step)
        step = begin(at, got, kept_total[at])
    step = (step,)
    todo = [(kept, at) for at in range(half) for kept in (False, True)]

    def read_some(pieces, *after):
        for _ in range(min(pieces, len(todo))):
            kept, at = todo.pop(0)
            read[kept, at] = reads(kept, at, *after)
            after = tuple(read[kept, at])
        return after

    while any(chain["left"] for chain in chains.values()):
        for at in range(half):
            if chains[at]["left"]:
                step = (join(at, *step),)
                if at == 0 or len(todo) > 1 + half:
                    step = read_some(1, *step)
    step = read_some(len(todo), *step)
    mine, other = {}, {}
    for at in range(half):
        mine[at], other[at] = down(at, *step)
        step = (mine[at],)
    others = swap(jnp.concatenate([other[at] for at in range(half)], 0), 1, count)
    last = finish(True, 0, [mine[at] for at in range(half)])
    others = lax.optimization_barrier((others, last))[0]
    return finish(False, 0, [others[at : at + 1] for at in range(half)])


def solution(mesh):
    return jax.shard_map(
        per_device,
        mesh=mesh,
        in_specs=(
            P(None, ("grp", "seq"), None),
            P(None, ("grp", "seq"), None),
            P(None, ("grp", "seq"), None),
            P(None, ("grp", "seq")),
            P(),
            P(),
            P(),
            P(),
        ),
        out_specs=P(None, ("grp", "seq"), None),
        check_vma=False,
    )
```

```python
import functools

import jax
import jax.numpy as jnp
from jax import lax
from jax.experimental import pallas as pl
from jax.experimental.pallas import tpu as pltpu
from jax.sharding import PartitionSpec as P

BLOCK = 128
GROUP = 16
HALF = BLOCK // 2
LIMIT = 20 << 20

f32 = jnp.float32
bf16 = jnp.bfloat16


def split(x):
    high = x.astype(bf16)
    low = (x - high.astype(f32)).astype(bf16)
    return jnp.concatenate([high, low], 1)


def mm(a, b):
    n = b.shape[1] // 2
    m, k = a.shape[0], b.shape[0]
    if m <= HALF:
        p = jnp.dot(
            jnp.concatenate([a[:, :k], a[:, k:]], 0), b, preferred_element_type=f32
        )
        p = p[:m] + p[m:]
        return p[:, :n] + p[:, n:]
    p = jnp.dot(a, jnp.concatenate([b, b], 0), preferred_element_type=f32)
    return p[:, :n] + p[:, n:]


def pick_row(x, r):
    row = lax.broadcasted_iota(jnp.int32, x.shape, 0)
    return jnp.sum(jnp.where(row == r, x, 0.0), 0, keepdims=True)


def silu(x):
    return x / (1.0 + jnp.exp(-x))


def step_time(r):
    return (r // GROUP) * GROUP + 2 * (r % 8) + (r // 8) % 2


def interleave(a, b):
    parts = []
    for g in range(0, a.shape[0], 8):
        parts += [a[g : g + 8], b[g : g + 8]]
    return jnp.concatenate(parts, 0)


def conv_taps(ref, weights, start, count):
    taps = weights.shape[0]
    total = weights[0:1] * ref[pl.ds(start + 9 - taps, count), :]
    for s in range(1, taps):
        total = total + weights[s : s + 1] * ref[pl.ds(start + 9 - taps + s, count), :]
    return silu(total)


def fill_rows(ref, halo, rows):
    rim = halo.shape[0]
    ref[8 - rim : 8, :] = halo.astype(f32)
    ref[8:, :] = rows.astype(f32)


def first_head(index_ref, kept, half):
    upper = index_ref[0] & 1
    return (upper if kept else 1 - upper) * half


def block_masks():
    row = lax.broadcasted_iota(jnp.int32, (BLOCK, BLOCK), 0)
    col = lax.broadcasted_iota(jnp.int32, (BLOCK, BLOCK), 1)
    lane = lax.broadcasted_iota(jnp.int32, (GROUP, BLOCK), 1)
    return row, col, lane


def block_inputs(units, keys):
    row, col, lane = block_masks()
    strict = step_time(col) < step_time(row)
    for i, (rows, ck, cv, t0, rates, kv, kb, low, diag) in enumerate(units):
        dim = rows[0].shape[1]
        taps = [w[:, j * dim : (j + 1) * dim] for w in (ck, cv) for j in range(2)]
        ka, kb_, va, vb = [conv_taps(r, w, t0, HALF) for r, w in zip(rows, taps)]
        k = interleave(ka, kb_)
        k = k * lax.rsqrt(jnp.sum(k * k, 1, keepdims=True) + 1e-06)
        keys[i] = k
        kv[:, : 2 * dim] = split(k)
        kv[:, 2 * dim :] = split(interleave(va, vb))
    for i, (rows, ck, cv, t0, rates, kv, kb, low, diag) in enumerate(units):
        kb[...] = split(keys[i].T * rates)
    for i, (rows, ck, cv, t0, rates, kv, kb, low, diag) in enumerate(units):
        lower = jnp.where(strict, mm(kv[:, : kb.shape[1]], kb[...]), 0.0)
        low[...] = lower
        groups = jnp.zeros((GROUP, BLOCK), f32)
        for g in range(BLOCK // GROUP):
            groups = jnp.where(lane // GROUP == g, lower[g * GROUP : (g + 1) * GROUP], groups)
        diag[...] = groups


def invert_groups(diag, out, blocks):
    lane = lax.broadcasted_iota(jnp.int32, (blocks, BLOCK), 1)
    times = [t // 2 + 8 * (t % 2) for t in range(GROUP)]
    coef = [diag[pl.ds(r, blocks, stride=GROUP), :] for r in range(GROUP)]
    sol = [(lane % GROUP == r).astype(f32) for r in range(GROUP)]
    for i, s in enumerate(times):
        pick = (lane // GROUP) * GROUP + s
        for r in times[i + 1 :]:
            sol[r] = sol[r] - jnp.take_along_axis(coef[r], pick, axis=1) * sol[s]
    for r in range(GROUP):
        out[pl.ds(r, blocks, stride=GROUP), :] = sol[r]


def front_kernel(
    index_ref, key_ref, value_ref, rate_ref, ck_ref, cv_ref,
    kv_ref, kb_ref, low_ref, sol_ref, rates_ref, rows, brow, diag, keys,
):
    dim = rows.shape[2]
    blocks = rates_ref.shape[1]
    row, col, _ = block_masks()
    order = (row == step_time(col)).astype(f32)

    def one(h, carry):
        for i, ref in enumerate((key_ref, value_ref)):
            for j in range(2):
                rows[2 * i + j, 8:, :] = ref[h, :, j * dim : (j + 1) * dim].astype(f32)
        for n in range(blocks):
            brow[n : n + 1, :] = pick_row(rate_ref[:, n * BLOCK : (n + 1) * BLOCK], h)
        rates = jnp.dot(
            brow[...], order, precision=lax.Precision.HIGHEST, preferred_element_type=f32
        )
        rates_ref[h] = rates
        ck, cv = ck_ref[h], cv_ref[h]
        block_inputs(
            [
                (
                    [rows.at[i] for i in range(4)], ck, cv, n * HALF, rates[n : n + 1],
                    kv_ref.at[h, n - 1], kb_ref.at[h, n - 1], low_ref.at[h, n - 1],
                    diag.at[h, n * GROUP : (n + 1) * GROUP],
                )
                for n in range(1, blocks)
            ],
            keys,
        )
        diag[h, 0:GROUP] = jnp.zeros((GROUP, BLOCK), f32)
        return carry

    lax.fori_loop(0, key_ref.shape[0], one, 0)
    for h in range(key_ref.shape[0]):
        invert_groups(diag.at[h], sol_ref.at[h], blocks)


def first_kernel(
    index_ref, key_ref, value_ref, halo_ref, ck_ref, cv_ref, rates_ref,
    kv_ref, kb_ref, low_ref, sol_ref, rows, diag, keys,
):
    heads = key_ref.shape[0]
    dim = rows.shape[3]
    for h in range(heads):
        halo = own_halo(index_ref, halo_ref[h])
        for i, ref in enumerate((key_ref, value_ref)):
            for j in range(2):
                at = (1 + 2 * i + j) * dim
                fill_rows(
                    rows.at[h, 2 * i + j],
                    halo[:, at : at + dim],
                    ref[h, :HALF, j * dim : (j + 1) * dim],
                )
    block_inputs(
        [
            (
                [rows.at[h, i] for i in range(4)], ck_ref[h], cv_ref[h], 0, rates_ref[h][0:1],
                kv_ref.at[h], kb_ref.at[h], low_ref.at[h], diag.at[h * GROUP : (h + 1) * GROUP],
            )
            for h in range(heads)
        ],
        keys,
    )
    invert_groups(diag, sol_ref, heads)


def own_halo(index_ref, halo):
    return jnp.where(index_ref[0] == 0, 0.0, halo.astype(f32))


def maps_kernel(
    kept, start, half, index_ref, kv_ref, kb_ref, low_ref, sol_ref,
    kv0_ref, kb0_ref, low0_ref, sol0_ref,
    inv_ref, p_ref, s_ref, total_ref, move, written,
):
    count, blocks = inv_ref.shape[:2]
    dim = total_ref.shape[1]
    slots = range(count)
    first = first_head(index_ref, kept, half) + start
    row, col, lane = block_masks()
    eye = (row == col).astype(f32)

    def at(inner, first_one, h, n):
        return first_one[first + h] if n == 0 else inner[first + h, n - 1]

    for h in slots:
        for n in range(blocks):
            if n == 0:
                base = sol0_ref[pl.ds((first + h) * GROUP, GROUP), :]
            else:
                base = sol_ref[first + h, n * GROUP : (n + 1) * GROUP, :]
            inv_ref[h, n] = split(
                jnp.concatenate(
                    [jnp.where(lane // GROUP == g, base, 0.0) for g in range(BLOCK // GROUP)], 0
                )
            )

    lane_h = lax.broadcasted_iota(jnp.int32, (HALF, BLOCK), 1)
    row_h = lax.broadcasted_iota(jnp.int32, (HALF, BLOCK), 0)
    size = GROUP
    while size < BLOCK:
        keep = lane_h // size == 2 * (row_h // size)
        starts = range(size, BLOCK, 2 * size)
        for h in slots:
            for n in range(blocks):
                inv = inv_ref[h, n]
                lower = at(low_ref, low0_ref, h, n)
                low = jnp.concatenate([lower[a : a + size] for a in starts], 0)
                z = split(mm(split(jnp.where(keep, low, 0.0)), inv))
                twice = []
                for i in range(len(starts)):
                    twice += [z[i * size : (i + 1) * size]] * 2
                odd = jnp.concatenate([inv[a : a + size] for a in starts], 0)
                new = mm(odd, jnp.concatenate(twice, 0))
                new = split(odd[:, :BLOCK].astype(f32) + odd[:, BLOCK:].astype(f32) - new)
                for i, a in enumerate(starts):
                    inv_ref[h, n, a : a + size] = new[i * size : (i + 1) * size]
        size *= 2

    for h in slots:
        for n in range(blocks):
            move[h, n] = split(mm(at(kb_ref, kb0_ref, h, n), inv_ref[h, n]))
    for h in slots:
        for n in range(blocks):
            both = at(kv_ref, kv0_ref, h, n)
            solved = move[h, n]
            written[h, n] = split(mm(solved, both[:, 2 * dim :]))
            move[h, n] = split(eye - mm(solved, both[:, : 2 * dim]))

    span = {(h, n, n + 1): (move[h, n], written[h, n]) for h in slots for n in range(blocks)}

    def run(h, i, mid, j):
        later, earlier = span[h, mid, j], span[h, i, mid]
        state = later[1]
        added = state[:, :dim].astype(f32) + state[:, dim:].astype(f32)
        full = (mm(later[0], earlier[0]), mm(later[0], earlier[1]) + added)
        if (i, j) == (0, blocks):
            total_ref[h, :, :dim], total_ref[h, :, dim:] = full
        span[h, i, j] = tuple(split(x) for x in full)

    size = 2
    while size <= blocks:
        for i in range(0, blocks, size):
            for j in range(i + size // 2 + 1, i + size + 1):
                for h in slots:
                    run(h, i, i + size // 2, j)
        size *= 2
    for h in slots:
        p_ref[h, 0] = split(eye)
        s_ref[h, 0] = jnp.zeros((dim, 2 * dim), bf16)
        for n in range(1, blocks):
            p_ref[h, n], s_ref[h, n] = span[h, 0, n]


def reads_kernel(
    kept, slot, at, half, index_ref, query_ref, halo_ref, cq_ref, kv_ref, kb_ref, kv0_ref, kb0_ref,
    inv_ref, p_ref, s_ref, pulled_ref, local_ref, q0, query, scores, pulled,
):
    head = first_head(index_ref, kept, half) + at
    dim = q0.shape[1]
    blocks = inv_ref.shape[1]
    fill_rows(q0, own_halo(index_ref, halo_ref[head])[:, :dim], query_ref[head])
    cq = cq_ref[head]
    row = lax.broadcasted_iota(jnp.int32, (HALF, BLOCK), 0)
    col = lax.broadcasted_iota(jnp.int32, (HALF, BLOCK), 1)
    causal = step_time(col) <= 2 * row + 1
    rows = [slice(n * HALF, (n + 1) * HALF) for n in range(blocks)]
    for n in range(blocks):
        q = conv_taps(q0, cq, n * HALF, HALF)
        query[rows[n]] = q
        kbs = kb0_ref[head] if n == 0 else kb_ref[head, n - 1]
        scores[rows[n]] = split(jnp.where(causal, mm(split(q), kbs), 0.0))
    for n in range(blocks):
        scores[rows[n]] = split(mm(scores[rows[n]], inv_ref[slot, n]))
    for n in range(blocks):
        both = kv0_ref[head] if n == 0 else kv_ref[head, n - 1]
        pulled[rows[n]] = split(query[rows[n]] - mm(scores[rows[n]], both[:, : 2 * dim]))
        local_ref[rows[n]] = mm(scores[rows[n]], both[:, 2 * dim :])
    for n in range(blocks):
        local_ref[rows[n]] += mm(pulled[rows[n]], s_ref[slot, n])
        pulled_ref[rows[n]] = split(mm(pulled[rows[n]], p_ref[slot, n]))


def out_kernel(kept, start, half, index_ref, gain_ref, *rest):
    out_ref = rest[-1]
    for i in range(len(rest) // 3):
        state_ref, pulled_ref, local_ref = rest[3 * i : 3 * i + 3]

        @pl.when(pl.program_id(0) == i)
        def _():
            h = first_head(index_ref, kept, half) + start + i
            state = split(state_ref[0])
            gain = pick_row(gain_ref[...], h)
            for at in range(0, pulled_ref.shape[0], BLOCK):
                rows = slice(at, at + BLOCK)
                raw = mm(pulled_ref[rows], state) + local_ref[rows]
                mean = jnp.mean(raw * raw, 1, keepdims=True)
                out_ref[0, rows] = raw * lax.rsqrt(mean + 1e-06) * gain


def then(later, earlier):
    dim = later.shape[0]
    prod = mm(split(later[:, :dim]), split(earlier))
    wide = prod.shape[1]
    if wide == dim:
        return prod + later[:, dim:]
    return jnp.concatenate([prod[:, :dim], prod[:, dim:] + later[:, dim:]], 1)


def pair_kernel(slot, index_ref, mine_ref, got_ref, total_ref, earlier_ref):
    upper = (index_ref[0] & 1) != 0
    for h in range(mine_ref.shape[0]):
        mine = mine_ref[h]
        got = got_ref[slot + h]
        earlier = jnp.where(upper, got, mine)
        earlier_ref[h] = earlier
        total_ref[h] = then(jnp.where(upper, mine, got), earlier)


def join_kernel(bits, index_ref, *refs):
    size = 1 << len(bits)
    got_refs, before_ref, (total_ref, after_ref) = refs[:size], refs[size:-2], refs[-2:]
    ups = [(index_ref[0] & bit) != 0 for bit in bits]
    dim = got_refs[0].shape[1]
    row = lax.broadcasted_iota(jnp.int32, (dim, 2 * dim), 0)
    col = lax.broadcasted_iota(jnp.int32, (dim, 2 * dim), 1)
    for h in range(got_refs[0].shape[0]):
        maps = [ref[h] for ref in got_refs]
        for i, up in enumerate(ups):
            maps = [jnp.where(up, maps[j ^ (1 << i)], maps[j]) for j in range(size)]
        part = slice(dim, None) if total_ref.shape[2] == dim else slice(None)
        identity = (row == col).astype(f32)
        if size == 2:
            total_ref[h] = then(maps[1], maps[0][:, part])
            prefix = jnp.where(ups[0], maps[0], identity)
        else:
            low = then(maps[1], maps[0])
            total_ref[h] = then(then(maps[3], maps[2]), low[:, part])
            prefix = jnp.where(
                ups[1],
                jnp.where(ups[0], then(maps[2], low), low),
                jnp.where(ups[0], maps[0], identity),
            )
        after_ref[h] = then(before_ref[0][h], prefix) if before_ref else prefix


def down_kernel(bit, index_ref, before_ref, got_ref, earlier_ref, mine_ref, other_ref):
    upper = (index_ref[0] & 1) != 0
    got = jnp.where((index_ref[0] & bit) != 0, got_ref[0], 0.0)
    state = then(before_ref[0], got)
    after = then(earlier_ref[0], state)
    mine_ref[0] = jnp.where(upper, after, state)
    other_ref[0] = jnp.where(upper, state, after)


def tails_kernel(index_ref, query_ref, key_ref, value_ref, out_ref):
    rim = out_ref.shape[1]
    at = 0
    for ref in (query_ref, key_ref, value_ref):
        wide = ref.shape[2]
        out_ref[:, :, at : at + wide] = ref[:, ref.shape[1] - rim :, :]
        at += wide


def shape(dims, dtype):
    return jax.ShapeDtypeStruct(dims, dtype)


def resident(kernel, index, args, outs, scratch=(), limit=4 << 20):
    smem = pl.BlockSpec(memory_space=pltpu.SMEM)
    vmem = pl.BlockSpec(memory_space=pltpu.VMEM)
    return pl.pallas_call(
        kernel,
        in_specs=[smem] + [vmem] * len(args),
        out_specs=[vmem] * len(outs),
        out_shape=[pltpu.VMEM(o.shape, o.dtype) for o in outs],
        scratch_shapes=list(scratch),
        compiler_params=pltpu.CompilerParams(vmem_limit_bytes=limit),
    )(index, *[pltpu.with_memory_space_constraint(a, pltpu.VMEM) for a in args])


def swap(x, bit, count):
    return lax.ppermute(x, "seq", [(i, i ^ bit) for i in range(count)])


def per_device(
    queries, key_pairs, value_pairs, write_rates, conv_query, conv_key, conv_value, out_gain
):
    heads, tokens, dim = queries.shape
    blocks = tokens // HALF
    half = heads // 2
    rim = conv_query.shape[1] - 1
    count = lax.axis_size("seq")
    index = lax.axis_index("seq").reshape(1)

    parts = (queries, key_pairs, value_pairs)
    last = [
        pl.BlockSpec((heads, 16, x.shape[2]), lambda i, index_ref: (0, tokens // 16 - 1, 0))
        for x in parts
    ]
    tails = pl.pallas_call(
        tails_kernel,
        grid_spec=pltpu.PrefetchScalarGridSpec(
            num_scalar_prefetch=1,
            grid=(1,),
            in_specs=last,
            out_specs=pl.BlockSpec((heads, rim, 5 * dim), lambda i, index_ref: (0, 0, 0)),
        ),
        out_shape=shape((heads, rim, 5 * dim), bf16),
        compiler_params=pltpu.CompilerParams(vmem_limit_bytes=4 << 20),
    )(index, *[pltpu.with_memory_space_constraint(x, pltpu.HBM) for x in parts])
    halo = lax.ppermute(tails, "seq", [(i, (i + 1) % count) for i in range(count)])

    def in_order(*after):
        return lax.optimization_barrier((index, after))[0]

    inner = (heads, blocks - 1, BLOCK)
    front = resident(
        front_kernel,
        in_order(tails),
        (key_pairs, value_pairs, write_rates, conv_key, conv_value),
        [
            shape(inner + (4 * dim,), bf16),
            shape(inner + (2 * dim,), bf16),
            shape(inner + (BLOCK,), f32),
            shape((heads, blocks * GROUP, BLOCK), f32),
            shape((heads, blocks, BLOCK), f32),
        ],
        [
            pltpu.VMEM((4, tokens + 8, dim), f32),
            pltpu.VMEM((blocks, BLOCK), f32),
            pltpu.VMEM((heads, blocks * GROUP, BLOCK), f32),
            pltpu.VMEM((blocks - 1, BLOCK, dim), f32),
        ],
        LIMIT,
    )
    *front, rates = front
    halo = lax.optimization_barrier((halo, rates))[0]
    opening = resident(
        first_kernel,
        in_order(rates),
        (key_pairs, value_pairs, halo, conv_key, conv_value, rates),
        [
            shape((heads, BLOCK, 4 * dim), bf16),
            shape((heads, BLOCK, 2 * dim), bf16),
            shape((heads, BLOCK, BLOCK), f32),
            shape((heads * GROUP, BLOCK), f32),
        ],
        [
            pltpu.VMEM((heads, 4, HALF + 8, dim), f32),
            pltpu.VMEM((heads * GROUP, BLOCK), f32),
            pltpu.VMEM((heads, BLOCK, dim), f32),
        ],
        LIMIT,
    )

    def maps(kept, start, size, *after):
        wide = shape((size, blocks, BLOCK, 2 * dim), bf16)
        return resident(
            functools.partial(maps_kernel, kept, start, half),
            in_order(*after),
            (*front, *opening),
            [wide] * 3 + [shape((size, dim, 2 * dim), f32)],
            [pltpu.VMEM((size, blocks, dim, 2 * dim), bf16)] * 2,
            LIMIT,
        )

    def reads(kept, at, *after):
        slot, saved = (0, kept_saved[at]) if kept else (at, sent_saved)
        return resident(
            functools.partial(reads_kernel, kept, slot, at, half),
            in_order(*after),
            (queries, halo, conv_query, *front[:2], *opening[:2], *saved),
            [shape((tokens, 2 * dim), bf16), shape((tokens, dim), f32)],
            [
                pltpu.VMEM((tokens + 8, dim), f32),
                pltpu.VMEM((tokens, dim), f32),
                pltpu.VMEM((tokens, 2 * dim), bf16),
                pltpu.VMEM((tokens, 2 * dim), bf16),
            ],
            LIMIT,
        )

    total_shape = shape((1, dim, 2 * dim), f32)
    state_shape = shape((1, dim, dim), f32)
    bits = []
    while 2 << len(bits) < count:
        bits.append(2 << len(bits))
    chains = {}

    def begin(at, got, *after):
        total, earlier = resident(
            functools.partial(pair_kernel, at),
            in_order(*after),
            (kept_total[at], got),
            [total_shape] * 2,
        )
        chains[at] = dict(current=total, earlier=earlier, before=(), left=[(bit,) for bit in bits[:-1]])
        send(at)
        return total

    def send(at):
        chain = chains[at]
        now = chain["left"][0] if chain["left"] else bits[-1:]
        flips = [sum(b for i, b in enumerate(now) if j >> i & 1) for j in range(1 << len(now))]
        chain["got"] = [swap(chain["current"], flip, count) for flip in flips[1:]]

    def join(at, *after):
        chain = chains[at]
        now = chain["left"].pop(0)
        got = lax.optimization_barrier((chain["got"], after))[0]
        chain["current"], before = resident(
            functools.partial(join_kernel, now),
            index,
            (chain["current"], *got, *chain["before"]),
            [total_shape if chain["left"] else state_shape, total_shape],
        )
        chain["before"] = (before,)
        send(at)
        return chain["current"]

    def down(at, *after):
        chain = chains[at]
        got = lax.optimization_barrier((chain["got"], after))[0][0]
        return resident(
            functools.partial(down_kernel, bits[-1]),
            index,
            (*chain["before"], got, chain["earlier"]),
            [state_shape] * 2,
        )

    out_shape = shape((heads, tokens, dim), f32)
    done = ()

    def finish(kept, start, states, *after):
        nonlocal done
        vmem = pl.BlockSpec(memory_space=pltpu.VMEM)

        def out_block(i, index_ref):
            upper = index_ref[0] & 1
            return ((upper if kept else 1 - upper) * half + start + i, 0, 0)

        args = [out_gain]
        for i, state in enumerate(states):
            args += [state, *read[kept, start + i]]
        args = [pltpu.with_memory_space_constraint(a, pltpu.VMEM) for a in args]

        def kernel(index_ref, *refs):
            out_kernel(kept, start, half, index_ref, *refs[: len(args)], refs[-1])

        out = pl.pallas_call(
            kernel,
            grid_spec=pltpu.PrefetchScalarGridSpec(
                num_scalar_prefetch=1,
                grid=(len(states),),
                in_specs=[vmem] * len(args) + [pl.BlockSpec(memory_space=pl.ANY)] * len(done),
                out_specs=pl.BlockSpec((1, tokens, dim), out_block),
            ),
            out_shape=out_shape,
            input_output_aliases={len(args) + 1: 0} if done else {},
            compiler_params=pltpu.CompilerParams(vmem_limit_bytes=LIMIT),
        )(in_order(*after), *args, *done)
        done = (out,)
        return out

    kept_saved, kept_total, read = {}, {}, {}

    def keep(at, *after):
        *kept_saved[at], kept_total[at] = maps(True, at, 1, *after)

    *sent_saved, sent_total = maps(False, 0, half)
    got = swap(sent_total, 1, count)
    keep(0, sent_total)
    step = begin(0, got)
    for at in range(1, half):
        keep(at, step)
        step = begin(at, got, kept_total[at])
    step = (step,)
    todo = [(kept, at) for at in range(half) for kept in (False, True)]

    def read_some(pieces, *after):
        for _ in range(min(pieces, len(todo))):
            kept, at = todo.pop(0)
            read[kept, at] = reads(kept, at, *after)
            after = tuple(read[kept, at])
        return after

    while any(chain["left"] for chain in chains.values()):
        for at in range(half):
            if chains[at]["left"]:
                step = (join(at, *step),)
                if len(todo) > half:
                    step = read_some(1, *step)
    step = read_some(len(todo), *step)
    mine, other = {}, {}
    for at in range(half):
        mine[at], other[at] = down(at, *step)
        step = (mine[at],)
    others = swap(jnp.concatenate([other[at] for at in range(half)], 0), 1, count)
    last = finish(True, 0, [mine[at] for at in range(half)])
    others = lax.optimization_barrier((others, last))[0]
    return finish(False, 0, [others[at : at + 1] for at in range(half)])


def solution(mesh):
    return jax.shard_map(
        per_device,
        mesh=mesh,
        in_specs=(
            P(None, ("grp", "seq"), None),
            P(None, ("grp", "seq"), None),
            P(None, ("grp", "seq"), None),
            P(None, ("grp", "seq")),
            P(),
            P(),
            P(),
            P(),
        ),
        out_specs=P(None, ("grp", "seq"), None),
        check_vma=False,
    )
```

```python
import functools

import jax
import jax.numpy as jnp
from jax import lax
from jax.experimental import pallas as pl
from jax.experimental.pallas import tpu as pltpu
from jax.sharding import PartitionSpec as P

BLOCK = 128
GROUP = 16
HALF = BLOCK // 2
LIMIT = 20 << 20

f32 = jnp.float32
bf16 = jnp.bfloat16


def split(x):
    high = x.astype(bf16)
    low = (x - high.astype(f32)).astype(bf16)
    return jnp.concatenate([high, low], 1)


def mm(a, b):
    n = b.shape[1] // 2
    m, k = a.shape[0], b.shape[0]
    if m <= HALF:
        p = jnp.dot(
            jnp.concatenate([a[:, :k], a[:, k:]], 0), b, preferred_element_type=f32
        )
        p = p[:m] + p[m:]
        return p[:, :n] + p[:, n:]
    p = jnp.dot(a, jnp.concatenate([b, b], 0), preferred_element_type=f32)
    return p[:, :n] + p[:, n:]


def pick_row(x, r):
    row = lax.broadcasted_iota(jnp.int32, x.shape, 0)
    return jnp.sum(jnp.where(row == r, x, 0.0), 0, keepdims=True)


def silu(x):
    return x / (1.0 + jnp.exp(-x))


def step_time(r):
    return (r // GROUP) * GROUP + 2 * (r % 8) + (r // 8) % 2


def interleave(a, b):
    parts = []
    for g in range(0, a.shape[0], 8):
        parts += [a[g : g + 8], b[g : g + 8]]
    return jnp.concatenate(parts, 0)


def conv_taps(ref, weights, start, count):
    taps = weights.shape[0]
    total = weights[0:1] * ref[pl.ds(start + 9 - taps, count), :]
    for s in range(1, taps):
        total = total + weights[s : s + 1] * ref[pl.ds(start + 9 - taps + s, count), :]
    return silu(total)


def fill_rows(ref, halo, rows):
    rim = halo.shape[0]
    ref[8 - rim : 8, :] = halo.astype(f32)
    ref[8:, :] = rows.astype(f32)


def first_head(index_ref, kept, half):
    upper = index_ref[0] & 1
    return (upper if kept else 1 - upper) * half


def block_masks():
    row = lax.broadcasted_iota(jnp.int32, (BLOCK, BLOCK), 0)
    col = lax.broadcasted_iota(jnp.int32, (BLOCK, BLOCK), 1)
    lane = lax.broadcasted_iota(jnp.int32, (GROUP, BLOCK), 1)
    return row, col, lane


def block_inputs(units, keys):
    row, col, lane = block_masks()
    strict = step_time(col) < step_time(row)
    for i, (rows, ck, cv, t0, rates, kv, kb, low, diag) in enumerate(units):
        dim = rows[0].shape[1]
        taps = [w[:, j * dim : (j + 1) * dim] for w in (ck, cv) for j in range(2)]
        ka, kb_, va, vb = [conv_taps(r, w, t0, HALF) for r, w in zip(rows, taps)]
        k = interleave(ka, kb_)
        k = k * lax.rsqrt(jnp.sum(k * k, 1, keepdims=True) + 1e-06)
        keys[i] = k
        kv[:, : 2 * dim] = split(k)
        kv[:, 2 * dim :] = split(interleave(va, vb))
    for i, (rows, ck, cv, t0, rates, kv, kb, low, diag) in enumerate(units):
        kb[...] = split(keys[i].T * rates)
    for i, (rows, ck, cv, t0, rates, kv, kb, low, diag) in enumerate(units):
        lower = jnp.where(strict, mm(kv[:, : kb.shape[1]], kb[...]), 0.0)
        low[...] = lower
        groups = jnp.zeros((GROUP, BLOCK), f32)
        for g in range(BLOCK // GROUP):
            groups = jnp.where(lane // GROUP == g, lower[g * GROUP : (g + 1) * GROUP], groups)
        diag[...] = groups


def invert_groups(diag, out, blocks):
    lane = lax.broadcasted_iota(jnp.int32, (blocks, BLOCK), 1)
    times = [t // 2 + 8 * (t % 2) for t in range(GROUP)]
    coef = [diag[pl.ds(r, blocks, stride=GROUP), :] for r in range(GROUP)]
    sol = [(lane % GROUP == r).astype(f32) for r in range(GROUP)]
    for i, s in enumerate(times):
        pick = (lane // GROUP) * GROUP + s
        for r in times[i + 1 :]:
            sol[r] = sol[r] - jnp.take_along_axis(coef[r], pick, axis=1) * sol[s]
    for r in range(GROUP):
        out[pl.ds(r, blocks, stride=GROUP), :] = sol[r]


def front_kernel(
    early, index_ref, key_ref, value_ref, rate_ref, ck_ref, cv_ref, *refs
):
    if early:
        kv_ref, kb_ref, low_ref, diag, rates_ref, rows, brow, keys = refs
    else:
        kv_ref, kb_ref, low_ref, diag, rates_ref, sol_ref, rows, brow, keys = refs[5:]
    upper = index_ref[0] & 1
    dim = rows.shape[2]
    blocks = rates_ref.shape[1]
    row, col, _ = block_masks()
    order = (row == step_time(col)).astype(f32)

    def one(h, carry):
        for i, ref in enumerate((key_ref, value_ref)):
            for j in range(2):
                rows[2 * i + j, 8:, :] = ref[h, :, j * dim : (j + 1) * dim].astype(f32)
        for n in range(blocks):
            brow[n : n + 1, :] = pick_row(rate_ref[:, n * BLOCK : (n + 1) * BLOCK], h)
        rates = jnp.dot(
            brow[...], order, precision=lax.Precision.HIGHEST, preferred_element_type=f32
        )
        rates_ref[h] = rates
        ck, cv = ck_ref[h], cv_ref[h]
        block_inputs(
            [
                (
                    [rows.at[i] for i in range(4)], ck, cv, n * HALF, rates[n : n + 1],
                    kv_ref.at[h, n - 1], kb_ref.at[h, n - 1], low_ref.at[h, n - 1],
                    diag.at[h, n * GROUP : (n + 1) * GROUP],
                )
                for n in range(1, blocks)
            ],
            keys,
        )
        diag[h, 0:GROUP] = jnp.zeros((GROUP, BLOCK), f32)
        return carry

    if early:
        lax.fori_loop(0, upper, one, 0)
        return
    lax.fori_loop(upper, key_ref.shape[0], one, 0)
    for h in range(key_ref.shape[0]):
        invert_groups(diag.at[h], sol_ref.at[h], blocks)


def first_kernel(
    index_ref, key_ref, value_ref, halo_ref, ck_ref, cv_ref, rates_ref,
    kv_ref, kb_ref, low_ref, sol_ref, rows, diag, keys,
):
    heads = key_ref.shape[0]
    dim = rows.shape[3]
    for h in range(heads):
        halo = own_halo(index_ref, halo_ref[h])
        for i, ref in enumerate((key_ref, value_ref)):
            for j in range(2):
                at = (1 + 2 * i + j) * dim
                fill_rows(
                    rows.at[h, 2 * i + j],
                    halo[:, at : at + dim],
                    ref[h, :HALF, j * dim : (j + 1) * dim],
                )
    block_inputs(
        [
            (
                [rows.at[h, i] for i in range(4)], ck_ref[h], cv_ref[h], 0, rates_ref[h][0:1],
                kv_ref.at[h], kb_ref.at[h], low_ref.at[h], diag.at[h * GROUP : (h + 1) * GROUP],
            )
            for h in range(heads)
        ],
        keys,
    )
    invert_groups(diag, sol_ref, heads)


def own_halo(index_ref, halo):
    return jnp.where(index_ref[0] == 0, 0.0, halo.astype(f32))


def maps_kernel(
    kept, start, half, index_ref, kv_ref, kb_ref, low_ref, sol_ref,
    kv0_ref, kb0_ref, low0_ref, sol0_ref,
    inv_ref, p_ref, s_ref, total_ref, move, written,
):
    count, blocks = inv_ref.shape[:2]
    dim = total_ref.shape[1]
    slots = range(count)
    first = first_head(index_ref, kept, half) + start
    row, col, lane = block_masks()
    eye = (row == col).astype(f32)

    def at(inner, first_one, h, n):
        return first_one[first + h] if n == 0 else inner[first + h, n - 1]

    for h in slots:
        for n in range(blocks):
            if n == 0:
                base = sol0_ref[pl.ds((first + h) * GROUP, GROUP), :]
            else:
                base = sol_ref[first + h, n * GROUP : (n + 1) * GROUP, :]
            inv_ref[h, n] = split(
                jnp.concatenate(
                    [jnp.where(lane // GROUP == g, base, 0.0) for g in range(BLOCK // GROUP)], 0
                )
            )

    lane_h = lax.broadcasted_iota(jnp.int32, (HALF, BLOCK), 1)
    row_h = lax.broadcasted_iota(jnp.int32, (HALF, BLOCK), 0)
    size = GROUP
    while size < BLOCK:
        keep = lane_h // size == 2 * (row_h // size)
        starts = range(size, BLOCK, 2 * size)
        for h in slots:
            for n in range(blocks):
                inv = inv_ref[h, n]
                lower = at(low_ref, low0_ref, h, n)
                low = jnp.concatenate([lower[a : a + size] for a in starts], 0)
                z = split(mm(split(jnp.where(keep, low, 0.0)), inv))
                twice = []
                for i in range(len(starts)):
                    twice += [z[i * size : (i + 1) * size]] * 2
                odd = jnp.concatenate([inv[a : a + size] for a in starts], 0)
                new = mm(odd, jnp.concatenate(twice, 0))
                new = split(odd[:, :BLOCK].astype(f32) + odd[:, BLOCK:].astype(f32) - new)
                for i, a in enumerate(starts):
                    inv_ref[h, n, a : a + size] = new[i * size : (i + 1) * size]
        size *= 2

    for h in slots:
        for n in range(blocks):
            move[h, n] = split(mm(at(kb_ref, kb0_ref, h, n), inv_ref[h, n]))
    for h in slots:
        for n in range(blocks):
            both = at(kv_ref, kv0_ref, h, n)
            solved = move[h, n]
            written[h, n] = split(mm(solved, both[:, 2 * dim :]))
            move[h, n] = split(eye - mm(solved, both[:, : 2 * dim]))

    span = {(h, n, n + 1): (move[h, n], written[h, n]) for h in slots for n in range(blocks)}

    def run(h, i, mid, j):
        later, earlier = span[h, mid, j], span[h, i, mid]
        state = later[1]
        added = state[:, :dim].astype(f32) + state[:, dim:].astype(f32)
        full = (mm(later[0], earlier[0]), mm(later[0], earlier[1]) + added)
        if (i, j) == (0, blocks):
            total_ref[h, :, :dim], total_ref[h, :, dim:] = full
        span[h, i, j] = tuple(split(x) for x in full)

    size = 2
    while size <= blocks:
        for i in range(0, blocks, size):
            for j in range(i + size // 2 + 1, i + size + 1):
                for h in slots:
                    run(h, i, i + size // 2, j)
        size *= 2
    for h in slots:
        p_ref[h, 0] = split(eye)
        s_ref[h, 0] = jnp.zeros((dim, 2 * dim), bf16)
        for n in range(1, blocks):
            p_ref[h, n], s_ref[h, n] = span[h, 0, n]


def reads_kernel(
    kept, slot, at, half, index_ref, query_ref, halo_ref, cq_ref, kv_ref, kb_ref, kv0_ref, kb0_ref,
    inv_ref, p_ref, s_ref, pulled_ref, local_ref, q0, query, scores, pulled,
):
    head = first_head(index_ref, kept, half) + at
    dim = q0.shape[1]
    blocks = inv_ref.shape[1]
    fill_rows(q0, own_halo(index_ref, halo_ref[head])[:, :dim], query_ref[head])
    cq = cq_ref[head]
    row = lax.broadcasted_iota(jnp.int32, (HALF, BLOCK), 0)
    col = lax.broadcasted_iota(jnp.int32, (HALF, BLOCK), 1)
    causal = step_time(col) <= 2 * row + 1
    rows = [slice(n * HALF, (n + 1) * HALF) for n in range(blocks)]
    for n in range(blocks):
        q = conv_taps(q0, cq, n * HALF, HALF)
        query[rows[n]] = q
        kbs = kb0_ref[head] if n == 0 else kb_ref[head, n - 1]
        scores[rows[n]] = split(jnp.where(causal, mm(split(q), kbs), 0.0))
    for n in range(blocks):
        scores[rows[n]] = split(mm(scores[rows[n]], inv_ref[slot, n]))
    for n in range(blocks):
        both = kv0_ref[head] if n == 0 else kv_ref[head, n - 1]
        pulled[rows[n]] = split(query[rows[n]] - mm(scores[rows[n]], both[:, : 2 * dim]))
        local_ref[rows[n]] = mm(scores[rows[n]], both[:, 2 * dim :])
    for n in range(blocks):
        local_ref[rows[n]] += mm(pulled[rows[n]], s_ref[slot, n])
        pulled_ref[rows[n]] = split(mm(pulled[rows[n]], p_ref[slot, n]))


def out_kernel(kept, half, index_ref, gain_ref, *rest):
    out_ref = rest[-1]
    first = first_head(index_ref, kept, half)
    for i in range(half):
        state_ref, pulled_ref, local_ref = rest[3 * i : 3 * i + 3]
        state = split(state_ref[0])
        gain = pick_row(gain_ref[...], first + i)
        for at in range(0, pulled_ref.shape[0], BLOCK):
            rows = slice(at, at + BLOCK)
            raw = mm(pulled_ref[rows], state) + local_ref[rows]
            mean = jnp.mean(raw * raw, 1, keepdims=True)
            out_ref[i, rows] = raw * lax.rsqrt(mean + 1e-06) * gain


def then(later, earlier):
    dim = later.shape[0]
    prod = mm(split(later[:, :dim]), split(earlier))
    wide = prod.shape[1]
    if wide == dim:
        return prod + later[:, dim:]
    return jnp.concatenate([prod[:, :dim], prod[:, dim:] + later[:, dim:]], 1)


def pair_kernel(slot, index_ref, mine_ref, got_ref, total_ref, earlier_ref):
    upper = (index_ref[0] & 1) != 0
    for h in range(mine_ref.shape[0]):
        mine = mine_ref[h]
        got = got_ref[slot + h]
        earlier = jnp.where(upper, got, mine)
        earlier_ref[h] = earlier
        total_ref[h] = then(jnp.where(upper, mine, got), earlier)


def join_kernel(bits, index_ref, *refs):
    size = 1 << len(bits)
    got_refs, before_ref, (total_ref, after_ref) = refs[:size], refs[size:-2], refs[-2:]
    ups = [(index_ref[0] & bit) != 0 for bit in bits]
    dim = got_refs[0].shape[1]
    row = lax.broadcasted_iota(jnp.int32, (dim, 2 * dim), 0)
    col = lax.broadcasted_iota(jnp.int32, (dim, 2 * dim), 1)
    for h in range(got_refs[0].shape[0]):
        maps = [ref[h] for ref in got_refs]
        for i, up in enumerate(ups):
            maps = [jnp.where(up, maps[j ^ (1 << i)], maps[j]) for j in range(size)]
        part = slice(dim, None) if total_ref.shape[2] == dim else slice(None)
        identity = (row == col).astype(f32)
        if size == 2:
            total_ref[h] = then(maps[1], maps[0][:, part])
            prefix = jnp.where(ups[0], maps[0], identity)
        else:
            low = then(maps[1], maps[0])
            total_ref[h] = then(then(maps[3], maps[2]), low[:, part])
            prefix = jnp.where(
                ups[1],
                jnp.where(ups[0], then(maps[2], low), low),
                jnp.where(ups[0], maps[0], identity),
            )
        after_ref[h] = then(before_ref[0][h], prefix) if before_ref else prefix


def down_kernel(bit, index_ref, before_ref, got_ref, earlier_ref, mine_ref, other_ref):
    upper = (index_ref[0] & 1) != 0
    got = jnp.where((index_ref[0] & bit) != 0, got_ref[0], 0.0)
    state = then(before_ref[0], got)
    after = then(earlier_ref[0], state)
    mine_ref[0] = jnp.where(upper, after, state)
    other_ref[0] = jnp.where(upper, state, after)


def tails_kernel(index_ref, query_ref, key_ref, value_ref, out_ref):
    rim = out_ref.shape[1]
    at = 0
    for ref in (query_ref, key_ref, value_ref):
        wide = ref.shape[2]
        out_ref[:, :, at : at + wide] = ref[:, ref.shape[1] - rim :, :]
        at += wide


def shape(dims, dtype):
    return jax.ShapeDtypeStruct(dims, dtype)


def resident(kernel, index, args, outs, scratch=(), limit=4 << 20, aliases={}):
    smem = pl.BlockSpec(memory_space=pltpu.SMEM)
    vmem = pl.BlockSpec(memory_space=pltpu.VMEM)
    return pl.pallas_call(
        kernel,
        in_specs=[smem] + [vmem] * len(args),
        out_specs=[vmem] * len(outs),
        out_shape=[pltpu.VMEM(o.shape, o.dtype) for o in outs],
        scratch_shapes=list(scratch),
        input_output_aliases=aliases,
        compiler_params=pltpu.CompilerParams(vmem_limit_bytes=limit),
    )(index, *[pltpu.with_memory_space_constraint(a, pltpu.VMEM) for a in args])


def swap(x, bit, count):
    return lax.ppermute(x, "seq", [(i, i ^ bit) for i in range(count)])


def per_device(
    queries, key_pairs, value_pairs, write_rates, conv_query, conv_key, conv_value, out_gain
):
    heads, tokens, dim = queries.shape
    blocks = tokens // HALF
    half = heads // 2
    rim = conv_query.shape[1] - 1
    count = lax.axis_size("seq")
    index = lax.axis_index("seq").reshape(1)

    parts = (queries, key_pairs, value_pairs)
    last = [
        pl.BlockSpec((heads, 16, x.shape[2]), lambda i, index_ref: (0, tokens // 16 - 1, 0))
        for x in parts
    ]
    tails = pl.pallas_call(
        tails_kernel,
        grid_spec=pltpu.PrefetchScalarGridSpec(
            num_scalar_prefetch=1,
            grid=(1,),
            in_specs=last,
            out_specs=pl.BlockSpec((heads, rim, 5 * dim), lambda i, index_ref: (0, 0, 0)),
        ),
        out_shape=shape((heads, rim, 5 * dim), bf16),
        compiler_params=pltpu.CompilerParams(vmem_limit_bytes=4 << 20),
    )(index, *[pltpu.with_memory_space_constraint(x, pltpu.HBM) for x in parts])
    def in_order(*after):
        return lax.optimization_barrier((index, after))[0]

    inner = (heads, blocks - 1, BLOCK)
    front_args = (key_pairs, value_pairs, write_rates, conv_key, conv_value)
    front_outs = [
        shape(inner + (4 * dim,), bf16),
        shape(inner + (2 * dim,), bf16),
        shape(inner + (BLOCK,), f32),
        shape((heads, blocks * GROUP, BLOCK), f32),
        shape((heads, blocks, BLOCK), f32),
    ]
    front_scratch = [
        pltpu.VMEM((4, tokens + 8, dim), f32),
        pltpu.VMEM((blocks, BLOCK), f32),
        pltpu.VMEM((blocks - 1, BLOCK, dim), f32),
    ]
    front = resident(
        functools.partial(front_kernel, True),
        in_order(tails),
        front_args,
        front_outs,
        front_scratch,
        LIMIT,
    )
    tails = lax.optimization_barrier((tails, front[-1]))[0]
    halo = lax.ppermute(tails, "seq", [(i, (i + 1) % count) for i in range(count)])
    kv, kb, low, _, rates, sol = resident(
        functools.partial(front_kernel, False),
        in_order(tails),
        (*front_args, *front),
        front_outs + front_outs[3:4],
        front_scratch,
        LIMIT,
        {1 + len(front_args) + i: i for i in range(5)},
    )
    front = (kv, kb, low, sol)
    halo = lax.optimization_barrier((halo, rates))[0]
    opening = resident(
        first_kernel,
        in_order(rates),
        (key_pairs, value_pairs, halo, conv_key, conv_value, rates),
        [
            shape((heads, BLOCK, 4 * dim), bf16),
            shape((heads, BLOCK, 2 * dim), bf16),
            shape((heads, BLOCK, BLOCK), f32),
            shape((heads * GROUP, BLOCK), f32),
        ],
        [
            pltpu.VMEM((heads, 4, HALF + 8, dim), f32),
            pltpu.VMEM((heads * GROUP, BLOCK), f32),
            pltpu.VMEM((heads, BLOCK, dim), f32),
        ],
        LIMIT,
    )

    def maps(kept, start, size, *after):
        wide = shape((size, blocks, BLOCK, 2 * dim), bf16)
        return resident(
            functools.partial(maps_kernel, kept, start, half),
            in_order(*after),
            (*front, *opening),
            [wide] * 3 + [shape((size, dim, 2 * dim), f32)],
            [pltpu.VMEM((size, blocks, dim, 2 * dim), bf16)] * 2,
            LIMIT,
        )

    def reads(kept, at, *after):
        slot, saved = (0, kept_saved[at]) if kept else (at, sent_saved)
        return resident(
            functools.partial(reads_kernel, kept, slot, at, half),
            in_order(*after),
            (queries, halo, conv_query, *front[:2], *opening[:2], *saved),
            [shape((tokens, 2 * dim), bf16), shape((tokens, dim), f32)],
            [
                pltpu.VMEM((tokens + 8, dim), f32),
                pltpu.VMEM((tokens, dim), f32),
                pltpu.VMEM((tokens, 2 * dim), bf16),
                pltpu.VMEM((tokens, 2 * dim), bf16),
            ],
            LIMIT,
        )

    total_shape = shape((1, dim, 2 * dim), f32)
    state_shape = shape((1, dim, dim), f32)
    bits = []
    while 2 << len(bits) < count:
        bits.append(2 << len(bits))
    chains = {}

    def begin(at, got, *after):
        total, earlier = resident(
            functools.partial(pair_kernel, at),
            in_order(*after),
            (kept_total[at], got),
            [total_shape] * 2,
        )
        chains[at] = dict(current=total, earlier=earlier, before=(), left=[(bit,) for bit in bits[:-1]])
        send(at)
        return total

    def send(at):
        chain = chains[at]
        now = chain["left"][0] if chain["left"] else bits[-1:]
        flips = [sum(b for i, b in enumerate(now) if j >> i & 1) for j in range(1 << len(now))]
        chain["got"] = [swap(chain["current"], flip, count) for flip in flips[1:]]

    def join(at, *after):
        chain = chains[at]
        now = chain["left"].pop(0)
        got = lax.optimization_barrier((chain["got"], after))[0]
        chain["current"], before = resident(
            functools.partial(join_kernel, now),
            index,
            (chain["current"], *got, *chain["before"]),
            [total_shape if chain["left"] else state_shape, total_shape],
        )
        chain["before"] = (before,)
        send(at)
        return chain["current"]

    def down(at, *after):
        chain = chains[at]
        got = lax.optimization_barrier((chain["got"], after))[0][0]
        return resident(
            functools.partial(down_kernel, bits[-1]),
            index,
            (*chain["before"], got, chain["earlier"]),
            [state_shape] * 2,
        )

    out_shape = shape((heads, tokens, dim), f32)
    done = ()

    def finish(kept, states, *after):
        nonlocal done
        vmem = pl.BlockSpec(memory_space=pltpu.VMEM)

        def out_block(i, index_ref):
            upper = index_ref[0] & 1
            return (upper if kept else 1 - upper, 0, 0)

        args = [out_gain]
        for i, state in enumerate(states):
            args += [state, *read[kept, i]]
        args = [pltpu.with_memory_space_constraint(a, pltpu.VMEM) for a in args]

        def kernel(index_ref, *refs):
            out_kernel(kept, half, index_ref, *refs[: len(args)], refs[-1])

        out = pl.pallas_call(
            kernel,
            grid_spec=pltpu.PrefetchScalarGridSpec(
                num_scalar_prefetch=1,
                grid=(1,),
                in_specs=[vmem] * len(args) + [pl.BlockSpec(memory_space=pl.ANY)] * len(done),
                out_specs=pl.BlockSpec((half, tokens, dim), out_block),
            ),
            out_shape=out_shape,
            input_output_aliases={len(args) + 1: 0} if done else {},
            compiler_params=pltpu.CompilerParams(vmem_limit_bytes=LIMIT),
        )(in_order(*after), *args, *done)
        done = (out,)
        return out

    kept_saved, kept_total, read = {}, {}, {}

    def keep(at, *after):
        *kept_saved[at], kept_total[at] = maps(True, at, 1, *after)

    *sent_saved, sent_total = maps(False, 0, half)
    got = swap(sent_total, 1, count)
    keep(0, sent_total)
    step = begin(0, got)
    for at in range(1, half):
        keep(at, step)
        step = begin(at, got, kept_total[at])
    step = (step,)
    todo = [(kept, at) for at in range(half) for kept in (False, True)]

    def read_some(pieces, *after):
        for _ in range(min(pieces, len(todo))):
            kept, at = todo.pop(0)
            read[kept, at] = reads(kept, at, *after)
            after = tuple(read[kept, at])
        return after

    while any(chain["left"] for chain in chains.values()):
        for at in range(half):
            if chains[at]["left"]:
                step = (join(at, *step),)
                if len(todo) > half:
                    step = read_some(1, *step)
    step = read_some(len(todo), *step)
    mine, other = {}, {}
    for at in range(half):
        mine[at], other[at] = down(at, *step)
        step = (mine[at],)
    others = swap(jnp.concatenate([other[at] for at in range(half)], 0), 1, count)
    last = finish(True, [mine[at] for at in range(half)])
    others = lax.optimization_barrier((others, last))[0]
    return finish(False, [others[at : at + 1] for at in range(half)])


def solution(mesh):
    return jax.shard_map(
        per_device,
        mesh=mesh,
        in_specs=(
            P(None, ("grp", "seq"), None),
            P(None, ("grp", "seq"), None),
            P(None, ("grp", "seq"), None),
            P(None, ("grp", "seq")),
            P(),
            P(),
            P(),
            P(),
        ),
        out_specs=P(None, ("grp", "seq"), None),
        check_vma=False,
    )
```

```python
import functools

import jax
import jax.numpy as jnp
from jax import lax
from jax.experimental import pallas as pl
from jax.experimental.pallas import tpu as pltpu
from jax.sharding import PartitionSpec as P

BLOCK = 128
GROUP = 16
HALF = BLOCK // 2
LIMIT = 20 << 20

f32 = jnp.float32
bf16 = jnp.bfloat16


def split(x):
    high = x.astype(bf16)
    low = (x - high.astype(f32)).astype(bf16)
    return jnp.concatenate([high, low], 1)


def mm(a, b):
    n = b.shape[1] // 2
    m, k = a.shape[0], b.shape[0]
    if m <= HALF:
        p = jnp.dot(
            jnp.concatenate([a[:, :k], a[:, k:]], 0), b, preferred_element_type=f32
        )
        p = p[:m] + p[m:]
        return p[:, :n] + p[:, n:]
    p = jnp.dot(a, jnp.concatenate([b, b], 0), preferred_element_type=f32)
    return p[:, :n] + p[:, n:]


def pick_row(x, r):
    row = lax.broadcasted_iota(jnp.int32, x.shape, 0)
    return jnp.sum(jnp.where(row == r, x, 0.0), 0, keepdims=True)


def silu(x):
    return x / (1.0 + jnp.exp(-x))


def step_time(r):
    return (r // GROUP) * GROUP + 2 * (r % 8) + (r // 8) % 2


def interleave(a, b):
    parts = []
    for g in range(0, a.shape[0], 8):
        parts += [a[g : g + 8], b[g : g + 8]]
    return jnp.concatenate(parts, 0)


def conv_taps(ref, weights, start, count):
    taps = weights.shape[0]
    total = weights[0:1] * ref[pl.ds(start + 9 - taps, count), :]
    for s in range(1, taps):
        total = total + weights[s : s + 1] * ref[pl.ds(start + 9 - taps + s, count), :]
    return silu(total)


def fill_rows(ref, halo, rows):
    rim = halo.shape[0]
    ref[8 - rim : 8, :] = halo.astype(f32)
    ref[8:, :] = rows.astype(f32)


def first_head(index_ref, kept, half):
    upper = index_ref[0] & 1
    return (upper if kept else 1 - upper) * half


def block_masks():
    row = lax.broadcasted_iota(jnp.int32, (BLOCK, BLOCK), 0)
    col = lax.broadcasted_iota(jnp.int32, (BLOCK, BLOCK), 1)
    lane = lax.broadcasted_iota(jnp.int32, (GROUP, BLOCK), 1)
    return row, col, lane


def block_inputs(units, keys):
    row, col, lane = block_masks()
    strict = step_time(col) < step_time(row)
    for i, (rows, ck, cv, t0, rates, kv, kb, low, diag) in enumerate(units):
        dim = rows[0].shape[1]
        taps = [w[:, j * dim : (j + 1) * dim] for w in (ck, cv) for j in range(2)]
        ka, kb_, va, vb = [conv_taps(r, w, t0, HALF) for r, w in zip(rows, taps)]
        k = interleave(ka, kb_)
        k = k * lax.rsqrt(jnp.sum(k * k, 1, keepdims=True) + 1e-06)
        keys[i] = k
        kv[:, : 2 * dim] = split(k)
        kv[:, 2 * dim :] = split(interleave(va, vb))
    for i, (rows, ck, cv, t0, rates, kv, kb, low, diag) in enumerate(units):
        kb[...] = split(keys[i].T * rates)
    for i, (rows, ck, cv, t0, rates, kv, kb, low, diag) in enumerate(units):
        lower = jnp.where(strict, mm(kv[:, : kb.shape[1]], kb[...]), 0.0)
        low[...] = lower
        groups = jnp.zeros((GROUP, BLOCK), f32)
        for g in range(BLOCK // GROUP):
            groups = jnp.where(lane // GROUP == g, lower[g * GROUP : (g + 1) * GROUP], groups)
        diag[...] = groups


def invert_groups(diag, out, blocks):
    lane = lax.broadcasted_iota(jnp.int32, (blocks, BLOCK), 1)
    times = [t // 2 + 8 * (t % 2) for t in range(GROUP)]
    coef = [diag[pl.ds(r, blocks, stride=GROUP), :] for r in range(GROUP)]
    sol = [(lane % GROUP == r).astype(f32) for r in range(GROUP)]
    for i, s in enumerate(times):
        pick = (lane // GROUP) * GROUP + s
        for r in times[i + 1 :]:
            sol[r] = sol[r] - jnp.take_along_axis(coef[r], pick, axis=1) * sol[s]
    for r in range(GROUP):
        out[pl.ds(r, blocks, stride=GROUP), :] = sol[r]


def front_kernel(
    early, index_ref, key_ref, value_ref, rate_ref, ck_ref, cv_ref, *refs
):
    if early:
        kv_ref, kb_ref, low_ref, diag, rates_ref, rows, brow, keys = refs
    else:
        kv_ref, kb_ref, low_ref, diag, rates_ref, sol_ref, rows, brow, keys = refs[5:]
    upper = index_ref[0] & 1
    dim = rows.shape[2]
    blocks = rates_ref.shape[1]
    row, col, _ = block_masks()
    order = (row == step_time(col)).astype(f32)

    def one(h, carry):
        for i, ref in enumerate((key_ref, value_ref)):
            for j in range(2):
                rows[2 * i + j, 8:, :] = ref[h, :, j * dim : (j + 1) * dim].astype(f32)
        for n in range(blocks):
            brow[n : n + 1, :] = pick_row(rate_ref[:, n * BLOCK : (n + 1) * BLOCK], h)
        rates = jnp.dot(
            brow[...], order, precision=lax.Precision.HIGHEST, preferred_element_type=f32
        )
        rates_ref[h] = rates
        ck, cv = ck_ref[h], cv_ref[h]
        block_inputs(
            [
                (
                    [rows.at[i] for i in range(4)], ck, cv, n * HALF, rates[n : n + 1],
                    kv_ref.at[h, n - 1], kb_ref.at[h, n - 1], low_ref.at[h, n - 1],
                    diag.at[h, n * GROUP : (n + 1) * GROUP],
                )
                for n in range(1, blocks)
            ],
            keys,
        )
        diag[h, 0:GROUP] = jnp.zeros((GROUP, BLOCK), f32)
        return carry

    if early:
        lax.fori_loop(0, upper, one, 0)
        return
    lax.fori_loop(upper, key_ref.shape[0], one, 0)
    for h in range(key_ref.shape[0]):
        invert_groups(diag.at[h], sol_ref.at[h], blocks)


def first_kernel(
    index_ref, key_ref, value_ref, halo_ref, ck_ref, cv_ref, rates_ref,
    kv_ref, kb_ref, low_ref, sol_ref, rows, diag, keys,
):
    heads = key_ref.shape[0]
    dim = rows.shape[3]
    for h in range(heads):
        halo = own_halo(index_ref, halo_ref[h])
        for i, ref in enumerate((key_ref, value_ref)):
            for j in range(2):
                at = (1 + 2 * i + j) * dim
                fill_rows(
                    rows.at[h, 2 * i + j],
                    halo[:, at : at + dim],
                    ref[h, :HALF, j * dim : (j + 1) * dim],
                )
    block_inputs(
        [
            (
                [rows.at[h, i] for i in range(4)], ck_ref[h], cv_ref[h], 0, rates_ref[h][0:1],
                kv_ref.at[h], kb_ref.at[h], low_ref.at[h], diag.at[h * GROUP : (h + 1) * GROUP],
            )
            for h in range(heads)
        ],
        keys,
    )
    invert_groups(diag, sol_ref, heads)


def own_halo(index_ref, halo):
    return jnp.where(index_ref[0] == 0, 0.0, halo.astype(f32))


def maps_kernel(
    kept, start, half, index_ref, kv_ref, kb_ref, low_ref, sol_ref,
    kv0_ref, kb0_ref, low0_ref, sol0_ref,
    inv_ref, p_ref, s_ref, total_ref, move, written,
):
    count, blocks = inv_ref.shape[:2]
    dim = total_ref.shape[1]
    slots = range(count)
    first = first_head(index_ref, kept, half) + start
    row, col, lane = block_masks()
    eye = (row == col).astype(f32)

    def at(inner, first_one, h, n):
        return first_one[first + h] if n == 0 else inner[first + h, n - 1]

    for h in slots:
        for n in range(blocks):
            if n == 0:
                base = sol0_ref[pl.ds((first + h) * GROUP, GROUP), :]
            else:
                base = sol_ref[first + h, n * GROUP : (n + 1) * GROUP, :]
            inv_ref[h, n] = split(
                jnp.concatenate(
                    [jnp.where(lane // GROUP == g, base, 0.0) for g in range(BLOCK // GROUP)], 0
                )
            )

    lane_h = lax.broadcasted_iota(jnp.int32, (HALF, BLOCK), 1)
    row_h = lax.broadcasted_iota(jnp.int32, (HALF, BLOCK), 0)
    size = GROUP
    while size < BLOCK:
        keep = lane_h // size == 2 * (row_h // size)
        starts = range(size, BLOCK, 2 * size)
        for h in slots:
            for n in range(blocks):
                inv = inv_ref[h, n]
                lower = at(low_ref, low0_ref, h, n)
                low = jnp.concatenate([lower[a : a + size] for a in starts], 0)
                z = split(mm(split(jnp.where(keep, low, 0.0)), inv))
                twice = []
                for i in range(len(starts)):
                    twice += [z[i * size : (i + 1) * size]] * 2
                odd = jnp.concatenate([inv[a : a + size] for a in starts], 0)
                new = mm(odd, jnp.concatenate(twice, 0))
                new = split(odd[:, :BLOCK].astype(f32) + odd[:, BLOCK:].astype(f32) - new)
                for i, a in enumerate(starts):
                    inv_ref[h, n, a : a + size] = new[i * size : (i + 1) * size]
        size *= 2

    for h in slots:
        for n in range(blocks):
            move[h, n] = split(mm(at(kb_ref, kb0_ref, h, n), inv_ref[h, n]))
    for h in slots:
        for n in range(blocks):
            both = at(kv_ref, kv0_ref, h, n)
            solved = move[h, n]
            written[h, n] = split(mm(solved, both[:, 2 * dim :]))
            move[h, n] = split(eye - mm(solved, both[:, : 2 * dim]))

    span = {(h, n, n + 1): (move[h, n], written[h, n]) for h in slots for n in range(blocks)}

    def run(h, i, mid, j):
        later, earlier = span[h, mid, j], span[h, i, mid]
        state = later[1]
        added = state[:, :dim].astype(f32) + state[:, dim:].astype(f32)
        full = (mm(later[0], earlier[0]), mm(later[0], earlier[1]) + added)
        if (i, j) == (0, blocks):
            total_ref[h, :, :dim], total_ref[h, :, dim:] = full
        span[h, i, j] = tuple(split(x) for x in full)

    size = 2
    while size <= blocks:
        for i in range(0, blocks, size):
            for j in range(i + size // 2 + 1, i + size + 1):
                for h in slots:
                    run(h, i, i + size // 2, j)
        size *= 2
    for h in slots:
        p_ref[h, 0] = split(eye)
        s_ref[h, 0] = jnp.zeros((dim, 2 * dim), bf16)
        for n in range(1, blocks):
            p_ref[h, n], s_ref[h, n] = span[h, 0, n]


def reads_kernel(
    kept, slot, at, half, index_ref, query_ref, halo_ref, cq_ref, kv_ref, kb_ref, kv0_ref, kb0_ref,
    inv_ref, p_ref, s_ref, pulled_ref, local_ref, q0, query, scores, pulled,
):
    head = first_head(index_ref, kept, half) + at
    dim = q0.shape[1]
    blocks = inv_ref.shape[1]
    fill_rows(q0, own_halo(index_ref, halo_ref[head])[:, :dim], query_ref[head])
    cq = cq_ref[head]
    row = lax.broadcasted_iota(jnp.int32, (HALF, BLOCK), 0)
    col = lax.broadcasted_iota(jnp.int32, (HALF, BLOCK), 1)
    causal = step_time(col) <= 2 * row + 1
    rows = [slice(n * HALF, (n + 1) * HALF) for n in range(blocks)]
    for n in range(blocks):
        q = conv_taps(q0, cq, n * HALF, HALF)
        query[rows[n]] = q
        kbs = kb0_ref[head] if n == 0 else kb_ref[head, n - 1]
        scores[rows[n]] = split(jnp.where(causal, mm(split(q), kbs), 0.0))
    for n in range(blocks):
        scores[rows[n]] = split(mm(scores[rows[n]], inv_ref[slot, n]))
    for n in range(blocks):
        both = kv0_ref[head] if n == 0 else kv_ref[head, n - 1]
        pulled[rows[n]] = split(query[rows[n]] - mm(scores[rows[n]], both[:, : 2 * dim]))
        local_ref[rows[n]] = mm(scores[rows[n]], both[:, 2 * dim :])
    for n in range(blocks):
        local_ref[rows[n]] += mm(pulled[rows[n]], s_ref[slot, n])
        pulled_ref[rows[n]] = split(mm(pulled[rows[n]], p_ref[slot, n]))


def out_kernel(kept, half, index_ref, gain_ref, *rest):
    out_ref = rest[-1]
    first = first_head(index_ref, kept, half)
    for i in range(half):
        state_ref, pulled_ref, local_ref = rest[3 * i : 3 * i + 3]
        state = split(state_ref[0])
        gain = pick_row(gain_ref[...], first + i)
        for at in range(0, pulled_ref.shape[0], BLOCK):
            rows = slice(at, at + BLOCK)
            raw = mm(pulled_ref[rows], state) + local_ref[rows]
            mean = jnp.mean(raw * raw, 1, keepdims=True)
            out_ref[i, rows] = raw * lax.rsqrt(mean + 1e-06) * gain


def then(later, earlier):
    dim = later.shape[0]
    prod = mm(split(later[:, :dim]), split(earlier))
    wide = prod.shape[1]
    if wide == dim:
        return prod + later[:, dim:]
    return jnp.concatenate([prod[:, :dim], prod[:, dim:] + later[:, dim:]], 1)


def pair_kernel(slot, index_ref, mine_ref, got_ref, total_ref, earlier_ref):
    upper = (index_ref[0] & 1) != 0
    for h in range(mine_ref.shape[0]):
        mine = mine_ref[h]
        got = got_ref[slot + h]
        earlier = jnp.where(upper, got, mine)
        earlier_ref[h] = earlier
        total_ref[h] = then(jnp.where(upper, mine, got), earlier)


def join_kernel(bits, index_ref, *refs):
    size = 1 << len(bits)
    got_refs, before_ref, (total_ref, after_ref) = refs[:size], refs[size:-2], refs[-2:]
    ups = [(index_ref[0] & bit) != 0 for bit in bits]
    dim = got_refs[0].shape[1]
    row = lax.broadcasted_iota(jnp.int32, (dim, 2 * dim), 0)
    col = lax.broadcasted_iota(jnp.int32, (dim, 2 * dim), 1)
    for h in range(got_refs[0].shape[0]):
        maps = [ref[h] for ref in got_refs]
        for i, up in enumerate(ups):
            maps = [jnp.where(up, maps[j ^ (1 << i)], maps[j]) for j in range(size)]
        part = slice(dim, None) if total_ref.shape[2] == dim else slice(None)
        identity = (row == col).astype(f32)
        if size == 2:
            total_ref[h] = then(maps[1], maps[0][:, part])
            prefix = jnp.where(ups[0], maps[0], identity)
        else:
            low = then(maps[1], maps[0])
            total_ref[h] = then(then(maps[3], maps[2]), low[:, part])
            prefix = jnp.where(
                ups[1],
                jnp.where(ups[0], then(maps[2], low), low),
                jnp.where(ups[0], maps[0], identity),
            )
        after_ref[h] = then(before_ref[0][h], prefix) if before_ref else prefix


def down_kernel(bit, index_ref, before_ref, got_ref, earlier_ref, mine_ref, other_ref):
    upper = (index_ref[0] & 1) != 0
    got = jnp.where((index_ref[0] & bit) != 0, got_ref[0], 0.0)
    state = then(before_ref[0], got)
    after = then(earlier_ref[0], state)
    mine_ref[0] = jnp.where(upper, after, state)
    other_ref[0] = jnp.where(upper, state, after)


def tails_kernel(index_ref, query_ref, key_ref, value_ref, out_ref):
    rim = out_ref.shape[1]
    at = 0
    for ref in (query_ref, key_ref, value_ref):
        wide = ref.shape[2]
        out_ref[:, :, at : at + wide] = ref[:, ref.shape[1] - rim :, :]
        at += wide


def shape(dims, dtype):
    return jax.ShapeDtypeStruct(dims, dtype)


def resident(kernel, index, args, outs, scratch=(), limit=4 << 20, aliases={}):
    smem = pl.BlockSpec(memory_space=pltpu.SMEM)
    vmem = pl.BlockSpec(memory_space=pltpu.VMEM)
    return pl.pallas_call(
        kernel,
        in_specs=[smem] + [vmem] * len(args),
        out_specs=[vmem] * len(outs),
        out_shape=[pltpu.VMEM(o.shape, o.dtype) for o in outs],
        scratch_shapes=list(scratch),
        input_output_aliases=aliases,
        compiler_params=pltpu.CompilerParams(vmem_limit_bytes=limit),
    )(index, *[pltpu.with_memory_space_constraint(a, pltpu.VMEM) for a in args])


def swap(x, bit, count):
    return lax.ppermute(x, "seq", [(i, i ^ bit) for i in range(count)])


def per_device(
    queries, key_pairs, value_pairs, write_rates, conv_query, conv_key, conv_value, out_gain
):
    heads, tokens, dim = queries.shape
    blocks = tokens // HALF
    half = heads // 2
    rim = conv_query.shape[1] - 1
    count = lax.axis_size("seq")
    index = lax.axis_index("seq").reshape(1)

    parts = (queries, key_pairs, value_pairs)
    last = [
        pl.BlockSpec((heads, 16, x.shape[2]), lambda i, index_ref: (0, tokens // 16 - 1, 0))
        for x in parts
    ]
    tails = pl.pallas_call(
        tails_kernel,
        grid_spec=pltpu.PrefetchScalarGridSpec(
            num_scalar_prefetch=1,
            grid=(1,),
            in_specs=last,
            out_specs=pl.BlockSpec((heads, rim, 5 * dim), lambda i, index_ref: (0, 0, 0)),
        ),
        out_shape=shape((heads, rim, 5 * dim), bf16),
        compiler_params=pltpu.CompilerParams(vmem_limit_bytes=4 << 20),
    )(index, *[pltpu.with_memory_space_constraint(x, pltpu.HBM) for x in parts])
    def in_order(*after):
        return lax.optimization_barrier((index, after))[0]

    inner = (heads, blocks - 1, BLOCK)
    front_args = (key_pairs, value_pairs, write_rates, conv_key, conv_value)
    front_outs = [
        shape(inner + (4 * dim,), bf16),
        shape(inner + (2 * dim,), bf16),
        shape(inner + (BLOCK,), f32),
        shape((heads, blocks * GROUP, BLOCK), f32),
        shape((heads, blocks, BLOCK), f32),
    ]
    front_scratch = [
        pltpu.VMEM((4, tokens + 8, dim), f32),
        pltpu.VMEM((blocks, BLOCK), f32),
        pltpu.VMEM((blocks - 1, BLOCK, dim), f32),
    ]
    front = resident(
        functools.partial(front_kernel, True),
        in_order(tails),
        front_args,
        front_outs,
        front_scratch,
        LIMIT,
    )
    tails = lax.optimization_barrier((tails, front[-1]))[0]
    halo = lax.ppermute(tails, "seq", [(i, (i + 1) % count) for i in range(count)])
    kv, kb, low, _, rates, sol = resident(
        functools.partial(front_kernel, False),
        in_order(tails),
        (*front_args, *front),
        front_outs + front_outs[3:4],
        front_scratch,
        LIMIT,
        {1 + len(front_args) + i: i for i in range(5)},
    )
    front = (kv, kb, low, sol)
    halo = lax.optimization_barrier((halo, rates))[0]
    opening = resident(
        first_kernel,
        in_order(rates),
        (key_pairs, value_pairs, halo, conv_key, conv_value, rates),
        [
            shape((heads, BLOCK, 4 * dim), bf16),
            shape((heads, BLOCK, 2 * dim), bf16),
            shape((heads, BLOCK, BLOCK), f32),
            shape((heads * GROUP, BLOCK), f32),
        ],
        [
            pltpu.VMEM((heads, 4, HALF + 8, dim), f32),
            pltpu.VMEM((heads * GROUP, BLOCK), f32),
            pltpu.VMEM((heads, BLOCK, dim), f32),
        ],
        LIMIT,
    )

    def maps(kept, start, size, *after):
        wide = shape((size, blocks, BLOCK, 2 * dim), bf16)
        return resident(
            functools.partial(maps_kernel, kept, start, half),
            in_order(*after),
            (*front, *opening),
            [wide] * 3 + [shape((size, dim, 2 * dim), f32)],
            [pltpu.VMEM((size, blocks, dim, 2 * dim), bf16)] * 2,
            LIMIT,
        )

    def reads(kept, at, *after):
        slot, saved = (0, kept_saved[at]) if kept else (at, sent_saved)
        return resident(
            functools.partial(reads_kernel, kept, slot, at, half),
            in_order(*after),
            (queries, halo, conv_query, *front[:2], *opening[:2], *saved),
            [shape((tokens, 2 * dim), bf16), shape((tokens, dim), f32)],
            [
                pltpu.VMEM((tokens + 8, dim), f32),
                pltpu.VMEM((tokens, dim), f32),
                pltpu.VMEM((tokens, 2 * dim), bf16),
                pltpu.VMEM((tokens, 2 * dim), bf16),
            ],
            LIMIT,
        )

    total_shape = shape((1, dim, 2 * dim), f32)
    state_shape = shape((1, dim, dim), f32)
    bits = []
    while 2 << len(bits) < count:
        bits.append(2 << len(bits))
    chains = {}

    def begin(at, got, *after):
        total, earlier = resident(
            functools.partial(pair_kernel, at),
            in_order(*after),
            (kept_total[at], got),
            [total_shape] * 2,
        )
        chains[at] = dict(current=total, earlier=earlier, before=(), left=[(bit,) for bit in bits[:-1]])
        send(at)
        return total

    def send(at):
        chain = chains[at]
        now = chain["left"][0] if chain["left"] else bits[-1:]
        flips = [sum(b for i, b in enumerate(now) if j >> i & 1) for j in range(1 << len(now))]
        chain["got"] = [swap(chain["current"], flip, count) for flip in flips[1:]]

    def join(at, *after):
        chain = chains[at]
        now = chain["left"].pop(0)
        got = lax.optimization_barrier((chain["got"], after))[0]
        chain["current"], before = resident(
            functools.partial(join_kernel, now),
            index,
            (chain["current"], *got, *chain["before"]),
            [total_shape if chain["left"] else state_shape, total_shape],
        )
        chain["before"] = (before,)
        send(at)
        return chain["current"]

    def down(at, *after):
        chain = chains[at]
        got = lax.optimization_barrier((chain["got"], after))[0][0]
        return resident(
            functools.partial(down_kernel, bits[-1]),
            index,
            (*chain["before"], got, chain["earlier"]),
            [state_shape] * 2,
        )

    out_shape = shape((heads, tokens, dim), f32)
    done = ()

    def finish(kept, states, *after):
        nonlocal done
        vmem = pl.BlockSpec(memory_space=pltpu.VMEM)

        def out_block(i, index_ref):
            upper = index_ref[0] & 1
            return (upper if kept else 1 - upper, 0, 0)

        args = [out_gain]
        for i, state in enumerate(states):
            args += [state, *read[kept, i]]
        args = [pltpu.with_memory_space_constraint(a, pltpu.VMEM) for a in args]

        def kernel(index_ref, *refs):
            out_kernel(kept, half, index_ref, *refs[: len(args)], refs[-1])

        out = pl.pallas_call(
            kernel,
            grid_spec=pltpu.PrefetchScalarGridSpec(
                num_scalar_prefetch=1,
                grid=(1,),
                in_specs=[vmem] * len(args) + [pl.BlockSpec(memory_space=pl.ANY)] * len(done),
                out_specs=pl.BlockSpec((half, tokens, dim), out_block),
            ),
            out_shape=out_shape,
            input_output_aliases={len(args) + 1: 0} if done else {},
            compiler_params=pltpu.CompilerParams(vmem_limit_bytes=LIMIT),
        )(in_order(*after), *args, *done)
        done = (out,)
        return out

    kept_saved, kept_total, read = {}, {}, {}

    def keep(at, *after):
        *kept_saved[at], kept_total[at] = maps(True, at, 1, *after)

    *sent_saved, sent_total = maps(False, 0, half)
    got = swap(sent_total, 1, count)
    keep(0, sent_total)
    step = begin(0, got)
    for at in range(1, half):
        keep(at, step)
        step = begin(at, got, kept_total[at])
    step = (step,)
    todo = [(kept, at) for at in range(half) for kept in (False, True)]

    def read_some(pieces, *after):
        for _ in range(min(pieces, len(todo))):
            kept, at = todo.pop(0)
            read[kept, at] = reads(kept, at, *after)
            after = tuple(read[kept, at])
        return after

    step = read_some(1, *step)
    while any(chain["left"] for chain in chains.values()):
        for at in range(half):
            if chains[at]["left"]:
                step = (join(at, *step),)
                if len(todo) > 1:
                    step = read_some(1, *step)
    step = read_some(len(todo), *step)
    mine, other = {}, {}
    for at in range(half):
        mine[at], other[at] = down(at, *step)
        step = (mine[at],)
    others = swap(jnp.concatenate([other[at] for at in range(half)], 0), 1, count)
    last = finish(True, [mine[at] for at in range(half)])
    others = lax.optimization_barrier((others, last))[0]
    return finish(False, [others[at : at + 1] for at in range(half)])


def solution(mesh):
    return jax.shard_map(
        per_device,
        mesh=mesh,
        in_specs=(
            P(None, ("grp", "seq"), None),
            P(None, ("grp", "seq"), None),
            P(None, ("grp", "seq"), None),
            P(None, ("grp", "seq")),
            P(),
            P(),
            P(),
            P(),
        ),
        out_specs=P(None, ("grp", "seq"), None),
        check_vma=False,
    )
```

```python
import functools

import jax
import jax.numpy as jnp
from jax import lax
from jax.experimental import pallas as pl
from jax.experimental.pallas import tpu as pltpu
from jax.sharding import PartitionSpec as P

BLOCK = 128
GROUP = 16
HALF = BLOCK // 2
LIMIT = 20 << 20

f32 = jnp.float32
bf16 = jnp.bfloat16


def split(x):
    high = x.astype(bf16)
    low = (x - high.astype(f32)).astype(bf16)
    return jnp.concatenate([high, low], 1)


def mm(a, b):
    n = b.shape[1] // 2
    m, k = a.shape[0], b.shape[0]
    if m <= HALF:
        p = jnp.dot(
            jnp.concatenate([a[:, :k], a[:, k:]], 0), b, preferred_element_type=f32
        )
        p = p[:m] + p[m:]
        return p[:, :n] + p[:, n:]
    p = jnp.dot(a, jnp.concatenate([b, b], 0), preferred_element_type=f32)
    return p[:, :n] + p[:, n:]


def pick_row(x, r):
    row = lax.broadcasted_iota(jnp.int32, x.shape, 0)
    return jnp.sum(jnp.where(row == r, x, 0.0), 0, keepdims=True)


def silu(x):
    return x / (1.0 + jnp.exp(-x))


def step_time(r):
    return (r // GROUP) * GROUP + 2 * (r % 8) + (r // 8) % 2


def interleave(a, b):
    parts = []
    for g in range(0, a.shape[0], 8):
        parts += [a[g : g + 8], b[g : g + 8]]
    return jnp.concatenate(parts, 0)


def conv_taps(ref, weights, start, count):
    taps = weights.shape[0]
    total = weights[0:1] * ref[pl.ds(start + 9 - taps, count), :]
    for s in range(1, taps):
        total = total + weights[s : s + 1] * ref[pl.ds(start + 9 - taps + s, count), :]
    return silu(total)


def fill_rows(ref, halo, rows):
    rim = halo.shape[0]
    ref[8 - rim : 8, :] = halo.astype(f32)
    ref[8:, :] = rows.astype(f32)


def first_head(index_ref, kept, half):
    upper = index_ref[0] & 1
    return (upper if kept else 1 - upper) * half


def block_masks():
    row = lax.broadcasted_iota(jnp.int32, (BLOCK, BLOCK), 0)
    col = lax.broadcasted_iota(jnp.int32, (BLOCK, BLOCK), 1)
    lane = lax.broadcasted_iota(jnp.int32, (GROUP, BLOCK), 1)
    return row, col, lane


def block_inputs(units, keys):
    row, col, lane = block_masks()
    strict = step_time(col) < step_time(row)
    for i, (rows, ck, cv, t0, rates, kv, kb, low, diag) in enumerate(units):
        dim = rows[0].shape[1]
        taps = [w[:, j * dim : (j + 1) * dim] for w in (ck, cv) for j in range(2)]
        ka, kb_, va, vb = [conv_taps(r, w, t0, HALF) for r, w in zip(rows, taps)]
        k = interleave(ka, kb_)
        k = k * lax.rsqrt(jnp.sum(k * k, 1, keepdims=True) + 1e-06)
        keys[i] = k
        kv[:, : 2 * dim] = split(k)
        kv[:, 2 * dim :] = split(interleave(va, vb))
    for i, (rows, ck, cv, t0, rates, kv, kb, low, diag) in enumerate(units):
        kb[...] = split(keys[i].T * rates)
    for i, (rows, ck, cv, t0, rates, kv, kb, low, diag) in enumerate(units):
        lower = jnp.where(strict, mm(kv[:, : kb.shape[1]], kb[...]), 0.0)
        low[...] = lower
        groups = jnp.zeros((GROUP, BLOCK), f32)
        for g in range(BLOCK // GROUP):
            groups = jnp.where(lane // GROUP == g, lower[g * GROUP : (g + 1) * GROUP], groups)
        diag[...] = groups


def invert_groups(diag, out, blocks):
    lane = lax.broadcasted_iota(jnp.int32, (blocks, BLOCK), 1)
    times = [t // 2 + 8 * (t % 2) for t in range(GROUP)]
    coef = [diag[pl.ds(r, blocks, stride=GROUP), :] for r in range(GROUP)]
    sol = [(lane % GROUP == r).astype(f32) for r in range(GROUP)]
    for i, s in enumerate(times):
        pick = (lane // GROUP) * GROUP + s
        for r in times[i + 1 :]:
            sol[r] = sol[r] - jnp.take_along_axis(coef[r], pick, axis=1) * sol[s]
    for r in range(GROUP):
        out[pl.ds(r, blocks, stride=GROUP), :] = sol[r]


def front_kernel(
    index_ref, key_ref, value_ref, rate_ref, ck_ref, cv_ref,
    kv_ref, kb_ref, low_ref, sol_ref, rates_ref, rows, brow, diag, keys,
):
    dim = rows.shape[2]
    blocks = rates_ref.shape[1]
    row, col, _ = block_masks()
    order = (row == step_time(col)).astype(f32)

    def one(h, carry):
        for i, ref in enumerate((key_ref, value_ref)):
            for j in range(2):
                rows[2 * i + j, 8:, :] = ref[h, :, j * dim : (j + 1) * dim].astype(f32)
        for n in range(blocks):
            brow[n : n + 1, :] = pick_row(rate_ref[:, n * BLOCK : (n + 1) * BLOCK], h)
        rates = jnp.dot(
            brow[...], order, precision=lax.Precision.HIGHEST, preferred_element_type=f32
        )
        rates_ref[h] = rates
        ck, cv = ck_ref[h], cv_ref[h]
        block_inputs(
            [
                (
                    [rows.at[i] for i in range(4)], ck, cv, n * HALF, rates[n : n + 1],
                    kv_ref.at[h, n - 1], kb_ref.at[h, n - 1], low_ref.at[h, n - 1],
                    diag.at[h, n * GROUP : (n + 1) * GROUP],
                )
                for n in range(1, blocks)
            ],
            keys,
        )
        diag[h, 0:GROUP] = jnp.zeros((GROUP, BLOCK), f32)
        return carry

    lax.fori_loop(0, key_ref.shape[0], one, 0)
    for h in range(key_ref.shape[0]):
        invert_groups(diag.at[h], sol_ref.at[h], blocks)


def first_kernel(
    index_ref, key_ref, value_ref, halo_ref, ck_ref, cv_ref, rates_ref,
    kv_ref, kb_ref, low_ref, sol_ref, rows, diag, keys,
):
    heads = key_ref.shape[0]
    dim = rows.shape[3]
    for h in range(heads):
        halo = own_halo(index_ref, halo_ref[h])
        for i, ref in enumerate((key_ref, value_ref)):
            for j in range(2):
                at = (1 + 2 * i + j) * dim
                fill_rows(
                    rows.at[h, 2 * i + j],
                    halo[:, at : at + dim],
                    ref[h, :HALF, j * dim : (j + 1) * dim],
                )
    block_inputs(
        [
            (
                [rows.at[h, i] for i in range(4)], ck_ref[h], cv_ref[h], 0, rates_ref[h][0:1],
                kv_ref.at[h], kb_ref.at[h], low_ref.at[h], diag.at[h * GROUP : (h + 1) * GROUP],
            )
            for h in range(heads)
        ],
        keys,
    )
    invert_groups(diag, sol_ref, heads)


def own_halo(index_ref, halo):
    return jnp.where(index_ref[0] == 0, 0.0, halo.astype(f32))


def maps_kernel(
    kept, start, half, index_ref, kv_ref, kb_ref, low_ref, sol_ref,
    kv0_ref, kb0_ref, low0_ref, sol0_ref,
    inv_ref, p_ref, s_ref, total_ref, move, written,
):
    count, blocks = inv_ref.shape[:2]
    dim = total_ref.shape[1]
    slots = range(count)
    first = first_head(index_ref, kept, half) + start
    row, col, lane = block_masks()
    eye = (row == col).astype(f32)

    def at(inner, first_one, h, n):
        return first_one[first + h] if n == 0 else inner[first + h, n - 1]

    for h in slots:
        for n in range(blocks):
            if n == 0:
                base = sol0_ref[pl.ds((first + h) * GROUP, GROUP), :]
            else:
                base = sol_ref[first + h, n * GROUP : (n + 1) * GROUP, :]
            inv_ref[h, n] = split(
                jnp.concatenate(
                    [jnp.where(lane // GROUP == g, base, 0.0) for g in range(BLOCK // GROUP)], 0
                )
            )

    lane_h = lax.broadcasted_iota(jnp.int32, (HALF, BLOCK), 1)
    row_h = lax.broadcasted_iota(jnp.int32, (HALF, BLOCK), 0)
    size = GROUP
    while size < BLOCK:
        keep = lane_h // size == 2 * (row_h // size)
        starts = range(size, BLOCK, 2 * size)
        for h in slots:
            for n in range(blocks):
                inv = inv_ref[h, n]
                lower = at(low_ref, low0_ref, h, n)
                low = jnp.concatenate([lower[a : a + size] for a in starts], 0)
                z = split(mm(split(jnp.where(keep, low, 0.0)), inv))
                twice = []
                for i in range(len(starts)):
                    twice += [z[i * size : (i + 1) * size]] * 2
                odd = jnp.concatenate([inv[a : a + size] for a in starts], 0)
                new = mm(odd, jnp.concatenate(twice, 0))
                new = split(odd[:, :BLOCK].astype(f32) + odd[:, BLOCK:].astype(f32) - new)
                for i, a in enumerate(starts):
                    inv_ref[h, n, a : a + size] = new[i * size : (i + 1) * size]
        size *= 2

    for h in slots:
        for n in range(blocks):
            move[h, n] = split(mm(at(kb_ref, kb0_ref, h, n), inv_ref[h, n]))
    for h in slots:
        for n in range(blocks):
            both = at(kv_ref, kv0_ref, h, n)
            solved = move[h, n]
            written[h, n] = split(mm(solved, both[:, 2 * dim :]))
            move[h, n] = split(eye - mm(solved, both[:, : 2 * dim]))

    span = {(h, n, n + 1): (move[h, n], written[h, n]) for h in slots for n in range(blocks)}

    def run(h, i, mid, j):
        later, earlier = span[h, mid, j], span[h, i, mid]
        state = later[1]
        added = state[:, :dim].astype(f32) + state[:, dim:].astype(f32)
        full = (mm(later[0], earlier[0]), mm(later[0], earlier[1]) + added)
        if (i, j) == (0, blocks):
            total_ref[h, :, :dim], total_ref[h, :, dim:] = full
        span[h, i, j] = tuple(split(x) for x in full)

    size = 2
    while size <= blocks:
        for i in range(0, blocks, size):
            for j in range(i + size // 2 + 1, i + size + 1):
                for h in slots:
                    run(h, i, i + size // 2, j)
        size *= 2
    for h in slots:
        p_ref[h, 0] = split(eye)
        s_ref[h, 0] = jnp.zeros((dim, 2 * dim), bf16)
        for n in range(1, blocks):
            p_ref[h, n], s_ref[h, n] = span[h, 0, n]


def reads_kernel(
    kept, slot, at, half, index_ref, query_ref, halo_ref, cq_ref, kv_ref, kb_ref, kv0_ref, kb0_ref,
    inv_ref, p_ref, s_ref, pulled_ref, local_ref, q0, query, scores, pulled,
):
    head = first_head(index_ref, kept, half) + at
    dim = q0.shape[1]
    blocks = inv_ref.shape[1]
    fill_rows(q0, own_halo(index_ref, halo_ref[head])[:, :dim], query_ref[head])
    cq = cq_ref[head]
    row = lax.broadcasted_iota(jnp.int32, (HALF, BLOCK), 0)
    col = lax.broadcasted_iota(jnp.int32, (HALF, BLOCK), 1)
    causal = step_time(col) <= 2 * row + 1
    rows = [slice(n * HALF, (n + 1) * HALF) for n in range(blocks)]
    for n in range(blocks):
        q = conv_taps(q0, cq, n * HALF, HALF)
        query[rows[n]] = q
        kbs = kb0_ref[head] if n == 0 else kb_ref[head, n - 1]
        scores[rows[n]] = split(jnp.where(causal, mm(split(q), kbs), 0.0))
    for n in range(blocks):
        scores[rows[n]] = split(mm(scores[rows[n]], inv_ref[slot, n]))
    for n in range(blocks):
        both = kv0_ref[head] if n == 0 else kv_ref[head, n - 1]
        pulled[rows[n]] = split(query[rows[n]] - mm(scores[rows[n]], both[:, : 2 * dim]))
        local_ref[rows[n]] = mm(scores[rows[n]], both[:, 2 * dim :])
    for n in range(blocks):
        local_ref[rows[n]] += mm(pulled[rows[n]], s_ref[slot, n])
        pulled_ref[rows[n]] = split(mm(pulled[rows[n]], p_ref[slot, n]))


def out_kernel(kept, half, index_ref, gain_ref, *rest):
    out_ref = rest[-1]
    first = first_head(index_ref, kept, half)
    for i in range(half):
        state_ref, pulled_ref, local_ref = rest[3 * i : 3 * i + 3]
        state = split(state_ref[0])
        gain = pick_row(gain_ref[...], first + i)
        for at in range(0, pulled_ref.shape[0], BLOCK):
            rows = slice(at, at + BLOCK)
            raw = mm(pulled_ref[rows], state) + local_ref[rows]
            mean = jnp.mean(raw * raw, 1, keepdims=True)
            out_ref[i, rows] = raw * lax.rsqrt(mean + 1e-06) * gain


def then(later, earlier):
    dim = later.shape[0]
    prod = mm(split(later[:, :dim]), split(earlier))
    wide = prod.shape[1]
    if wide == dim:
        return prod + later[:, dim:]
    return jnp.concatenate([prod[:, :dim], prod[:, dim:] + later[:, dim:]], 1)


def pair_kernel(slot, index_ref, mine_ref, got_ref, total_ref, earlier_ref):
    upper = (index_ref[0] & 1) != 0
    for h in range(mine_ref.shape[0]):
        mine = mine_ref[h]
        got = got_ref[slot + h]
        earlier = jnp.where(upper, got, mine)
        earlier_ref[h] = earlier
        total_ref[h] = then(jnp.where(upper, mine, got), earlier)


def join_kernel(bits, index_ref, *refs):
    size = 1 << len(bits)
    got_refs, before_ref, (total_ref, after_ref) = refs[:size], refs[size:-2], refs[-2:]
    ups = [(index_ref[0] & bit) != 0 for bit in bits]
    dim = got_refs[0].shape[1]
    row = lax.broadcasted_iota(jnp.int32, (dim, 2 * dim), 0)
    col = lax.broadcasted_iota(jnp.int32, (dim, 2 * dim), 1)
    for h in range(got_refs[0].shape[0]):
        maps = [ref[h] for ref in got_refs]
        for i, up in enumerate(ups):
            maps = [jnp.where(up, maps[j ^ (1 << i)], maps[j]) for j in range(size)]
        part = slice(dim, None) if total_ref.shape[2] == dim else slice(None)
        identity = (row == col).astype(f32)
        if size == 2:
            total_ref[h] = then(maps[1], maps[0][:, part])
            prefix = jnp.where(ups[0], maps[0], identity)
        else:
            low = then(maps[1], maps[0])
            total_ref[h] = then(then(maps[3], maps[2]), low[:, part])
            prefix = jnp.where(
                ups[1],
                jnp.where(ups[0], then(maps[2], low), low),
                jnp.where(ups[0], maps[0], identity),
            )
        after_ref[h] = then(before_ref[0][h], prefix) if before_ref else prefix


def down_kernel(bit, index_ref, before_ref, got_ref, earlier_ref, mine_ref, other_ref):
    upper = (index_ref[0] & 1) != 0
    got = jnp.where((index_ref[0] & bit) != 0, got_ref[0], 0.0)
    state = then(before_ref[0], got)
    after = then(earlier_ref[0], state)
    mine_ref[0] = jnp.where(upper, after, state)
    other_ref[0] = jnp.where(upper, state, after)


def tails_kernel(index_ref, query_ref, key_ref, value_ref, out_ref):
    rim = out_ref.shape[1]
    at = 0
    for ref in (query_ref, key_ref, value_ref):
        wide = ref.shape[2]
        out_ref[:, :, at : at + wide] = ref[:, ref.shape[1] - rim :, :]
        at += wide


def shape(dims, dtype):
    return jax.ShapeDtypeStruct(dims, dtype)


def resident(kernel, index, args, outs, scratch=(), limit=4 << 20):
    smem = pl.BlockSpec(memory_space=pltpu.SMEM)
    vmem = pl.BlockSpec(memory_space=pltpu.VMEM)
    return pl.pallas_call(
        kernel,
        in_specs=[smem] + [vmem] * len(args),
        out_specs=[vmem] * len(outs),
        out_shape=[pltpu.VMEM(o.shape, o.dtype) for o in outs],
        scratch_shapes=list(scratch),
        compiler_params=pltpu.CompilerParams(vmem_limit_bytes=limit),
    )(index, *[pltpu.with_memory_space_constraint(a, pltpu.VMEM) for a in args])


def swap(x, bit, count):
    return lax.ppermute(x, "seq", [(i, i ^ bit) for i in range(count)])


def per_device(
    queries, key_pairs, value_pairs, write_rates, conv_query, conv_key, conv_value, out_gain
):
    heads, tokens, dim = queries.shape
    blocks = tokens // HALF
    half = heads // 2
    rim = conv_query.shape[1] - 1
    count = lax.axis_size("seq")
    index = lax.axis_index("seq").reshape(1)

    parts = (queries, key_pairs, value_pairs)
    last = [
        pl.BlockSpec((heads, 16, x.shape[2]), lambda i, index_ref: (0, tokens // 16 - 1, 0))
        for x in parts
    ]
    tails = pl.pallas_call(
        tails_kernel,
        grid_spec=pltpu.PrefetchScalarGridSpec(
            num_scalar_prefetch=1,
            grid=(1,),
            in_specs=last,
            out_specs=pl.BlockSpec((heads, rim, 5 * dim), lambda i, index_ref: (0, 0, 0)),
        ),
        out_shape=shape((heads, rim, 5 * dim), bf16),
        compiler_params=pltpu.CompilerParams(vmem_limit_bytes=4 << 20),
    )(index, *[pltpu.with_memory_space_constraint(x, pltpu.HBM) for x in parts])
    halo = lax.ppermute(tails, "seq", [(i, (i + 1) % count) for i in range(count)])

    def in_order(*after):
        return lax.optimization_barrier((index, after))[0]

    inner = (heads, blocks - 1, BLOCK)
    front = resident(
        front_kernel,
        in_order(tails),
        (key_pairs, value_pairs, write_rates, conv_key, conv_value),
        [
            shape(inner + (4 * dim,), bf16),
            shape(inner + (2 * dim,), bf16),
            shape(inner + (BLOCK,), f32),
            shape((heads, blocks * GROUP, BLOCK), f32),
            shape((heads, blocks, BLOCK), f32),
        ],
        [
            pltpu.VMEM((4, tokens + 8, dim), f32),
            pltpu.VMEM((blocks, BLOCK), f32),
            pltpu.VMEM((heads, blocks * GROUP, BLOCK), f32),
            pltpu.VMEM((blocks - 1, BLOCK, dim), f32),
        ],
        LIMIT,
    )
    *front, rates = front
    halo = lax.optimization_barrier((halo, rates))[0]
    opening = resident(
        first_kernel,
        in_order(rates),
        (key_pairs, value_pairs, halo, conv_key, conv_value, rates),
        [
            shape((heads, BLOCK, 4 * dim), bf16),
            shape((heads, BLOCK, 2 * dim), bf16),
            shape((heads, BLOCK, BLOCK), f32),
            shape((heads * GROUP, BLOCK), f32),
        ],
        [
            pltpu.VMEM((heads, 4, HALF + 8, dim), f32),
            pltpu.VMEM((heads * GROUP, BLOCK), f32),
            pltpu.VMEM((heads, BLOCK, dim), f32),
        ],
        LIMIT,
    )

    def maps(kept, start, size, *after):
        wide = shape((size, blocks, BLOCK, 2 * dim), bf16)
        return resident(
            functools.partial(maps_kernel, kept, start, half),
            in_order(*after),
            (*front, *opening),
            [wide] * 3 + [shape((size, dim, 2 * dim), f32)],
            [pltpu.VMEM((size, blocks, dim, 2 * dim), bf16)] * 2,
            LIMIT,
        )

    def reads(kept, at, *after):
        slot, saved = (0, kept_saved[at]) if kept else (at, sent_saved)
        return resident(
            functools.partial(reads_kernel, kept, slot, at, half),
            in_order(*after),
            (queries, halo, conv_query, *front[:2], *opening[:2], *saved),
            [shape((tokens, 2 * dim), bf16), shape((tokens, dim), f32)],
            [
                pltpu.VMEM((tokens + 8, dim), f32),
                pltpu.VMEM((tokens, dim), f32),
                pltpu.VMEM((tokens, 2 * dim), bf16),
                pltpu.VMEM((tokens, 2 * dim), bf16),
            ],
            LIMIT,
        )

    total_shape = shape((1, dim, 2 * dim), f32)
    state_shape = shape((1, dim, dim), f32)
    bits = []
    while 2 << len(bits) < count:
        bits.append(2 << len(bits))
    chains = {}

    def begin(at, got, *after):
        total, earlier = resident(
            functools.partial(pair_kernel, at),
            in_order(*after),
            (kept_total[at], got),
            [total_shape] * 2,
        )
        chains[at] = dict(current=total, earlier=earlier, before=(), left=[(bit,) for bit in bits[:-1]])
        send(at)
        return total

    def send(at):
        chain = chains[at]
        now = chain["left"][0] if chain["left"] else bits[-1:]
        flips = [sum(b for i, b in enumerate(now) if j >> i & 1) for j in range(1 << len(now))]
        chain["got"] = [swap(chain["current"], flip, count) for flip in flips[1:]]

    def join(at, *after):
        chain = chains[at]
        now = chain["left"].pop(0)
        got = lax.optimization_barrier((chain["got"], after))[0]
        chain["current"], before = resident(
            functools.partial(join_kernel, now),
            index,
            (chain["current"], *got, *chain["before"]),
            [total_shape if chain["left"] else state_shape, total_shape],
        )
        chain["before"] = (before,)
        send(at)
        return chain["current"]

    def down(at, *after):
        chain = chains[at]
        got = lax.optimization_barrier((chain["got"], after))[0][0]
        return resident(
            functools.partial(down_kernel, bits[-1]),
            index,
            (*chain["before"], got, chain["earlier"]),
            [state_shape] * 2,
        )

    out_shape = shape((heads, tokens, dim), f32)
    done = ()

    def finish(kept, states, *after):
        nonlocal done
        vmem = pl.BlockSpec(memory_space=pltpu.VMEM)

        def out_block(i, index_ref):
            upper = index_ref[0] & 1
            return (upper if kept else 1 - upper, 0, 0)

        args = [out_gain]
        for i, state in enumerate(states):
            args += [state, *read[kept, i]]
        args = [pltpu.with_memory_space_constraint(a, pltpu.VMEM) for a in args]

        def kernel(index_ref, *refs):
            out_kernel(kept, half, index_ref, *refs[: len(args)], refs[-1])

        out = pl.pallas_call(
            kernel,
            grid_spec=pltpu.PrefetchScalarGridSpec(
                num_scalar_prefetch=1,
                grid=(1,),
                in_specs=[vmem] * len(args) + [pl.BlockSpec(memory_space=pl.ANY)] * len(done),
                out_specs=pl.BlockSpec((half, tokens, dim), out_block),
            ),
            out_shape=out_shape,
            input_output_aliases={len(args) + 1: 0} if done else {},
            compiler_params=pltpu.CompilerParams(vmem_limit_bytes=LIMIT),
        )(in_order(*after), *args, *done)
        done = (out,)
        return out

    kept_saved, kept_total, read = {}, {}, {}

    def keep(at, *after):
        *kept_saved[at], kept_total[at] = maps(True, at, 1, *after)

    *sent_saved, sent_total = maps(False, 0, half)
    got = swap(sent_total, 1, count)
    keep(0, sent_total)
    step = begin(0, got)
    for at in range(1, half):
        keep(at, step)
        step = begin(at, got, kept_total[at])
    step = (step,)
    todo = [(kept, at) for at in range(half) for kept in (False, True)]

    def read_some(pieces, *after):
        for _ in range(min(pieces, len(todo))):
            kept, at = todo.pop(0)
            read[kept, at] = reads(kept, at, *after)
            after = tuple(read[kept, at])
        return after

    step = read_some(1, *step)
    while any(chain["left"] for chain in chains.values()):
        for at in range(half):
            if chains[at]["left"]:
                step = (join(at, *step),)
                if len(todo) > 1:
                    step = read_some(1, *step)
    step = read_some(len(todo), *step)
    mine, other = {}, {}
    for at in range(half):
        mine[at], other[at] = down(at, *step)
        step = (mine[at],)
    others = swap(jnp.concatenate([other[at] for at in range(half)], 0), 1, count)
    last = finish(True, [mine[at] for at in range(half)])
    others = lax.optimization_barrier((others, last))[0]
    return finish(False, [others[at : at + 1] for at in range(half)])


def solution(mesh):
    return jax.shard_map(
        per_device,
        mesh=mesh,
        in_specs=(
            P(None, ("grp", "seq"), None),
            P(None, ("grp", "seq"), None),
            P(None, ("grp", "seq"), None),
            P(None, ("grp", "seq")),
            P(),
            P(),
            P(),
            P(),
        ),
        out_specs=P(None, ("grp", "seq"), None),
        check_vma=False,
    )
```
